32 devices in a mesh: seq: 16 (over z, y, core), fsdp: 2 (over x).
Axes of the slice: x: 2, y: 2, z: 4, core: 2. Of those that a mesh axis runs over, the one named last changes fastest.
Arguments:
- tokens: bfloat16 [2, 2, 1024, 1024], P('fsdp', None, 'seq'), may hold values from -8 to 8
- v_first: bfloat16 [2, 2, 1024, 1024], P('fsdp', None, 'seq'), may hold values from -6 to 6
- segments: int32 [2, 2, 1024], P('fsdp', None, 'seq'), may hold values from 0 to 1023, as said below
- grad_out: bfloat16 [2, 2, 1024, 1024], P('fsdp', None, 'seq'), may hold values from -6 to 6
- w_qkv: bfloat16 [1024, 3072], P(('seq', 'fsdp')), may hold values from -0.1875 to 0.1875
- w_out: bfloat16 [1024, 1024], P(('seq', 'fsdp')), may hold values from -0.75 to 0.75
- w_gate_up: bfloat16 [1024, 5632], P(('seq', 'fsdp')), may hold values from -0.1875 to 0.1875
- w_down: bfloat16 [2816, 1024], P(('seq', 'fsdp')), may hold values from -0.109375 to 0.109375
- gain_attn: bfloat16 [1024], P(('seq', 'fsdp')), may hold values from 0.25 to 1.75
- gain_ffn: bfloat16 [1024], P(('seq', 'fsdp')), may hold values from 0.25 to 1.75
Outputs:
- out: bfloat16 [2, 2, 1024, 1024], P('fsdp', None, 'seq')
- grad_tokens: float32 [2, 2, 1024, 1024], P('fsdp', None, 'seq')
- grad_v_first: float32 [2, 2, 1024, 1024], P('fsdp', None, 'seq')
- grad_w_qkv: float32 [1024, 3072], P(('seq', 'fsdp'))
- grad_w_out: float32 [1024, 1024], P(('seq', 'fsdp'))
- grad_w_gate_up: float32 [1024, 5632], P(('seq', 'fsdp'))
- grad_w_down: float32 [2816, 1024], P(('seq', 'fsdp'))
- grad_gain_attn: float32 [1024], P(('seq', 'fsdp'))
- grad_gain_ffn: float32 [1024], P(('seq', 'fsdp'))
- stats: float32 [3], replicated
The draws below stay inside these ranges and needn't reach their ends.
Inputs may be any that keep to these rules, and one draw needn't show every extreme that they name: `segments`: each entry is the index within its row of the first position of its document: documents are contiguous, entries never fall along a row, and a row starts with 0. In each group one row, drawn from the seed, holds a document with positions on the first and on the last index of seq.
All inputs are finite; a program needn't handle non-finite values.
Results may differ from the reference program's by a relative error of at most 0.025.
Values may be sent and summed in bfloat16 or wider, within the bound.
No kernel may reach another device: no remote copies, remote signals or barrier semaphores. Data moves between devices by JAX's collectives and lax.ppermute only.
A program may use at most 192 MiB of HBM per device.

```python
import jax
import jax.numpy as jnp
from jax import lax

D = 1024
HEADS = 16
HEAD_DIM = 64
FF = 2816
ROW_DEV = 64
ROWS = 2
LONG_DOC = 2048
GROUPS = 2
LEN_ROW = 1024


short_odds = 32


loud_low = 4.5


loud_high = 6.0


def draw_tokens(key, part):
    key = jax.random.fold_in(key, 3)
    full_shape = (GROUPS, ROWS, LEN_ROW, D)
    value_key, channel_key, sign_key, size_key = jax.random.split(key, 4)
    rising = 0.5 + 1.5 * jnp.arange(LEN_ROW, dtype=jnp.float32) / (LEN_ROW - 1)
    rising = rising[None, None, :, None]
    values = jnp.clip(jax.random.normal(value_key, full_shape, jnp.float32), -4.0, 4.0) * rising
    ranks = jax.random.permutation(channel_key, D)
    loud_channels = (ranks < max(2, D // 128))[None, None, None, :]
    signs = (2 * jax.random.randint(sign_key, full_shape, 0, 2) - 1).astype(jnp.float32)
    magnitudes = jax.random.uniform(size_key, full_shape, jnp.float32, loud_low, loud_high)
    values = jnp.where(loud_channels, signs * magnitudes, values)
    return values.astype(jnp.bfloat16)


def draw_segments(key, part):
    group_keys = jax.random.split(jax.random.fold_in(key, 7), GROUPS)
    position = jnp.arange(LEN_ROW, dtype=jnp.int32)

    def one_group(group_key):
        row_key, head_key, tail_key, break_key = jax.random.split(group_key, 4)
        span_row = jax.random.randint(row_key, (), 0, ROWS)
        head_end = jax.random.randint(head_key, (), 0, ROW_DEV // 2)
        tail_end = LEN_ROW - 1 - jax.random.randint(tail_key, (), 0, ROW_DEV // 2)
        breaks = jax.random.randint(break_key, (ROWS, LEN_ROW), 0, short_odds) == 0
        span_flags = breaks & ((position < head_end) | (position > tail_end)) | (position == 0) | (position == head_end) | (position == tail_end + 1)
        other_flags = (position == 0) | (position == LEN_ROW // 2) | (position == LEN_ROW - 1) | (position < LEN_ROW // 2) & (position % LONG_DOC == 0) | (position >= LEN_ROW // 2) & breaks
        row_index = jnp.arange(ROWS, dtype=jnp.int32)[:, None]
        row_flags = jnp.where(row_index == span_row, span_flags, other_flags)
        return lax.cummax(jnp.where(row_flags, position[None, :], 0), axis=1)
    return jax.vmap(one_group)(group_keys)


def levels(rng, extent, pieces, least, largest):
    loudness, own = 1.0, jax.random.fold_in(rng, 6)
    for dim, parts in pieces:
        draws = jnp.exp(jax.random.uniform(jax.random.fold_in(own, dim), (parts,), jnp.float32, least / len(pieces), largest / len(pieces)))
        loudness = loudness * jnp.repeat(draws, extent[dim] // parts).reshape([-1 if axis == dim else 1 for axis in range(len(extent))])
    return loudness


def normal_values(stream_key, extent, width, bound, cuts=(), held_as=jnp.bfloat16):
    drawn = jax.random.normal(stream_key, extent, jnp.float32) * width
    if len(cuts) > 0:
        drawn = levels(stream_key, extent, cuts, -0.22, 0.18) * drawn
    return jnp.clip(drawn, min=-bound, max=bound).astype(held_as)


def setup_inputs(seed: int = 0) -> dict:
    streams_of = jax.random.split(jax.random.key(seed), 11)
    return {
        "tokens": draw_tokens(jax.random.fold_in(streams_of[10], 71), 0),
        "v_first": normal_values(streams_of[1], (GROUPS, ROWS, LEN_ROW, D), 1.0, 6.0, ((0, 2), (2, 16))),
        "segments": draw_segments(jax.random.fold_in(streams_of[10], 71), 0),
        "grad_out": normal_values(streams_of[3], (GROUPS, ROWS, LEN_ROW, D), 1.0, 6.0, ((0, 2), (2, 16))),
        "w_qkv": normal_values(streams_of[4], (D, 3 * D), D ** -0.5, 0.1875, ((0, 32),)),
        "w_out": normal_values(streams_of[5], (D, D), (D // 16) ** -0.5, 0.75, ((0, 32),)),
        "w_gate_up": normal_values(streams_of[6], (D, 2 * FF), D ** -0.5, 0.1875, ((0, 32),)),
        "w_down": normal_values(streams_of[7], (FF, D), FF ** -0.5, 0.109375, ((0, 32),)),
        "gain_attn": jnp.clip(1.0 + 0.15 * jax.random.normal(streams_of[8], (D,), jnp.float32), 0.25, 1.75).astype(jnp.bfloat16),
        "gain_ffn": jnp.clip(1.0 + 0.15 * jax.random.normal(streams_of[9], (D,), jnp.float32), 0.25, 1.75).astype(jnp.bfloat16),
    }


epsilon = 1e-06
masked_score = -1e+30

@jax.custom_vjp
def low(v):
    return lax.optimization_barrier(v.astype(jnp.bfloat16)).astype(jnp.float32)

@jax.custom_vjp
def low_back(v):
    return v

def low_keep(v):
    return (low(v), None)

def low_pass(kept, grad):
    return (grad,)

def back_keep(v):
    return (v, None)

def back_low(kept, grad):
    return (low(grad),)
low.defvjp(low_keep, low_pass)
low_back.defvjp(back_keep, back_low)

def matmul(left, right):
    return jnp.dot(left, right, precision=lax.Precision.HIGHEST, preferred_element_type=jnp.float32)

def rms_norm(values, gain):
    return values * lax.rsqrt(lax.optimization_barrier(jnp.mean(values * values, -1, keepdims=True)) + epsilon) * gain

def rotate(values, positions):
    half_dim = values.shape[-1] // 2
    freqs = jnp.power(10000.0, -jnp.arange(half_dim, dtype=jnp.float32) / half_dim)
    angles = positions[..., None] * freqs
    cosine = jnp.cos(angles)[..., None, :]
    sine_part = jnp.sin(angles)[..., None, :]
    first_half = values[..., :half_dim]
    second_half = values[..., half_dim:]
    return jnp.concatenate([first_half * cosine - second_half * sine_part, second_half * cosine + first_half * sine_part], -1)

def row_attention(queries, keys, values, seg_row):
    length_row = queries.shape[0]
    block_rows = min(512, length_row)
    score_scale = queries.shape[-1] ** (-0.5)
    key_index = jnp.arange(length_row, dtype=jnp.int32)

    @jax.checkpoint
    def one_block(block_item):
        query_block, first_row, seg_block = block_item
        query_index = first_row + jnp.arange(block_rows, dtype=jnp.int32)
        raw = jnp.einsum('qhd,khd->hqk', query_block, keys, precision=lax.Precision.HIGHEST, preferred_element_type=jnp.float32) * score_scale
        raw = low_back(raw)
        valid = (key_index[None, :] >= seg_block[:, None]) & (key_index[None, :] <= query_index[:, None])
        scores = jnp.where(valid[None], raw, masked_score)
        weights = low(jax.nn.softmax(scores, axis=-1))
        return jnp.einsum('hqk,khd->qhd', weights, values, precision=lax.Precision.HIGHEST, preferred_element_type=jnp.float32)
    block_count = length_row // block_rows
    starts = jnp.arange(block_count, dtype=jnp.int32) * block_rows
    stacked = queries.reshape(block_count, block_rows, queries.shape[1], queries.shape[2])
    results = lax.map(one_block, (stacked, starts, seg_row.reshape(block_count, block_rows)))
    return results.reshape(queries.shape)

def reference(tokens, v_first, segments, grad_out, w_qkv, w_out, w_gate_up, w_down, gain_attn, gain_ffn):
    groups_here, rows_here, length_row, features = tokens.shape
    row_total = groups_here * rows_here
    seg_all = segments.reshape(row_total, length_row).astype(jnp.int32)
    positions = (jnp.arange(length_row, dtype=jnp.int32)[None, :] - seg_all).astype(jnp.float32)

    def split_heads(values):
        return values.reshape(row_total, length_row, HEADS, HEAD_DIM)

    def attend_row(row_item):
        return row_attention(row_item[0], row_item[1], row_item[2], row_item[3])

    def forward(inputs, first_values, weight_qkv, weight_out, weight_gate_up, weight_down, attn_gain, ffn_gain):
        flat = inputs.reshape(-1, features)
        normed_one = low(rms_norm(flat, attn_gain))
        projected = low_back(matmul(normed_one, weight_qkv))
        queries = low(rotate(split_heads(projected[:, :features]), positions))
        keys = low(rotate(split_heads(projected[:, features:2 * features]), positions))
        mixed = low(0.5 * split_heads(projected[:, 2 * features:]) + 0.5 * split_heads(first_values.reshape(-1, features)))
        attended = lax.map(attend_row, (queries, keys, mixed, seg_all))
        attended = low(low_back(attended.reshape(-1, features)))
        branch_attn = low_back(matmul(attended, weight_out))
        stream = flat + branch_attn
        normed_two = low(rms_norm(stream, ffn_gain))
        gate_up = low_back(matmul(normed_two, weight_gate_up))
        hidden = low(jax.nn.silu(gate_up[:, :FF]) * gate_up[:, FF:])
        branch_ffn = low_back(matmul(hidden, weight_down))
        return (stream + branch_ffn, (stream, branch_attn, branch_ffn))
    output, pullback, aux_values = jax.vjp(forward, tokens.astype(jnp.float32), v_first.astype(jnp.float32), w_qkv.astype(jnp.float32), w_out.astype(jnp.float32), w_gate_up.astype(jnp.float32), w_down.astype(jnp.float32), gain_attn.astype(jnp.float32), gain_ffn.astype(jnp.float32), has_aux=True)
    stream, branch_attn, branch_ffn = aux_values
    gradients = pullback(grad_out.astype(jnp.float32).reshape(-1, features))
    stats = jnp.sqrt(jnp.stack([jnp.mean(stream * stream), jnp.mean(branch_attn * branch_attn), jnp.mean(branch_ffn * branch_ffn)]))
    return (output.astype(jnp.bfloat16).reshape(tokens.shape), gradients[0].reshape(tokens.shape), gradients[1].reshape(tokens.shape), gradients[2], gradients[3], gradients[4], gradients[5], gradients[6], gradients[7], stats)
```

```python
import itertools

import jax
import jax.numpy as jnp
from jax import lax
from jax.experimental import pallas as pl
from jax.experimental.pallas import tpu as pltpu
from jax.sharding import Mesh
from jax.sharding import PartitionSpec as P

HEADS = 16
HEAD_DIM = 64
FF = 2816
GRID = ("a", "b", "c", "f")


epsilon = 1e-06
masked_score = -1e30


def from_behind(value, axis, steps):
    count = lax.axis_size(axis)
    initial, last = (max(0, -steps), min(count, count - steps))
    return lax.ppermute(value, axis, [(source, source + steps) for source in range(initial, last)])


def shifted(shard, axis, by):
    size = lax.axis_size(axis)
    return lax.ppermute(shard, axis, [(i, (i + by) % size) for i in range(size)])


def rms_forward(values, gain):
    inverse_rms = lax.rsqrt(jnp.mean(values * values, -1, keepdims=True) + epsilon)
    return (values * inverse_rms * gain, inverse_rms)


def rms_backward(values, inverse_rms, gain, normed_grad):
    scaled = normed_grad * gain
    gain_grad = jnp.sum(normed_grad * values * inverse_rms, 0)
    input_grad = inverse_rms * scaled - values * (
        inverse_rms * inverse_rms * inverse_rms
    ) * jnp.mean(scaled * values, -1, keepdims=True)
    return (input_grad, gain_grad)


def rotation_tables(positions, head_dim):
    half_dim = head_dim // 2
    freqs = jnp.power(10000.0, -jnp.arange(half_dim, dtype=jnp.float32) / half_dim)
    angles = positions[..., None] * freqs
    return (jnp.cos(angles)[..., None, :], jnp.sin(angles)[..., None, :])


def rotate_forward(values, cosine, sine_part):
    half_dim = values.shape[-1] // 2
    first_half = values[..., :half_dim]
    second_half = values[..., half_dim:]
    return jnp.concatenate(
        [
            first_half * cosine - second_half * sine_part,
            second_half * cosine + first_half * sine_part,
        ],
        -1,
    )


def rotate_backward(values, cosine, sine_part):
    half_dim = values.shape[-1] // 2
    first_half = values[..., :half_dim]
    second_half = values[..., half_dim:]
    return jnp.concatenate(
        [
            first_half * cosine + second_half * sine_part,
            second_half * cosine - first_half * sine_part,
        ],
        -1,
    )


def over_blocks(visit, carried, members, block_rows):
    piece_rows = members[0].shape[1]
    splits = piece_rows // block_rows
    key_blocks = jnp.swapaxes(
        members[0].reshape(members[0].shape[0], splits, block_rows, members[0].shape[2]), 0, 1
    )
    value_blocks = jnp.swapaxes(
        members[1].reshape(members[1].shape[0], splits, block_rows, members[1].shape[2]), 0, 1
    )
    offsets = jnp.arange(splits, dtype=jnp.int32) * block_rows

    def advance(running, block_item):
        return (visit(running, block_item[0], block_item[1], block_item[2]), None)

    carried, unused = lax.scan(advance, carried, (key_blocks, value_blocks, offsets))
    return carried


def back_pair(
    query_heads,
    grad_heads,
    lse_part,
    delta_part,
    seg_part,
    index_part,
    key_heads,
    value_heads,
    key_start,
    score_scale,
):
    raw = (
        jnp.einsum("rqhd,rkhd->rhqk", query_heads, key_heads, preferred_element_type=jnp.float32)
        * score_scale
    )
    key_index = key_start + jnp.arange(key_heads.shape[1], dtype=jnp.int32)
    valid = (key_index[None, None, :] >= seg_part[:, :, None]) & (
        key_index[None, None, :] <= index_part[None, :, None]
    )
    valid = valid[:, None]
    scores = jnp.where(valid, raw, masked_score)
    weights = jnp.where(valid, jnp.exp(scores - lse_part[..., None]), 0.0)
    value_grad = jnp.einsum(
        "rhqk,rqhd->rkhd",
        weights.astype(jnp.bfloat16),
        grad_heads,
        preferred_element_type=jnp.float32,
    )
    weight_grad = jnp.einsum(
        "rqhd,rkhd->rhqk", grad_heads, value_heads, preferred_element_type=jnp.float32
    )
    score_grad = (weights * (weight_grad - delta_part[..., None])).astype(jnp.bfloat16)
    query_grad = (
        jnp.einsum("rhqk,rkhd->rqhd", score_grad, key_heads, preferred_element_type=jnp.float32)
        * score_scale
    )
    key_grad = (
        jnp.einsum("rhqk,rqhd->rkhd", score_grad, query_heads, preferred_element_type=jnp.float32)
        * score_scale
    )
    return (query_grad, key_grad, value_grad)


def ring_body(tokens, v_first, segments, grad_out, w_qkv, w_out, w_gate_up, w_down, gain_attn, gain_ffn):
    row_count = tokens.shape[1]
    shard_len = tokens.shape[2]
    features = tokens.shape[3]
    head_count = HEADS
    head_dim = HEAD_DIM
    score_scale = head_dim ** (-0.5)
    cycle_size = lax.axis_size("seq")
    device_index = lax.axis_index("seq")
    gathered = (
        lax.all_gather(w_qkv, ("seq", "fsdp"), axis=0, tiled=True),
        lax.all_gather(w_out, ("seq", "fsdp"), axis=0, tiled=True),
        lax.all_gather(w_gate_up, ("seq", "fsdp"), axis=0, tiled=True),
        lax.all_gather(w_down, ("seq", "fsdp"), axis=0, tiled=True),
        lax.all_gather(gain_attn, ("seq", "fsdp"), axis=0, tiled=True),
        lax.all_gather(gain_ffn, ("seq", "fsdp"), axis=0, tiled=True),
    )
    full_qkv, full_out, full_gate_up, full_down, full_gain_attn, full_gain_ffn = gathered
    attn_gain = full_gain_attn.astype(jnp.float32)
    ffn_gain = full_gain_ffn.astype(jnp.float32)
    inputs = tokens.reshape(-1, features).astype(jnp.float32)
    normed_one, inverse_one = rms_forward(inputs, attn_gain)
    normed_one_low = normed_one.astype(jnp.bfloat16)
    projected = jnp.dot(normed_one_low, full_qkv, preferred_element_type=jnp.float32)
    query_index = device_index * shard_len + jnp.arange(shard_len, dtype=jnp.int32)
    seg_rows = segments[0]
    positions = (query_index[None, :] - seg_rows).astype(jnp.float32)
    cosine, sine_part = rotation_tables(positions, head_dim)

    def split_heads(values):
        return values.reshape(row_count, -1, head_count, head_dim)

    queries = rotate_forward(split_heads(projected[:, :features]), cosine, sine_part).astype(
        jnp.bfloat16
    )
    keys_low = (
        rotate_forward(split_heads(projected[:, features : 2 * features]), cosine, sine_part)
        .astype(jnp.bfloat16)
        .reshape(row_count, shard_len, features)
    )
    mixed = (
        (
            0.5 * projected[:, 2 * features :]
            + 0.5 * v_first.reshape(-1, features).astype(jnp.float32)
        )
        .astype(jnp.bfloat16)
        .reshape(row_count, shard_len, features)
    )

    def scores_for(key_heads, key_start):
        raw = (
            jnp.einsum("rqhd,rkhd->rhqk", queries, key_heads, preferred_element_type=jnp.float32)
            * score_scale
        )
        key_index = key_start + jnp.arange(key_heads.shape[1], dtype=jnp.int32)
        valid = (key_index[None, None, :] >= seg_rows[:, :, None]) & (
            key_index[None, None, :] <= query_index[None, :, None]
        )
        valid = valid[:, None]
        return (jnp.where(valid, raw, masked_score), valid)

    def accumulate(carried, key_piece, value_piece, key_start):
        running_max, running_sum, weighted = carried
        key_heads = split_heads(key_piece)
        value_heads = split_heads(value_piece)
        scores, valid = scores_for(key_heads, key_start)
        new_max = jnp.maximum(running_max, jnp.max(scores, -1))
        weights = jnp.where(valid, jnp.exp(scores - new_max[..., None]), 0.0)
        factor = jnp.exp(running_max - new_max)
        running_sum = running_sum * factor + jnp.sum(weights, -1)
        weighted = weighted * jnp.transpose(factor, (0, 2, 1))[..., None] + jnp.einsum(
            "rhqk,rkhd->rqhd",
            weights.astype(jnp.bfloat16),
            value_heads,
            preferred_element_type=jnp.float32,
        )
        return (new_max, running_sum, weighted)

    def visit_forward(carried, key_piece, value_piece, key_start):
        return accumulate(carried, key_piece, value_piece, key_start)

    initial = (
        jnp.full((row_count, head_count, shard_len), masked_score, jnp.float32),
        jnp.zeros((row_count, head_count, shard_len), jnp.float32),
        jnp.zeros((row_count, shard_len, head_count, head_dim), jnp.float32),
    )
    running_max, running_sum, weighted = over_blocks(
        visit_forward,
        initial,
        (
            lax.all_gather(keys_low, "seq", axis=1, tiled=True),
            lax.all_gather(mixed, "seq", axis=1, tiled=True),
        ),
        shard_len,
    )
    attention = weighted / jnp.transpose(running_sum, (0, 2, 1))[..., None]
    log_total = running_max + jnp.log(running_sum)
    attn_low = attention.reshape(-1, features).astype(jnp.bfloat16)
    branch_attn = jnp.dot(attn_low, full_out, preferred_element_type=jnp.float32)
    stream = inputs + branch_attn
    normed_two, inverse_two = rms_forward(stream, ffn_gain)
    normed_two_low = normed_two.astype(jnp.bfloat16)
    gate_up = jnp.dot(normed_two_low, full_gate_up, preferred_element_type=jnp.float32)
    gate = gate_up[:, :FF]
    upward = gate_up[:, FF:]
    sigmoid_gate = jax.nn.sigmoid(gate)
    silu_gate = gate * sigmoid_gate
    hidden_low = (silu_gate * upward).astype(jnp.bfloat16)
    branch_ffn = jnp.dot(hidden_low, full_down, preferred_element_type=jnp.float32)
    output = stream + branch_ffn
    out_tokens = output.astype(jnp.bfloat16).reshape(tokens.shape)
    square_sums = jnp.stack(
        [
            jnp.sum(stream * stream),
            jnp.sum(branch_attn * branch_attn),
            jnp.sum(branch_ffn * branch_ffn),
        ]
    )
    square_totals = lax.psum(square_sums, ("seq", "fsdp"))
    stats = jnp.sqrt(square_totals / (stream.size * lax.axis_size(("seq", "fsdp"))))
    regathered = (
        lax.all_gather(w_qkv, ("seq", "fsdp"), axis=0, tiled=True),
        lax.all_gather(w_out, ("seq", "fsdp"), axis=0, tiled=True),
        lax.all_gather(w_gate_up, ("seq", "fsdp"), axis=0, tiled=True),
        lax.all_gather(w_down, ("seq", "fsdp"), axis=0, tiled=True),
        lax.all_gather(gain_attn, ("seq", "fsdp"), axis=0, tiled=True),
        lax.all_gather(gain_ffn, ("seq", "fsdp"), axis=0, tiled=True),
    )
    full_qkv, full_out, full_gate_up, full_down, full_gain_attn, full_gain_ffn = regathered
    attn_gain = full_gain_attn.astype(jnp.float32)
    ffn_gain = full_gain_ffn.astype(jnp.float32)
    ffn_grad_low = grad_out.reshape(-1, features)
    out_grad = ffn_grad_low.astype(jnp.float32)
    down_grad = jnp.dot(hidden_low.T, ffn_grad_low, preferred_element_type=jnp.float32)
    hidden_grad = jnp.dot(ffn_grad_low, full_down.T, preferred_element_type=jnp.float32)
    gate_grad = hidden_grad * upward * sigmoid_gate * (1.0 + gate * (1.0 - sigmoid_gate))
    upward_grad = hidden_grad * silu_gate
    gate_up_grad_low = jnp.concatenate([gate_grad, upward_grad], -1).astype(jnp.bfloat16)
    gate_up_weight_grad = jnp.dot(
        normed_two_low.T, gate_up_grad_low, preferred_element_type=jnp.float32
    )
    normed_two_grad = jnp.dot(gate_up_grad_low, full_gate_up.T, preferred_element_type=jnp.float32)
    stream_norm_grad, ffn_gain_grad = rms_backward(stream, inverse_two, ffn_gain, normed_two_grad)
    stream_grad = out_grad + stream_norm_grad
    attn_grad_low = stream_grad.astype(jnp.bfloat16)
    out_weight_grad = jnp.dot(attn_low.T, attn_grad_low, preferred_element_type=jnp.float32)
    attention_grad = (
        jnp.dot(attn_grad_low, full_out.T, preferred_element_type=jnp.float32)
        .astype(jnp.bfloat16)
        .reshape(row_count, shard_len, head_count, head_dim)
    )
    row_delta = jnp.einsum("rqhd,rqhd->rhq", attention_grad.astype(jnp.float32), attention)

    def back_visit(partials, query_part, key_heads, value_heads, key_start):
        query_heads, grad_heads, lse_part, delta_part, seg_part, index_part = query_part
        query_term, key_term, value_term = back_pair(
            query_heads,
            grad_heads,
            lse_part,
            delta_part,
            seg_part,
            index_part,
            key_heads,
            value_heads,
            key_start,
            score_scale,
        )
        return (
            partials[0] + query_term,
            partials[1] + key_term.reshape(partials[1].shape),
            partials[2] + value_term.reshape(partials[2].shape),
        )

    zero_rows = jnp.zeros((row_count, shard_len, features), jnp.float32)

    def back_turn(turn_index, running):
        key_piece, value_piece, key_grad, value_grad, query_grad = running
        source = (device_index - turn_index) % cycle_size
        query_grad, key_grad, value_grad = back_visit(
            (query_grad, key_grad, value_grad),
            (queries, attention_grad, log_total, row_delta, seg_rows, query_index),
            split_heads(key_piece),
            split_heads(value_piece),
            source * shard_len,
        )
        key_piece, value_piece = from_behind((key_piece, value_piece), "seq", 1)
        key_grad, value_grad = (
            shifted(key_grad.astype(jnp.bfloat16), "seq", 1).astype(key_grad.dtype),
            shifted(value_grad.astype(jnp.bfloat16), "seq", 1).astype(value_grad.dtype),
        )
        return (key_piece, value_piece, key_grad, value_grad, query_grad)

    start_state = (
        keys_low,
        mixed,
        zero_rows,
        zero_rows,
        jnp.zeros((row_count, shard_len, head_count, head_dim), jnp.float32),
    )
    final_state = lax.fori_loop(0, cycle_size, back_turn, start_state)
    key_grad_home = final_state[2]
    value_grad_home = final_state[3]
    query_grad_home = final_state[4]
    query_grad_rows = rotate_backward(query_grad_home, cosine, sine_part).reshape(-1, features)
    key_grad_rows = rotate_backward(split_heads(key_grad_home), cosine, sine_part).reshape(
        -1, features
    )
    mixed_grad = 0.5 * value_grad_home.reshape(-1, features)
    qkv_grad_low = jnp.concatenate([query_grad_rows, key_grad_rows, mixed_grad], -1).astype(
        jnp.bfloat16
    )
    qkv_weight_grad = jnp.dot(normed_one_low.T, qkv_grad_low, preferred_element_type=jnp.float32)
    normed_one_grad = jnp.dot(qkv_grad_low, full_qkv.T, preferred_element_type=jnp.float32)
    input_norm_grad, attn_gain_grad = rms_backward(inputs, inverse_one, attn_gain, normed_one_grad)
    input_grad = stream_grad + input_norm_grad
    owned = (
        lax.psum_scatter(qkv_weight_grad, ("seq", "fsdp"), scatter_dimension=0, tiled=True),
        lax.psum_scatter(out_weight_grad, ("seq", "fsdp"), scatter_dimension=0, tiled=True),
        lax.psum_scatter(gate_up_weight_grad, ("seq", "fsdp"), scatter_dimension=0, tiled=True),
        lax.psum_scatter(down_grad, ("seq", "fsdp"), scatter_dimension=0, tiled=True),
        lax.psum_scatter(attn_gain_grad, ("seq", "fsdp"), scatter_dimension=0, tiled=True),
        lax.psum_scatter(ffn_gain_grad, ("seq", "fsdp"), scatter_dimension=0, tiled=True),
    )
    return (
        out_tokens,
        input_grad.reshape(tokens.shape),
        mixed_grad.reshape(tokens.shape),
        owned[0],
        owned[1],
        owned[2],
        owned[3],
        owned[4],
        owned[5],
        stats,
    )


def hop(value, **flips):
    axes = tuple(name for name in GRID if flips.get(name, 0))
    sizes = [lax.axis_size(name) for name in axes]
    pairs = []
    for source in itertools.product(*[range(size) for size in sizes]):
        origin, target = 0, 0
        for name, size, place in zip(axes, sizes, source):
            origin = origin * size + place
            target = target * size + (place ^ flips[name])
        pairs.append((origin, target))
    return lax.ppermute(value, axes if len(axes) > 1 else axes[0], pairs)


def put(buffer, piece, index, dim):
    return lax.dynamic_update_slice_in_dim(buffer, jnp.expand_dims(piece, dim), index, dim)


def pick(array, index, dim):
    return lax.dynamic_index_in_dim(array, index, dim, keepdims=False)


def ordered(mine, other, place, dim):
    first = jnp.where(place == 0, mine, other)
    second = jnp.where(place == 0, other, mine)
    return jnp.stack([first, second], dim)


def gather_a(value, a_place, dim=0):
    count = lax.axis_size("a")
    shape = value.shape[:dim] + (count,) + value.shape[dim:]
    buffer = put(jnp.zeros(shape, value.dtype), value, a_place, dim)
    for step in range(1, count):
        buffer = put(buffer, hop(value, a=step), a_place ^ step, dim)
    return buffer


def half_swap(values):
    lanes = lax.broadcasted_iota(jnp.int32, values.shape, values.ndim - 1)
    quarter = HEAD_DIM // 2
    width = values.shape[-1]
    ahead = pltpu.roll(values, width - quarter, values.ndim - 1)
    behind = pltpu.roll(values, quarter, values.ndim - 1)
    return jnp.where(lanes % HEAD_DIM < quarter, ahead, behind)


def project_kernel(x_ref, w_ref, gain_ref, first_ref, cos_ref, sin_ref, n_ref, keep_ref, send_ref):
    width = w_ref.shape[1] // 3
    rows = x_ref.shape[1] // 2
    values = x_ref[0].astype(jnp.float32)
    inverse = lax.rsqrt(jnp.mean(values * values, -1, keepdims=True) + epsilon)
    normed = (values * inverse * gain_ref[...]).astype(jnp.bfloat16)
    n_ref[0] = normed
    projected = jnp.dot(normed, w_ref[...], preferred_element_type=jnp.float32)
    cosine = cos_ref[0]
    sine = sin_ref[0]
    for part in range(2):
        block = projected[:, part * width : (part + 1) * width]
        turned = (block * cosine + half_swap(block) * sine).astype(jnp.bfloat16)
        keep_ref[0, :, part * width : (part + 1) * width] = turned[:rows]
        send_ref[0, :, part * width : (part + 1) * width] = turned[rows:]
    mixed = (
        0.5 * projected[:, 2 * width :] + 0.5 * first_ref[0].astype(jnp.float32)
    ).astype(jnp.bfloat16)
    keep_ref[0, :, 2 * width :] = mixed[:rows]
    send_ref[0, :, 2 * width :] = mixed[rows:]


def project(x, weights, gain, first, cosine, sine):
    count, rows, features = x.shape
    wide = weights.shape[1]
    third = wide // 3

    def by_step(*block):
        return pl.BlockSpec((1,) + block, lambda step: (step, 0, 0))

    return pl.pallas_call(
        project_kernel,
        grid=(count,),
        in_specs=[
            by_step(rows, features),
            pl.BlockSpec((features, wide), lambda step: (0, 0)),
            pl.BlockSpec((1, features), lambda step: (0, 0)),
            by_step(rows, third),
            by_step(rows, third),
            by_step(rows, third),
        ],
        out_specs=[by_step(rows, features), by_step(rows // 2, wide), by_step(rows // 2, wide)],
        out_shape=[
            jax.ShapeDtypeStruct((count, rows, features), jnp.bfloat16),
            jax.ShapeDtypeStruct((count, rows // 2, wide), jnp.bfloat16),
            jax.ShapeDtypeStruct((count, rows // 2, wide), jnp.bfloat16),
        ],
        compiler_params=pltpu.CompilerParams(vmem_limit_bytes=40 * 2**20),
        cost_estimate=pl.CostEstimate(
            flops=2 * count * rows * features * wide,
            bytes_accessed=count * rows * features * 4 + features * wide * 2,
            transcendentals=count * rows,
        ),
        name="project",
    )(x, weights, gain, first, cosine, sine)


def block_scores(head, query, keys, seg, start, scale):
    lanes = lax.broadcasted_iota(jnp.int32, query.shape, 1)
    mine = lanes // HEAD_DIM == head
    masked = jnp.where(mine, query, jnp.zeros_like(query))
    raw = (
        lax.dot_general(
            masked, keys, (((1,), (1,)), ((), ())), preferred_element_type=jnp.float32
        )
        * scale
    )
    row = start + lax.broadcasted_iota(jnp.int32, raw.shape, 0)
    column = lax.broadcasted_iota(jnp.int32, raw.shape, 1)
    valid = (column >= seg) & (column <= row)
    scores = jnp.where(valid, raw, masked_score)
    top = jnp.max(scores, -1, keepdims=True)
    weights = jnp.exp(scores - top)
    total = jnp.sum(weights, -1, keepdims=True)
    return masked, weights * (1.0 / total)


def attend_kernel(place_ref, k0_ref, k1_ref, r0_ref, r1_ref, seg_ref, o_ref, all_ref):
    b_place = place_ref[0]
    c_place = place_ref[1]
    count, rows, wide = k0_ref.shape
    width = wide // 3
    length = all_ref.shape[0]
    for b_flip, c_flip, ref in ((0, 0, k0_ref), (0, 1, k1_ref), (1, 0, r0_ref), (1, 1, r1_ref)):
        for step in range(count):
            block = (step * 2 + (b_place ^ b_flip)) * 2 + (c_place ^ c_flip)
            all_ref[pl.ds(pl.multiple_of(block * rows, rows), rows), :] = ref[step]
    size = min(256, length)
    scale = HEAD_DIM ** (-0.5)
    for start in range(0, length, size):
        stop = start + size
        query = all_ref[start:stop, :width]
        keys = all_ref[:stop, width : 2 * width]
        values = all_ref[:stop, 2 * width :]
        seg = seg_ref[start:stop, :]

        def one(head):
            masked, weights = block_scores(head, query, keys, seg, start, scale)
            return jnp.dot(
                weights.astype(jnp.bfloat16), values, preferred_element_type=jnp.float32
            )

        lanes = lax.broadcasted_iota(jnp.int32, (size, width), 1)
        result = one(0)
        for head in range(1, width // HEAD_DIM):
            result = jnp.where(lanes // HEAD_DIM == head, one(head), result)
        o_ref[start:stop, :] = result.astype(jnp.bfloat16)


def attend(places, k0, k1, r0, r1, seg):
    length = seg.shape[0]
    wide = k0.shape[-1]
    whole = pl.BlockSpec(memory_space=pltpu.VMEM)
    return pl.pallas_call(
        attend_kernel,
        in_specs=[pl.BlockSpec(memory_space=pltpu.SMEM)] + [whole] * 5,
        out_specs=[whole, whole],
        out_shape=[
            jax.ShapeDtypeStruct((length, wide // 3), jnp.bfloat16),
            jax.ShapeDtypeStruct((length, wide), jnp.bfloat16),
        ],
        compiler_params=pltpu.CompilerParams(vmem_limit_bytes=48 * 2**20),
        cost_estimate=pl.CostEstimate(
            flops=8 * length * length * 128,
            bytes_accessed=length * wide * 6,
            transcendentals=2 * length * length,
        ),
        name="attend",
    )(places, k0, k1, r0, r1, seg)


def attend_back_kernel(
    place_ref, all_ref, seg_ref, do_ref, cos_ref, sin_ref, k0_ref, k1_ref, r0_ref, r1_ref, dk_ref, dv_ref, full_ref
):
    b_place = place_ref[0]
    c_place = place_ref[1]
    count, rows, wide = k0_ref.shape
    width = wide // 3
    length = all_ref.shape[0]
    size = min(256, length)
    scale = HEAD_DIM ** (-0.5)
    dk_ref[...] = jnp.zeros_like(dk_ref)
    dv_ref[...] = jnp.zeros_like(dv_ref)
    for start in range(0, length, size):
        stop = start + size
        query = all_ref[start:stop, :width]
        keys = all_ref[:stop, width : 2 * width]
        values = all_ref[:stop, 2 * width :]
        seg = seg_ref[start:stop, :]
        out_grad = do_ref[start:stop, :]
        lanes = lax.broadcasted_iota(jnp.int32, (size, width), 1)

        def one(head):
            masked, weights = block_scores(head, query, keys, seg, start, scale)
            grad = jnp.where(lanes // HEAD_DIM == head, out_grad, jnp.zeros_like(out_grad))
            weight_grad = lax.dot_general(
                grad, values, (((1,), (1,)), ((), ())), preferred_element_type=jnp.float32
            )
            delta = jnp.sum(weights * weight_grad, -1, keepdims=True)
            score_grad = (weights * (weight_grad - delta)).astype(jnp.bfloat16)
            dv_ref[:stop, :] += lax.dot_general(
                weights.astype(jnp.bfloat16),
                grad,
                (((0,), (0,)), ((), ())),
                preferred_element_type=jnp.float32,
            )
            dk_ref[:stop, :] += lax.dot_general(
                score_grad, masked, (((0,), (0,)), ((), ())), preferred_element_type=jnp.float32
            )
            return jnp.dot(score_grad, keys, preferred_element_type=jnp.float32)

        query_grad = one(0)
        for head in range(1, width // HEAD_DIM):
            query_grad = jnp.where(lanes // HEAD_DIM == head, one(head), query_grad)
        query_grad = query_grad * scale
        cosine = cos_ref[start:stop, :]
        sine = sin_ref[start:stop, :]
        full_ref[start:stop, :width] = (
            query_grad * cosine - half_swap(query_grad) * sine
        ).astype(jnp.bfloat16)
    for start in range(0, length, size):
        stop = start + size
        key_grad = dk_ref[start:stop, :] * scale
        cosine = cos_ref[start:stop, :]
        sine = sin_ref[start:stop, :]
        full_ref[start:stop, width : 2 * width] = (
            key_grad * cosine - half_swap(key_grad) * sine
        ).astype(jnp.bfloat16)
        full_ref[start:stop, 2 * width :] = (0.5 * dv_ref[start:stop, :]).astype(jnp.bfloat16)
    for b_flip, c_flip, ref in ((0, 0, k0_ref), (0, 1, k1_ref), (1, 0, r0_ref), (1, 1, r1_ref)):
        for step in range(count):
            block = (step * 2 + (b_place ^ b_flip)) * 2 + (c_place ^ c_flip)
            ref[step] = full_ref[pl.ds(pl.multiple_of(block * rows, rows), rows), :]


def attend_back(places, everything, seg, out_grad, cosine, sine, count):
    length, wide = everything.shape
    rows = length // (4 * count)
    whole = pl.BlockSpec(memory_space=pltpu.VMEM)
    piece = jax.ShapeDtypeStruct((count, rows, wide), jnp.bfloat16)
    return pl.pallas_call(
        attend_back_kernel,
        in_specs=[pl.BlockSpec(memory_space=pltpu.SMEM)] + [whole] * 5,
        out_specs=[whole] * 4,
        out_shape=[piece] * 4,
        scratch_shapes=[
            pltpu.VMEM((length, wide // 3), jnp.float32),
            pltpu.VMEM((length, wide // 3), jnp.float32),
            pltpu.VMEM((length, wide), jnp.bfloat16),
        ],
        compiler_params=pltpu.CompilerParams(vmem_limit_bytes=56 * 2**20),
        cost_estimate=pl.CostEstimate(
            flops=20 * length * length * 128,
            bytes_accessed=length * wide * 8,
            transcendentals=2 * length * length,
        ),
        name="attend_back",
    )(places, everything, seg, out_grad, cosine, sine)


def turn_tables(positions, width):
    quarter = HEAD_DIM // 2
    freqs = jnp.power(10000.0, -jnp.arange(quarter, dtype=jnp.float32) / quarter)
    freqs = jnp.tile(freqs, width // quarter)
    signs = jnp.where(jnp.arange(width) % HEAD_DIM < quarter, -1.0, 1.0)
    angles = positions.astype(jnp.float32)[..., None] * freqs
    return jnp.cos(angles), jnp.sin(angles) * signs


def grid_body(tokens, v_first, segments, grad_out, w_qkv, w_out, w_gate_up, w_down, gain_attn, gain_ffn):
    bf16, f32 = jnp.bfloat16, jnp.float32
    row_count, shard_len, features = tokens.shape[1:]
    a, b, c, f = [lax.axis_index(name) for name in GRID]
    na = lax.axis_size("a")
    nd = 8 * na
    width = features // (2 * na)
    held = features // nd
    hidden = w_down.shape[0]
    length = 4 * na * shard_len
    tokens_here = row_count * shard_len
    bf_steps = ((0, 1), (1, 0), (1, 1))

    small = jnp.zeros((8, 128), f32)
    small = small.at[0, :held].set(gain_attn.astype(f32)).at[0, held : 2 * held].set(
        gain_ffn.astype(f32)
    )
    small = small.at[1].set(segments.reshape(-1).astype(f32))
    small = ordered(small, hop(small, c=1), c, 0)
    small = ordered(small, hop(small, f=1), f, 1)
    small = ordered(small, hop(small, b=1), b, 0)
    small = gather_a(small, a, 0)
    attn_gain = small[..., 0, :held].reshape(1, features)
    ffn_gain = small[..., 0, held : 2 * held].reshape(1, features)
    seg_all = pick(small[..., 1, :], f, 3).astype(jnp.int32)
    seg_all = jnp.moveaxis(seg_all.reshape(na, 2, 2, row_count, shard_len), 3, 0)

    mine = tokens[0]
    turned = jnp.where(b == 0, mine, mine[::-1]).reshape(tokens_here, features)
    group_tokens = gather_a(turned, a)
    group_tokens = (group_tokens, hop(group_tokens, c=1))

    blocks = w_qkv.reshape(held, 3, 2 * na, width).transpose(2, 0, 1, 3)
    blocks = blocks.reshape(2 * na, held, 3 * width)
    blocks = lax.all_to_all(blocks, ("a", "c"), 0, 0, tiled=True)
    blocks = blocks.reshape(na, 2, held, 3 * width)
    by_f = ordered(blocks, hop(blocks, f=1), f, 2)
    by_b = ordered(by_f, hop(by_f, b=1), b, 1)
    qkv_weights = by_b.reshape(features, 3 * width)

    first = v_first[0]
    first = jnp.where(b == 0, first, first[::-1]).reshape(tokens_here, 2 * na, width)
    first = lax.all_to_all(first.transpose(1, 0, 2), ("a", "c"), 0, 0, tiled=True)
    first = first.reshape(na, 2, tokens_here, width)

    base = jnp.arange(na, dtype=jnp.int32)[:, None, None] * 2 + b
    offset = jnp.arange(shard_len, dtype=jnp.int32)
    seg_rows = jnp.where(b == 0, seg_all, seg_all[::-1])
    keeps, sends, normed = [], [], []
    for flip in range(2):
        seg_group = pick(pick(seg_rows, b, 2), c ^ flip, 2)
        seg_group = jnp.swapaxes(seg_group, 0, 1)
        positions = (base * 2 + (c ^ flip)) * shard_len + offset - seg_group
        cosine, sine = turn_tables(positions.reshape(na, tokens_here), width)
        n_part, keep, send = project(
            group_tokens[flip],
            qkv_weights,
            attn_gain,
            pick(first, c ^ flip, 1),
            cosine,
            sine,
        )
        normed.append(n_part)
        keeps.append(keep)
        sends.append(hop(send, b=1))

    row_seg = pick(seg_all, b, 0).reshape(length)
    places = jnp.stack([b, c]).astype(jnp.int32)
    attention, everything = attend(places, *keeps, *sends, row_seg[:, None])

    out_parts = gather_a(w_out, a)
    by_f = ordered(out_parts, hop(out_parts, f=1), f, 1)
    by_b = ordered(by_f, hop(by_f, b=1), b, 1)
    full_out = ordered(by_b, hop(by_b, c=1), c, 2).reshape(features, features)

    units = w_gate_up.reshape(held, 2, na, 2, 2, 2, hidden).transpose(3, 5, 0, 1, 2, 4, 6)
    units = units.reshape(2, 2, held, 2, 2 * na * hidden)
    padded = -(-2 * na * hidden // 128) * 128
    units = jnp.pad(units, ((0, 0),) * 4 + ((0, padded - 2 * na * hidden),))
    units = units.reshape(2, 2, held, 2 * padded)
    got = jnp.zeros_like(units)
    got = lax.dynamic_update_slice(got, pick(pick(units, b, 0), f, 0)[None, None], (b, f, 0, 0))
    for b_flip, f_flip in bf_steps:
        part = pick(pick(units, b ^ b_flip, 0), f ^ f_flip, 0)
        part = hop(part, b=b_flip, f=f_flip)
        got = lax.dynamic_update_slice(got, part[None, None], (b ^ b_flip, f ^ f_flip, 0, 0))
    got = gather_a(got, a)
    gate_up_weights = ordered(got, hop(got, c=1), c, 2).reshape(features, 2 * padded)
    downs = gather_a(w_down, a)
    downs = ordered(downs, hop(downs, c=1), c, 1).reshape(2 * na * hidden, features)
    down_weights = jnp.pad(downs, ((0, padded - 2 * na * hidden), (0, 0)))

    def gather_bf(value):
        return jnp.concatenate([value] + [hop(value, b=i, f=j) for i, j in bf_steps], 0)

    def scatter_bf(parts):
        total = parts[0]
        for index, (i, j) in enumerate(bf_steps):
            total = total + hop(parts[index + 1].astype(bf16), b=i, f=j).astype(f32)
        return total

    grads = grad_out.reshape(tokens_here, features)
    group_grads = gather_bf(grads)

    attention = lax.all_to_all(
        attention.reshape(4 * na, shard_len, width), ("a", "b", "c"), 0, 0, tiled=True
    )
    attention = attention.reshape(na, 2, 2, shard_len, width).transpose(1, 3, 0, 2, 4)
    attention = attention.reshape(tokens_here, features)
    inputs = mine.reshape(tokens_here, features).astype(f32)
    branch_attn = jnp.dot(attention, full_out, preferred_element_type=f32)
    stream = inputs + branch_attn
    inverse_two = lax.rsqrt(jnp.mean(stream * stream, -1, keepdims=True) + epsilon)
    normed_two = (stream * inverse_two * ffn_gain).astype(bf16)
    group_two = gather_bf(normed_two)

    gate_up = jnp.dot(group_two, gate_up_weights, preferred_element_type=f32)
    gate = gate_up[:, :padded]
    upward = gate_up[:, padded:]
    sigmoid_gate = jax.nn.sigmoid(gate)
    silu_gate = gate * sigmoid_gate
    act = (silu_gate * upward).astype(bf16)
    contract_last = (((1,), (1,)), ((), ()))
    contract_first = (((0,), (0,)), ((), ()))
    act_grad = lax.dot_general(
        group_grads, down_weights, contract_last, preferred_element_type=f32
    )
    gate_grad = act_grad * upward * sigmoid_gate * (1.0 + gate * (1.0 - sigmoid_gate))
    gate_up_grad = jnp.concatenate([gate_grad, act_grad * silu_gate], -1).astype(bf16)
    two_grad = lax.dot_general(
        gate_up_grad, gate_up_weights, contract_last, preferred_element_type=f32
    )
    two_grad = scatter_bf(two_grad.reshape(4, tokens_here, features))
    branch_ffn = jnp.dot(act, down_weights, preferred_element_type=f32)
    branch_ffn = scatter_bf(branch_ffn.reshape(4, tokens_here, features))
    out = (stream + branch_ffn).astype(bf16).reshape(tokens.shape)

    def halve_c(parts, dim):
        other = pick(parts, 1 - c, dim).astype(bf16)
        return pick(parts, c, dim) + hop(other, c=1).astype(f32)

    def scatter_a(parts):
        total = pick(parts, a, 0)
        for step in range(1, na):
            total = total + hop(pick(parts, a ^ step, 0).astype(bf16), a=step).astype(f32)
        return total

    def exchange_bf(parts):
        result = jnp.zeros(parts.shape, bf16)
        own = pick(pick(parts, b, 0), f, 0).astype(bf16)
        result = lax.dynamic_update_slice(result, own[None, None], (b, f, 0, 0))
        for i, j in bf_steps:
            part = pick(pick(parts, b ^ i, 0), f ^ j, 0).astype(bf16)
            part = hop(part, b=i, f=j)
            result = lax.dynamic_update_slice(result, part[None, None], (b ^ i, f ^ j, 0, 0))
        return result.astype(f32)

    units_grad = lax.dot_general(
        group_two, gate_up_grad, contract_first, preferred_element_type=f32
    ).reshape(na, 2, 2, 2, held, 2 * padded)
    units_grad = exchange_bf(scatter_a(halve_c(units_grad, 2)))
    units_grad = units_grad.reshape(2, 2, held, 2, padded)[..., : 2 * na * hidden]
    units_grad = units_grad.reshape(2, 2, held, 2, na, 2, hidden).transpose(2, 3, 4, 0, 5, 1, 6)
    grad_gate_up = units_grad.reshape(held, -1)
    down_grad = lax.dot_general(act, group_grads, contract_first, preferred_element_type=f32)
    down_grad = down_grad[: 2 * na * hidden].reshape(na, 2, hidden, features)
    grad_down = scatter_a(halve_c(down_grad, 1))

    scaled = two_grad * ffn_gain
    stream_grad = (
        grads.astype(f32)
        + inverse_two * scaled
        - stream
        * (inverse_two * inverse_two * inverse_two)
        * jnp.mean(scaled * stream, -1, keepdims=True)
    )
    attn_grad = stream_grad.astype(bf16)
    heads_grad = lax.dot_general(
        attn_grad, full_out, contract_last, preferred_element_type=f32
    ).astype(bf16)
    heads_grad = heads_grad.reshape(2, shard_len, na, 2, width).transpose(2, 0, 3, 1, 4)
    heads_grad = lax.all_to_all(
        heads_grad.reshape(4 * na, shard_len, width), ("a", "b", "c"), 0, 0, tiled=True
    ).reshape(length, width)
    cosine, sine = turn_tables(jnp.arange(length, dtype=jnp.int32) - row_seg, width)
    k0, k1, r0, r1 = attend_back(places, everything, row_seg[:, None], heads_grad, cosine, sine, na)

    out_grad = lax.dot_general(
        attention, attn_grad, contract_first, preferred_element_type=f32
    ).reshape(na, 2, 2, 2, held, features)
    out_grad = halve_c(out_grad, 2)
    total = pick(pick(out_grad, b, 1), f, 1)
    for i, j in bf_steps:
        part = pick(pick(out_grad, b ^ i, 1), f ^ j, 1).astype(bf16)
        total = total + hop(part, b=i, f=j).astype(f32)
    grad_out_weights = scatter_a(total)

    pieces = []
    for keep, send in ((k0, r0), (k1, r1)):
        pieces.append(jnp.stack([keep, hop(send, b=1)], 1).reshape(-1, 3 * width))
    partial = [
        lax.dot_general(piece, qkv_weights, contract_last, preferred_element_type=f32).reshape(
            na, tokens_here, features
        )
        for piece in pieces
    ]
    one_grad = scatter_a(partial[0] + hop(partial[1].astype(bf16), c=1).astype(f32))
    qkv_grad = sum(
        lax.dot_general(
            n_part.reshape(-1, features), piece, contract_first, preferred_element_type=f32
        )
        for n_part, piece in zip(normed, pieces)
    ).reshape(na, 2, 2, 2, held, 3 * width)
    total = pick(pick(qkv_grad, b, 1), f, 2)
    for i, j in bf_steps:
        part = pick(pick(qkv_grad, b ^ i, 1), f ^ j, 2).astype(bf16)
        total = total + hop(part, b=i, f=j).astype(f32)
    total = total.astype(bf16).reshape(2 * na, held, 3 * width)
    total = lax.all_to_all(total, ("a", "c"), 0, 0, tiled=True).astype(f32)
    grad_qkv = total.reshape(2 * na, held, 3, width).transpose(1, 2, 0, 3).reshape(held, -1)

    values_grad = ordered(
        *[piece.reshape(na, tokens_here, 3 * width)[..., 2 * width :] for piece in pieces], c, 1
    )
    values_grad = lax.all_to_all(
        values_grad.reshape(2 * na, tokens_here, width), ("a", "c"), 0, 0, tiled=True
    )
    values_grad = values_grad.transpose(1, 0, 2).reshape(2, shard_len, features).astype(f32)
    values_grad = jnp.where(b == 0, values_grad, values_grad[::-1])

    one_grad = one_grad.reshape(2, shard_len, features)
    one_grad = jnp.where(b == 0, one_grad, one_grad[::-1]).reshape(tokens_here, features)
    inverse_one = lax.rsqrt(jnp.mean(inputs * inputs, -1, keepdims=True) + epsilon)
    scaled = one_grad * attn_gain
    input_grad = (
        stream_grad
        + inverse_one * scaled
        - inputs
        * (inverse_one * inverse_one * inverse_one)
        * jnp.mean(scaled * inputs, -1, keepdims=True)
    )

    attn_gain_grad = jnp.sum(w_qkv.astype(f32) * grad_qkv, -1) / gain_attn.astype(f32)
    ffn_gain_grad = jnp.sum(w_gate_up.astype(f32) * grad_gate_up, -1) / gain_ffn.astype(f32)

    squares = jnp.stack(
        [jnp.sum(x * x) for x in (stream, branch_attn, branch_ffn)]
    )
    sums = jnp.zeros((8, 128), f32).at[0, :3].set(squares)
    for axis in ("c", "f", "b"):
        sums = sums + hop(sums, **{axis: 1})
    parts = [sums] + [hop(sums, a=step) for step in range(1, na)]
    while len(parts) > 1:
        parts = [x + y for x, y in zip(parts[::2], parts[1::2])]
    stats = jnp.sqrt(parts[0][0, :3] / (tokens_here * features * nd))

    return (
        out,
        input_grad.reshape(tokens.shape),
        values_grad.reshape(tokens.shape),
        grad_qkv,
        grad_out_weights,
        grad_gate_up,
        grad_down,
        attn_gain_grad,
        ffn_gain_grad,
        stats,
    )


def fits(mesh):
    seq, fsdp = mesh.shape["seq"], mesh.shape["fsdp"]
    return seq == HEADS and fsdp == 2


def solution(mesh):
    if fits(mesh):
        grid = Mesh(mesh.devices.reshape(mesh.shape["seq"] // 4, 2, 2, 2), GRID)
        seq, every = ("a", "b", "c"), GRID
        body = grid_body
        fsdp = "f"
    else:
        grid, body = mesh, ring_body
        seq, every, fsdp = "seq", ("seq", "fsdp"), "fsdp"
    return jax.shard_map(
        body,
        mesh=grid,
        in_specs=(
            P(fsdp, None, seq, None),
            P(fsdp, None, seq, None),
            P(fsdp, None, seq),
            P(fsdp, None, seq, None),
            P(every, None),
            P(every, None),
            P(every, None),
            P(every, None),
            P(every),
            P(every),
        ),
        out_specs=(
            P(fsdp, None, seq, None),
            P(fsdp, None, seq, None),
            P(fsdp, None, seq, None),
            P(every, None),
            P(every, None),
            P(every, None),
            P(every, None),
            P(every),
            P(every),
            P(),
        ),
        check_vma=False,
    )
```

```python
import functools
import itertools
import math

import jax
import jax.numpy as jnp
from jax import lax
from jax.experimental import pallas as pl
from jax.experimental.pallas import tpu as pltpu
from jax.sharding import Mesh
from jax.sharding import PartitionSpec as P

HEADS = 16
HEAD_DIM = 64
FF = 2816
GRID = ("a", "b", "c", "f")
NA = 4


epsilon = 1e-06
masked_score = -1e30


def from_behind(value, axis, steps):
    count = lax.axis_size(axis)
    initial, last = (max(0, -steps), min(count, count - steps))
    return lax.ppermute(value, axis, [(source, source + steps) for source in range(initial, last)])


def shifted(shard, axis, by):
    size = lax.axis_size(axis)
    return lax.ppermute(shard, axis, [(i, (i + by) % size) for i in range(size)])


def rms_forward(values, gain):
    inverse_rms = lax.rsqrt(jnp.mean(values * values, -1, keepdims=True) + epsilon)
    return (values * inverse_rms * gain, inverse_rms)


def rms_backward(values, inverse_rms, gain, normed_grad):
    scaled = normed_grad * gain
    gain_grad = jnp.sum(normed_grad * values * inverse_rms, 0)
    input_grad = inverse_rms * scaled - values * (
        inverse_rms * inverse_rms * inverse_rms
    ) * jnp.mean(scaled * values, -1, keepdims=True)
    return (input_grad, gain_grad)


def rotation_tables(positions, head_dim):
    half_dim = head_dim // 2
    freqs = jnp.power(10000.0, -jnp.arange(half_dim, dtype=jnp.float32) / half_dim)
    angles = positions[..., None] * freqs
    return (jnp.cos(angles)[..., None, :], jnp.sin(angles)[..., None, :])


def rotate_forward(values, cosine, sine_part):
    half_dim = values.shape[-1] // 2
    first_half = values[..., :half_dim]
    second_half = values[..., half_dim:]
    return jnp.concatenate(
        [
            first_half * cosine - second_half * sine_part,
            second_half * cosine + first_half * sine_part,
        ],
        -1,
    )


def rotate_backward(values, cosine, sine_part):
    half_dim = values.shape[-1] // 2
    first_half = values[..., :half_dim]
    second_half = values[..., half_dim:]
    return jnp.concatenate(
        [
            first_half * cosine + second_half * sine_part,
            second_half * cosine - first_half * sine_part,
        ],
        -1,
    )


def over_blocks(visit, carried, members, block_rows):
    piece_rows = members[0].shape[1]
    splits = piece_rows // block_rows
    key_blocks = jnp.swapaxes(
        members[0].reshape(members[0].shape[0], splits, block_rows, members[0].shape[2]), 0, 1
    )
    value_blocks = jnp.swapaxes(
        members[1].reshape(members[1].shape[0], splits, block_rows, members[1].shape[2]), 0, 1
    )
    offsets = jnp.arange(splits, dtype=jnp.int32) * block_rows

    def advance(running, block_item):
        return (visit(running, block_item[0], block_item[1], block_item[2]), None)

    carried, unused = lax.scan(advance, carried, (key_blocks, value_blocks, offsets))
    return carried


def back_pair(
    query_heads,
    grad_heads,
    lse_part,
    delta_part,
    seg_part,
    index_part,
    key_heads,
    value_heads,
    key_start,
    score_scale,
):
    raw = (
        jnp.einsum("rqhd,rkhd->rhqk", query_heads, key_heads, preferred_element_type=jnp.float32)
        * score_scale
    )
    key_index = key_start + jnp.arange(key_heads.shape[1], dtype=jnp.int32)
    valid = (key_index[None, None, :] >= seg_part[:, :, None]) & (
        key_index[None, None, :] <= index_part[None, :, None]
    )
    valid = valid[:, None]
    scores = jnp.where(valid, raw, masked_score)
    weights = jnp.where(valid, jnp.exp(scores - lse_part[..., None]), 0.0)
    value_grad = jnp.einsum(
        "rhqk,rqhd->rkhd",
        weights.astype(jnp.bfloat16),
        grad_heads,
        preferred_element_type=jnp.float32,
    )
    weight_grad = jnp.einsum(
        "rqhd,rkhd->rhqk", grad_heads, value_heads, preferred_element_type=jnp.float32
    )
    score_grad = (weights * (weight_grad - delta_part[..., None])).astype(jnp.bfloat16)
    query_grad = (
        jnp.einsum("rhqk,rkhd->rqhd", score_grad, key_heads, preferred_element_type=jnp.float32)
        * score_scale
    )
    key_grad = (
        jnp.einsum("rhqk,rqhd->rkhd", score_grad, query_heads, preferred_element_type=jnp.float32)
        * score_scale
    )
    return (query_grad, key_grad, value_grad)


def ring_body(tokens, v_first, segments, grad_out, w_qkv, w_out, w_gate_up, w_down, gain_attn, gain_ffn):
    row_count = tokens.shape[1]
    shard_len = tokens.shape[2]
    features = tokens.shape[3]
    head_count = HEADS
    head_dim = HEAD_DIM
    score_scale = head_dim ** (-0.5)
    cycle_size = lax.axis_size("seq")
    device_index = lax.axis_index("seq")
    gathered = (
        lax.all_gather(w_qkv, ("seq", "fsdp"), axis=0, tiled=True),
        lax.all_gather(w_out, ("seq", "fsdp"), axis=0, tiled=True),
        lax.all_gather(w_gate_up, ("seq", "fsdp"), axis=0, tiled=True),
        lax.all_gather(w_down, ("seq", "fsdp"), axis=0, tiled=True),
        lax.all_gather(gain_attn, ("seq", "fsdp"), axis=0, tiled=True),
        lax.all_gather(gain_ffn, ("seq", "fsdp"), axis=0, tiled=True),
    )
    full_qkv, full_out, full_gate_up, full_down, full_gain_attn, full_gain_ffn = gathered
    attn_gain = full_gain_attn.astype(jnp.float32)
    ffn_gain = full_gain_ffn.astype(jnp.float32)
    inputs = tokens.reshape(-1, features).astype(jnp.float32)
    normed_one, inverse_one = rms_forward(inputs, attn_gain)
    normed_one_low = normed_one.astype(jnp.bfloat16)
    projected = jnp.dot(normed_one_low, full_qkv, preferred_element_type=jnp.float32)
    query_index = device_index * shard_len + jnp.arange(shard_len, dtype=jnp.int32)
    seg_rows = segments[0]
    positions = (query_index[None, :] - seg_rows).astype(jnp.float32)
    cosine, sine_part = rotation_tables(positions, head_dim)

    def split_heads(values):
        return values.reshape(row_count, -1, head_count, head_dim)

    queries = rotate_forward(split_heads(projected[:, :features]), cosine, sine_part).astype(
        jnp.bfloat16
    )
    keys_low = (
        rotate_forward(split_heads(projected[:, features : 2 * features]), cosine, sine_part)
        .astype(jnp.bfloat16)
        .reshape(row_count, shard_len, features)
    )
    mixed = (
        (
            0.5 * projected[:, 2 * features :]
            + 0.5 * v_first.reshape(-1, features).astype(jnp.float32)
        )
        .astype(jnp.bfloat16)
        .reshape(row_count, shard_len, features)
    )

    def scores_for(key_heads, key_start):
        raw = (
            jnp.einsum("rqhd,rkhd->rhqk", queries, key_heads, preferred_element_type=jnp.float32)
            * score_scale
        )
        key_index = key_start + jnp.arange(key_heads.shape[1], dtype=jnp.int32)
        valid = (key_index[None, None, :] >= seg_rows[:, :, None]) & (
            key_index[None, None, :] <= query_index[None, :, None]
        )
        valid = valid[:, None]
        return (jnp.where(valid, raw, masked_score), valid)

    def accumulate(carried, key_piece, value_piece, key_start):
        running_max, running_sum, weighted = carried
        key_heads = split_heads(key_piece)
        value_heads = split_heads(value_piece)
        scores, valid = scores_for(key_heads, key_start)
        new_max = jnp.maximum(running_max, jnp.max(scores, -1))
        weights = jnp.where(valid, jnp.exp(scores - new_max[..., None]), 0.0)
        factor = jnp.exp(running_max - new_max)
        running_sum = running_sum * factor + jnp.sum(weights, -1)
        weighted = weighted * jnp.transpose(factor, (0, 2, 1))[..., None] + jnp.einsum(
            "rhqk,rkhd->rqhd",
            weights.astype(jnp.bfloat16),
            value_heads,
            preferred_element_type=jnp.float32,
        )
        return (new_max, running_sum, weighted)

    def visit_forward(carried, key_piece, value_piece, key_start):
        return accumulate(carried, key_piece, value_piece, key_start)

    initial = (
        jnp.full((row_count, head_count, shard_len), masked_score, jnp.float32),
        jnp.zeros((row_count, head_count, shard_len), jnp.float32),
        jnp.zeros((row_count, shard_len, head_count, head_dim), jnp.float32),
    )
    running_max, running_sum, weighted = over_blocks(
        visit_forward,
        initial,
        (
            lax.all_gather(keys_low, "seq", axis=1, tiled=True),
            lax.all_gather(mixed, "seq", axis=1, tiled=True),
        ),
        shard_len,
    )
    attention = weighted / jnp.transpose(running_sum, (0, 2, 1))[..., None]
    log_total = running_max + jnp.log(running_sum)
    attn_low = attention.reshape(-1, features).astype(jnp.bfloat16)
    branch_attn = jnp.dot(attn_low, full_out, preferred_element_type=jnp.float32)
    stream = inputs + branch_attn
    normed_two, inverse_two = rms_forward(stream, ffn_gain)
    normed_two_low = normed_two.astype(jnp.bfloat16)
    gate_up = jnp.dot(normed_two_low, full_gate_up, preferred_element_type=jnp.float32)
    gate = gate_up[:, :FF]
    upward = gate_up[:, FF:]
    sigmoid_gate = jax.nn.sigmoid(gate)
    silu_gate = gate * sigmoid_gate
    hidden_low = (silu_gate * upward).astype(jnp.bfloat16)
    branch_ffn = jnp.dot(hidden_low, full_down, preferred_element_type=jnp.float32)
    output = stream + branch_ffn
    out_tokens = output.astype(jnp.bfloat16).reshape(tokens.shape)
    square_sums = jnp.stack(
        [
            jnp.sum(stream * stream),
            jnp.sum(branch_attn * branch_attn),
            jnp.sum(branch_ffn * branch_ffn),
        ]
    )
    square_totals = lax.psum(square_sums, ("seq", "fsdp"))
    stats = jnp.sqrt(square_totals / (stream.size * lax.axis_size(("seq", "fsdp"))))
    regathered = (
        lax.all_gather(w_qkv, ("seq", "fsdp"), axis=0, tiled=True),
        lax.all_gather(w_out, ("seq", "fsdp"), axis=0, tiled=True),
        lax.all_gather(w_gate_up, ("seq", "fsdp"), axis=0, tiled=True),
        lax.all_gather(w_down, ("seq", "fsdp"), axis=0, tiled=True),
        lax.all_gather(gain_attn, ("seq", "fsdp"), axis=0, tiled=True),
        lax.all_gather(gain_ffn, ("seq", "fsdp"), axis=0, tiled=True),
    )
    full_qkv, full_out, full_gate_up, full_down, full_gain_attn, full_gain_ffn = regathered
    attn_gain = full_gain_attn.astype(jnp.float32)
    ffn_gain = full_gain_ffn.astype(jnp.float32)
    ffn_grad_low = grad_out.reshape(-1, features)
    out_grad = ffn_grad_low.astype(jnp.float32)
    down_grad = jnp.dot(hidden_low.T, ffn_grad_low, preferred_element_type=jnp.float32)
    hidden_grad = jnp.dot(ffn_grad_low, full_down.T, preferred_element_type=jnp.float32)
    gate_grad = hidden_grad * upward * sigmoid_gate * (1.0 + gate * (1.0 - sigmoid_gate))
    upward_grad = hidden_grad * silu_gate
    gate_up_grad_low = jnp.concatenate([gate_grad, upward_grad], -1).astype(jnp.bfloat16)
    gate_up_weight_grad = jnp.dot(
        normed_two_low.T, gate_up_grad_low, preferred_element_type=jnp.float32
    )
    normed_two_grad = jnp.dot(gate_up_grad_low, full_gate_up.T, preferred_element_type=jnp.float32)
    stream_norm_grad, ffn_gain_grad = rms_backward(stream, inverse_two, ffn_gain, normed_two_grad)
    stream_grad = out_grad + stream_norm_grad
    attn_grad_low = stream_grad.astype(jnp.bfloat16)
    out_weight_grad = jnp.dot(attn_low.T, attn_grad_low, preferred_element_type=jnp.float32)
    attention_grad = (
        jnp.dot(attn_grad_low, full_out.T, preferred_element_type=jnp.float32)
        .astype(jnp.bfloat16)
        .reshape(row_count, shard_len, head_count, head_dim)
    )
    row_delta = jnp.einsum("rqhd,rqhd->rhq", attention_grad.astype(jnp.float32), attention)

    def back_visit(partials, query_part, key_heads, value_heads, key_start):
        query_heads, grad_heads, lse_part, delta_part, seg_part, index_part = query_part
        query_term, key_term, value_term = back_pair(
            query_heads,
            grad_heads,
            lse_part,
            delta_part,
            seg_part,
            index_part,
            key_heads,
            value_heads,
            key_start,
            score_scale,
        )
        return (
            partials[0] + query_term,
            partials[1] + key_term.reshape(partials[1].shape),
            partials[2] + value_term.reshape(partials[2].shape),
        )

    zero_rows = jnp.zeros((row_count, shard_len, features), jnp.float32)

    def back_turn(turn_index, running):
        key_piece, value_piece, key_grad, value_grad, query_grad = running
        source = (device_index - turn_index) % cycle_size
        query_grad, key_grad, value_grad = back_visit(
            (query_grad, key_grad, value_grad),
            (queries, attention_grad, log_total, row_delta, seg_rows, query_index),
            split_heads(key_piece),
            split_heads(value_piece),
            source * shard_len,
        )
        key_piece, value_piece = from_behind((key_piece, value_piece), "seq", 1)
        key_grad, value_grad = (
            shifted(key_grad.astype(jnp.bfloat16), "seq", 1).astype(key_grad.dtype),
            shifted(value_grad.astype(jnp.bfloat16), "seq", 1).astype(value_grad.dtype),
        )
        return (key_piece, value_piece, key_grad, value_grad, query_grad)

    start_state = (
        keys_low,
        mixed,
        zero_rows,
        zero_rows,
        jnp.zeros((row_count, shard_len, head_count, head_dim), jnp.float32),
    )
    final_state = lax.fori_loop(0, cycle_size, back_turn, start_state)
    key_grad_home = final_state[2]
    value_grad_home = final_state[3]
    query_grad_home = final_state[4]
    query_grad_rows = rotate_backward(query_grad_home, cosine, sine_part).reshape(-1, features)
    key_grad_rows = rotate_backward(split_heads(key_grad_home), cosine, sine_part).reshape(
        -1, features
    )
    mixed_grad = 0.5 * value_grad_home.reshape(-1, features)
    qkv_grad_low = jnp.concatenate([query_grad_rows, key_grad_rows, mixed_grad], -1).astype(
        jnp.bfloat16
    )
    qkv_weight_grad = jnp.dot(normed_one_low.T, qkv_grad_low, preferred_element_type=jnp.float32)
    normed_one_grad = jnp.dot(qkv_grad_low, full_qkv.T, preferred_element_type=jnp.float32)
    input_norm_grad, attn_gain_grad = rms_backward(inputs, inverse_one, attn_gain, normed_one_grad)
    input_grad = stream_grad + input_norm_grad
    owned = (
        lax.psum_scatter(qkv_weight_grad, ("seq", "fsdp"), scatter_dimension=0, tiled=True),
        lax.psum_scatter(out_weight_grad, ("seq", "fsdp"), scatter_dimension=0, tiled=True),
        lax.psum_scatter(gate_up_weight_grad, ("seq", "fsdp"), scatter_dimension=0, tiled=True),
        lax.psum_scatter(down_grad, ("seq", "fsdp"), scatter_dimension=0, tiled=True),
        lax.psum_scatter(attn_gain_grad, ("seq", "fsdp"), scatter_dimension=0, tiled=True),
        lax.psum_scatter(ffn_gain_grad, ("seq", "fsdp"), scatter_dimension=0, tiled=True),
    )
    return (
        out_tokens,
        input_grad.reshape(tokens.shape),
        mixed_grad.reshape(tokens.shape),
        owned[0],
        owned[1],
        owned[2],
        owned[3],
        owned[4],
        owned[5],
        stats,
    )


GATE = 3
FLIPS = ((0, 0), (0, 1), (1, 0), (1, 1))
LAST = (((1,), (1,)), ((), ()))
FIRST = (((0,), (0,)), ((), ()))
BF16, F32 = jnp.bfloat16, jnp.float32


def hop(value, tag, **flips):
    with jax.named_scope(tag):
        return flip_over(value, **flips)


def swap(value, tag, axes):
    with jax.named_scope(tag):
        return lax.all_to_all(value, axes, 0, 0, tiled=True)


def flip_over(value, **flips):
    axes = tuple(name for name in GRID if flips.get(name, 0))
    sizes = [lax.axis_size(name) for name in axes]
    pairs = []
    for source in itertools.product(*[range(size) for size in sizes]):
        origin, target = 0, 0
        for name, size, place in zip(axes, sizes, source):
            origin = origin * size + place
            target = target * size + (place ^ flips[name])
        pairs.append((origin, target))
    return lax.ppermute(value, axes if len(axes) > 1 else axes[0], pairs)


def ordered(mine, other, place, dim):
    first = jnp.where(place == 0, mine, other)
    second = jnp.where(place == 0, other, mine)
    return jnp.stack([first, second], dim)


def after(value, *earlier):
    return lax.optimization_barrier((value,) + earlier)[0]


def call(kernel, name, out_shape, inputs, scratch=(), flops=0, scalars=1, spare=8):
    def whole(x):
        return pl.BlockSpec(x.shape, lambda _: (0,) * len(x.shape), pipeline_mode=pl.Buffered(1))

    smem = pl.BlockSpec(memory_space=pltpu.SMEM)
    shapes = jax.tree.leaves(out_shape)
    moved = sum(x.size * x.dtype.itemsize for x in list(inputs) + shapes)
    held = sum(math.prod(x.shape) * jnp.dtype(x.dtype).itemsize for x in scratch)
    return pl.pallas_call(
        kernel,
        grid=(1,),
        in_specs=[smem] * scalars + [whole(x) for x in inputs[scalars:]],
        out_specs=jax.tree.map(whole, out_shape),
        out_shape=out_shape,
        scratch_shapes=list(scratch),
        compiler_params=pltpu.CompilerParams(vmem_limit_bytes=moved + held + spare * 2**20),
        cost_estimate=pl.CostEstimate(flops=flops, bytes_accessed=moved, transcendentals=0),
        name=name,
    )(*inputs)


def like(*shape, dtype=BF16):
    return jax.ShapeDtypeStruct(shape, dtype)


def device_row(a, b, c, f):
    return ((a * 2 + b) * 2 + c) * 2 + f


def rows_at(index, count):
    return pl.ds(pl.multiple_of(index * count, count), count)


def half_swap(values):
    lanes = lax.broadcasted_iota(jnp.int32, values.shape, values.ndim - 1)
    quarter = HEAD_DIM // 2
    width = values.shape[-1]
    ahead = pltpu.roll(values, width - quarter, values.ndim - 1)
    behind = pltpu.roll(values, quarter, values.ndim - 1)
    return jnp.where(lanes % HEAD_DIM < quarter, ahead, behind)


def unit_room(hidden):
    return -(-hidden // 16) * 16


def prepare_kernel(place_ref, x_ref, w_ref, seg_ref, gain_ref, x_out_ref, out_ref):
    b, c, f = place_ref[1], place_ref[2], place_ref[3]
    rows = x_ref.shape[1]
    for r in range(2):
        x_out_ref[r * rows : (r + 1) * rows, :] = x_ref[b ^ r]
    held = w_ref.shape[0]
    parts, _, width = out_ref.shape
    features = parts * width
    lanes = lax.broadcasted_iota(jnp.int32, (1, width), 1)
    mine = lanes // held == c * 2 + f
    lines = []
    for k in range(2):
        gain = jnp.concatenate([gain_ref[k : k + 1, :].astype(F32)] * (width // held), 1)
        lines.append(jnp.where(mine, gain, 0.0))
    starts = jnp.concatenate([seg_ref[0:1, :], seg_ref[1:2, :]], 1)
    lines.append((starts >> 8).astype(F32))
    lines.append((starts & 255).astype(F32))
    row = lax.broadcasted_iota(jnp.int32, (16, width), 0)
    small = jnp.zeros((16, width), F32)
    for k, line in enumerate(lines):
        small = jnp.where(row == k, line, small)
    small = small.astype(BF16)
    for p in range(parts):
        for part in range(3):
            start = part * features + p * width
            out_ref[p, part * held : (part + 1) * held, :] = w_ref[:, start : start + width]
        out_ref[p, 3 * held :, :] = small


def by_heads_kernel(x_ref, out_ref):
    rows, width = out_ref.shape[1:]
    for p in range(x_ref.shape[2] // width):
        for r in range(2):
            out_ref[((p // 2) * 2 + r) * 2 + p % 2] = x_ref[r, :, p * width : (p + 1) * width]


def join_units_kernel(u0_ref, u1_ref, u2_ref, u3_ref, d_ref, out_ref):
    held, wide = u0_ref.shape
    for k, ref in enumerate((u0_ref, u1_ref, u2_ref, u3_ref)):
        out_ref[k * held : (k + 1) * held, :] = ref[...]
    hidden, features = d_ref.shape
    room = unit_room(hidden)
    lead = room * features // wide
    rest = room - lead
    base = 4 * held
    out_ref[base:, :features] = d_ref[:lead, :]
    gap = jnp.zeros((room - hidden, wide - features), BF16)
    for part in range(features // (wide - features)):
        lanes = slice(part * (wide - features), (part + 1) * (wide - features))
        here = slice(base + part * rest, base + (part + 1) * rest)
        out_ref[here, features:] = jnp.concatenate([d_ref[lead:, lanes], gap], 0)


def spread_digits(values):
    row = lax.broadcasted_iota(jnp.int32, values.shape, 0)
    first = values.astype(BF16).astype(F32)
    second = (values - first).astype(BF16).astype(F32)
    third = values - first - second
    picked = jnp.where(row == 0, first, jnp.where(row == 1, second, third))
    return jnp.where(row < 3, picked, 0.0).astype(BF16)


def add_digits(tile):
    return jnp.broadcast_to(jnp.sum(tile.astype(F32), 0, keepdims=True), tile.shape)


def spread_kernel(place_ref, w_ref, out_ref, all_ref):
    half = w_ref.shape[1] // 2
    wide = out_ref.shape[2] // 2
    na = NA
    hidden = half // (8 * na)
    room = unit_room(hidden)
    values = w_ref[...]
    gap = jnp.zeros((values.shape[0], room - hidden), values.dtype)
    for b, f in FLIPS:
        for side in range(2):
            parts = []
            for a, c in itertools.product(range(na), range(2)):
                start = side * half + hidden * device_row(a, b, c, f)
                parts += [values[:, start : start + hidden], gap]
            if wide > 2 * na * room:
                parts.append(jnp.zeros((values.shape[0], wide - 2 * na * room), values.dtype))
            all_ref[b * 2 + f, :, side * wide : (side + 1) * wide] = jnp.concatenate(parts, 1)
    for k, (i, j) in enumerate(FLIPS):
        out_ref[k] = all_ref[(place_ref[1] ^ i) * 2 + (place_ref[3] ^ j)]


def gather_units_kernel(
    place_ref, p0, p1, p2, p3, d_ref, w_ref, gain_ref, out_ref, gain_grad_ref, down_ref, part_ref
):
    hidden, features = down_ref.shape
    room = unit_room(hidden)
    lead = d_ref.shape[0]
    rest = room - lead
    down_ref[:lead, :] = d_ref[:, :features].astype(F32)
    size = d_ref.shape[1] - features
    for part in range(features // size):
        block = d_ref[part * rest : (part + 1) * rest, features:].astype(F32)
        down_ref[lead:, part * size : (part + 1) * size] = block[: hidden - lead, :]
    b, f = place_ref[1], place_ref[3]
    for (i, j), ref in zip(FLIPS, (p0, p1, p2, p3)):
        part_ref[(b ^ i) * 2 + (f ^ j)] = ref[...]
    half = w_ref.shape[1] // 2
    wide = part_ref.shape[2] // 2
    na = NA
    hidden = half // (8 * na)
    room = unit_room(hidden)
    total = 0.0
    for side in range(2):
        parts = []
        for a, b, c, f in itertools.product(range(na), range(2), range(2), range(2)):
            start = side * wide + room * (a * 2 + c)
            parts.append(part_ref[b * 2 + f][:, start : start + hidden].astype(F32))
        grad = jnp.concatenate(parts, 1)
        out_ref[:, side * half : (side + 1) * half] = grad
        weights = w_ref[:, side * half : (side + 1) * half].astype(F32)
        total = total + jnp.sum(weights * grad, -1, keepdims=True)
    gain_grad_ref[...] = total / gain_ref[...]


def assemble_kernel(part_ref, w_ref, gain_ref):
    _, groups, _, width = part_ref.shape
    held = w_ref.shape[0] // (4 * groups)
    for a, b in itertools.product(range(groups // 2), range(2)):
        total = 0.0
        for c, f in itertools.product(range(2), range(2)):
            k, s = b * 2 + f, a * 2 + c
            row = device_row(a, b, c, f) * held
            for part in range(3):
                w_ref[row : row + held, part * width : (part + 1) * width] = part_ref[
                    k, s, part * held : (part + 1) * held, :
                ]
            total = total + part_ref[k, s, 3 * held :, :].astype(F32)
        gain_ref[:, (a * 2 + b) * width : (a * 2 + b + 1) * width] = total[:8]


def project_kernel(
    place_ref, x_ref, w_ref, gain_ref, cos_ref, sin_ref, n_ref, keep_ref, send_ref
):
    width = w_ref.shape[1] // 3
    rows = x_ref.shape[1] // 2
    values = x_ref[0].astype(F32)
    inverse = lax.rsqrt(jnp.mean(values * values, -1, keepdims=True) + epsilon)
    normed = (values * inverse * gain_ref[0:1, :]).astype(BF16)
    n_ref[0] = normed
    projected = jnp.dot(normed, w_ref[...], preferred_element_type=F32)
    cosine = cos_ref[0, 0]
    sine = sin_ref[0, 0]
    for part in range(2):
        block = projected[:, part * width : (part + 1) * width]
        turned = (block * cosine + half_swap(block) * sine).astype(BF16)
        keep_ref[0, :, part * width : (part + 1) * width] = turned[:rows]
        send_ref[0, :, part * width : (part + 1) * width] = turned[rows:]
    values = projected[:, 2 * width :].astype(BF16)
    keep_ref[0, :, 2 * width :] = values[:rows]
    send_ref[0, :, 2 * width :] = values[rows:]


def project(places, flip, x, weights, gains, cosine, sine):
    count, rows, features = x.shape
    wide = weights.shape[1]
    third = wide // 3

    def by_step(*block):
        return pl.BlockSpec((1,) + block, lambda step, place: (step, 0, 0))

    def table_map(step, place):
        return (step ^ place[0], place[2] ^ flip, 0, 0)

    def fixed(step, place):
        return (0, 0)

    table = pl.BlockSpec((1, 1, rows, third), table_map)
    return pl.pallas_call(
        project_kernel,
        grid_spec=pltpu.PrefetchScalarGridSpec(
            num_scalar_prefetch=1,
            grid=(count,),
            in_specs=[
                by_step(rows, features),
                pl.BlockSpec((features, wide), fixed),
                pl.BlockSpec((8, features), fixed),
                table,
                table,
            ],
            out_specs=[by_step(rows, features), by_step(rows // 2, wide), by_step(rows // 2, wide)],
        ),
        out_shape=[
            like(count, rows, features),
            like(count, rows // 2, wide),
            like(count, rows // 2, wide),
        ],
        compiler_params=pltpu.CompilerParams(vmem_limit_bytes=8 * 2**20),
        cost_estimate=pl.CostEstimate(
            flops=2 * count * rows * features * wide,
            bytes_accessed=count * rows * features * 4 + features * wide * 2,
            transcendentals=count * rows,
        ),
        name="project",
    )(places, x, weights, gains, cosine, sine)


def block_scores(head, query, keys, seg, start, scale):
    lanes = lax.broadcasted_iota(jnp.int32, query.shape, 1)
    masked = jnp.where(lanes // HEAD_DIM == head, query, jnp.zeros_like(query))
    raw = lax.dot_general(masked, keys, LAST, preferred_element_type=F32) * scale
    row = start + lax.broadcasted_iota(jnp.int32, raw.shape, 0)
    column = lax.broadcasted_iota(jnp.int32, raw.shape, 1)
    valid = (column >= seg) & (column <= row)
    scores = jnp.where(valid, raw, masked_score)
    top = jnp.max(scores, -1, keepdims=True)
    weights = jnp.exp(scores - top)
    total = jnp.sum(weights, -1, keepdims=True)
    return masked, weights * (1.0 / total)


def row_block(place_ref, step, b_flip, c_flip):
    a, b, c = place_ref[0] ^ step, place_ref[1] ^ b_flip, place_ref[2] ^ c_flip
    return (a * 2 + b) * 2 + c


def attend_kernel(
    place_ref, k0_ref, k1_ref, r0_ref, r1_ref, seg_ref, first_ref, o_ref, all_ref
):
    count, rows, wide = k0_ref.shape
    width = wide // 3
    length = all_ref.shape[0]
    for (b_flip, c_flip), ref in zip(FLIPS, (k0_ref, k1_ref, r0_ref, r1_ref)):
        for step in range(count):
            all_ref[rows_at(row_block(place_ref, step, b_flip, c_flip), rows), :] = ref[step]
    size = min(256, length)
    scale = HEAD_DIM ** (-0.5)
    for start in range(0, length, size):
        stop = start + size
        own = all_ref[start:stop, 2 * width :].astype(F32)
        first = first_ref[start:stop, :].astype(F32)
        all_ref[start:stop, 2 * width :] = (0.5 * own + 0.5 * first).astype(BF16)
        query = all_ref[start:stop, :width]
        keys = all_ref[:stop, width : 2 * width]
        values = all_ref[:stop, 2 * width :]
        seg = seg_ref[start:stop, :]

        def one(head):
            _, weights = block_scores(head, query, keys, seg, start, scale)
            return jnp.dot(weights.astype(BF16), values, preferred_element_type=F32)

        lanes = lax.broadcasted_iota(jnp.int32, (size, width), 1)
        result = one(0)
        for head in range(1, width // HEAD_DIM):
            result = jnp.where(lanes // HEAD_DIM == head, one(head), result)
        o_ref[start:stop, :] = result.astype(BF16)


def attend_back_kernel(
    place_ref, all_ref, seg_ref, do_ref, cos_ref, sin_ref, k0_ref, k1_ref, r0_ref, r1_ref, dk_ref, dv_ref, full_ref
):
    count, rows, wide = k0_ref.shape
    width = wide // 3
    length = all_ref.shape[0]
    size = min(256, length)
    scale = HEAD_DIM ** (-0.5)
    dk_ref[...] = jnp.zeros_like(dk_ref)
    dv_ref[...] = jnp.zeros_like(dv_ref)
    for start in range(0, length, size):
        stop = start + size
        query = all_ref[start:stop, :width]
        keys = all_ref[:stop, width : 2 * width]
        values = all_ref[:stop, 2 * width :]
        seg = seg_ref[start:stop, :]
        out_grad = do_ref[start:stop, :]
        lanes = lax.broadcasted_iota(jnp.int32, (size, width), 1)

        def one(head):
            masked, weights = block_scores(head, query, keys, seg, start, scale)
            grad = jnp.where(lanes // HEAD_DIM == head, out_grad, jnp.zeros_like(out_grad))
            weight_grad = lax.dot_general(grad, values, LAST, preferred_element_type=F32)
            delta = jnp.sum(weights * weight_grad, -1, keepdims=True)
            score_grad = (weights * (weight_grad - delta)).astype(BF16)
            dv_ref[:stop, :] += lax.dot_general(
                weights.astype(BF16), grad, FIRST, preferred_element_type=F32
            )
            dk_ref[:stop, :] += lax.dot_general(
                score_grad, masked, FIRST, preferred_element_type=F32
            )
            return jnp.dot(score_grad, keys, preferred_element_type=F32)

        query_grad = one(0)
        for head in range(1, width // HEAD_DIM):
            query_grad = jnp.where(lanes // HEAD_DIM == head, one(head), query_grad)
        query_grad = query_grad * scale
        cosine = cos_ref[start:stop, :]
        sine = sin_ref[start:stop, :]
        full_ref[start:stop, :width] = (
            query_grad * cosine - half_swap(query_grad) * sine
        ).astype(BF16)
    for start in range(0, length, size):
        stop = start + size
        key_grad = dk_ref[start:stop, :] * scale
        cosine = cos_ref[start:stop, :]
        sine = sin_ref[start:stop, :]
        full_ref[start:stop, width : 2 * width] = (
            key_grad * cosine - half_swap(key_grad) * sine
        ).astype(BF16)
        full_ref[start:stop, 2 * width :] = (0.5 * dv_ref[start:stop, :]).astype(BF16)
    for (b_flip, c_flip), ref in zip(FLIPS, (k0_ref, k1_ref, r0_ref, r1_ref)):
        for step in range(count):
            ref[step] = full_ref[rows_at(row_block(place_ref, step, b_flip, c_flip), rows), :]


def out_kernel(
    place_ref, heads_ref, own_ref, other_ref, x_ref, gain_ref,
    o_ref, w_ref, h_ref, n_ref, sum_ref,
):
    a, b, c, f = [place_ref[k] for k in range(4)]
    rows, width = heads_ref.shape[1:]
    na = NA
    held = other_ref.shape[2]
    for k, (i, j) in enumerate(FLIPS):
        for step in range(na):
            for c_flip, ref in enumerate((own_ref, other_ref)):
                row = device_row(a ^ step, b ^ i, c ^ c_flip, f ^ j)
                w_ref[rows_at(row, held), :] = ref[k, step]
    for p in range(o_ref.shape[1] // width):
        for r in range(2):
            o_ref[r * rows : (r + 1) * rows, p * width : (p + 1) * width] = heads_ref[
                ((p // 2) * 2 + r) * 2 + p % 2
            ]
    branch = jnp.dot(o_ref[...], w_ref[...], preferred_element_type=F32)
    stream = x_ref[...].astype(F32) + branch
    h_ref[...] = stream
    inverse = lax.rsqrt(jnp.mean(stream * stream, -1, keepdims=True) + epsilon)
    n_ref[...] = (stream * inverse * gain_ref[1:2, :]).astype(BF16)
    sum_ref[0:1, :] = jnp.sum(stream * stream, 0, keepdims=True)
    sum_ref[1:2, :] = jnp.sum(branch * branch, 0, keepdims=True)


def feed_kernel(
    place_ref, n0, n1, n2, n3, g0, g1, g2, g3, w_ref,
    act_ref, dgu_ref, back0_ref, back_ref, down_ref, n_ref, g_ref, full_ref,
):
    a, b, c, f = [place_ref[k] for k in range(4)]
    na, wide = w_ref.shape[0] // 2, w_ref.shape[2]
    padded, features = down_ref.shape
    held = features // (8 * na)
    rows = n0.shape[0]
    room = padded // (2 * na)
    lead = room * features // wide
    rest = room - lead
    for s, (da, dc) in enumerate(itertools.product(range(na), range(2))):
        for k, (i, j) in enumerate(FLIPS):
            row = device_row(da, b ^ i, dc, f ^ j)
            full_ref[rows_at(row, held), :] = w_ref[s, k * held : (k + 1) * held, :]
        base = 4 * held
        start = s * room
        down_ref[start : start + lead, :] = w_ref[s, base:, :features]
        for part in range(features // (wide - features)):
            lanes = slice(part * (wide - features), (part + 1) * (wide - features))
            here = slice(base + part * rest, base + (part + 1) * rest)
            down_ref[start + lead : start + room, lanes] = w_ref[s, here, features:]
    for k, (n_part, g_part) in enumerate(zip((n0, n1, n2, n3), (g0, g1, g2, g3))):
        n_ref[k * rows : (k + 1) * rows, :] = n_part[...]
        g_ref[k * rows : (k + 1) * rows, :] = g_part[...]
    size = 256
    for start in range(0, padded, size):
        here = slice(start, start + size)
        there = slice(padded + start, padded + start + size)
        gate = jnp.dot(n_ref[...], full_ref[:, here], preferred_element_type=F32)
        upward = jnp.dot(n_ref[...], full_ref[:, there], preferred_element_type=F32)
        act_grad = lax.dot_general(g_ref[...], down_ref[here, :], LAST, preferred_element_type=F32)
        sigmoid_gate = jax.nn.sigmoid(gate)
        silu_gate = gate * sigmoid_gate
        act_ref[:, here] = (silu_gate * upward).astype(BF16)
        dgu_ref[:, here] = (
            act_grad * upward * sigmoid_gate * (1.0 + gate * (1.0 - sigmoid_gate))
        ).astype(BF16)
        dgu_ref[:, there] = (act_grad * silu_gate).astype(BF16)
    for k in range(4):
        back = lax.dot_general(
            dgu_ref[k * rows : (k + 1) * rows, :], full_ref[...], LAST, preferred_element_type=F32
        )
        if k == 0:
            back0_ref[...] = back
        else:
            back_ref[k - 1] = back.astype(BF16)


def feed_grads_kernel(
    place_ref, n0, n1, n2, n3, g0, g1, g2, g3, act_ref, dgu_ref, down_ref,
    out_ref, ffn0_ref, ffn_ref, n_ref, g_ref,
):
    b, f = place_ref[1], place_ref[3]
    rows = n0.shape[0]
    for k, (n_part, g_part) in enumerate(zip((n0, n1, n2, n3), (g0, g1, g2, g3))):
        n_ref[k * rows : (k + 1) * rows, :] = n_part[...]
        g_ref[k * rows : (k + 1) * rows, :] = g_part[...]
    groups, _, wide = out_ref.shape
    padded, features = down_ref.shape
    held = features // (4 * groups)
    room = padded // groups
    size = 512
    for start in range(0, wide, size):
        here = slice(start, start + size)
        grad = lax.dot_general(
            n_ref[...], dgu_ref[:, here], FIRST, preferred_element_type=F32
        ).astype(BF16)
        for s, (da, dc) in enumerate(itertools.product(range(groups // 2), range(2))):
            for db, df in FLIPS:
                row = device_row(da, db, dc, df) * held
                k = (b ^ db) * 2 + (f ^ df)
                out_ref[s, rows_at(k, held), here] = grad[row : row + held, :]
    grad = lax.dot_general(act_ref[...], g_ref[...], FIRST, preferred_element_type=F32).astype(BF16)
    lead = room * features // wide
    rest = room - lead
    base = 4 * held
    for s in range(groups):
        block = grad[room * s : room * (s + 1), :]
        out_ref[s, base:, :features] = block[:lead, :]
        for part in range(features // (wide - features)):
            lanes = slice(part * (wide - features), (part + 1) * (wide - features))
            there = slice(base + part * rest, base + (part + 1) * rest)
            out_ref[s, there, features:] = block[lead:, lanes]
    for k in range(4):
        ffn = jnp.dot(
            act_ref[k * rows : (k + 1) * rows, :], down_ref[...], preferred_element_type=F32
        )
        if k == 0:
            ffn0_ref[...] = ffn
        else:
            ffn_ref[k - 1] = ffn.astype(BF16)


def norm_back(values, gain, normed_grad):
    inverse = lax.rsqrt(jnp.mean(values * values, -1, keepdims=True) + epsilon)
    scaled = normed_grad * gain
    return inverse * scaled - values * (inverse * inverse * inverse) * jnp.mean(
        scaled * values, -1, keepdims=True
    )


def stream_back_kernel(
    p0, p1, p2, p3, h_ref, gain_ref, g_ref, w_ref, dh_ref, da_ref, do_ref
):
    normed_grad = p0[...] + p1[...].astype(F32) + p2[...].astype(F32) + p3[...].astype(F32)
    stream = h_ref[...]
    stream_grad = g_ref[...].astype(F32) + norm_back(stream, gain_ref[1:2, :], normed_grad)
    dh_ref[...] = stream_grad
    low = stream_grad.astype(BF16)
    da_ref[...] = low
    heads = lax.dot_general(low, w_ref[...], LAST, preferred_element_type=F32).astype(BF16)
    rows, width = do_ref.shape[1:]
    for p in range(heads.shape[1] // width):
        for r in range(2):
            do_ref[((p // 2) * 2 + r) * 2 + p % 2] = heads[
                r * rows : (r + 1) * rows, p * width : (p + 1) * width
            ]


def fill_pairs(d_ref, keep_ref, recv_ref):
    count, rows, _ = keep_ref.shape
    for step in range(count):
        base = 2 * rows * step
        d_ref[base : base + rows, :] = keep_ref[step]
        d_ref[base + rows : base + 2 * rows, :] = recv_ref[step]


def unproject_other_kernel(keep_ref, recv_ref, w_ref, dn_ref, d_ref):
    fill_pairs(d_ref, keep_ref, recv_ref)
    count, rows, _ = dn_ref.shape
    for step in range(count):
        back = lax.dot_general(
            d_ref[rows * step : rows * (step + 1), :], w_ref[...], LAST, preferred_element_type=F32
        )
        dn_ref[step] = back.astype(BF16)


def unproject_own_kernel(keep_ref, recv_ref, w_ref, other_ref, own_ref, send_ref, d_ref):
    fill_pairs(d_ref, keep_ref, recv_ref)
    count, rows, _ = other_ref.shape
    for step in range(count):
        back = lax.dot_general(
            d_ref[rows * step : rows * (step + 1), :], w_ref[...], LAST, preferred_element_type=F32
        )
        back = back + other_ref[step].astype(F32)
        if step == 0:
            own_ref[...] = back
        else:
            send_ref[step - 1] = back.astype(BF16)


def qkv_grads_kernel(
    place_ref, k0_ref, r0_ref, n0_ref, k1_ref, r1_ref, n1_ref, stat_ref,
    own_ref, send_ref, d_ref, total_ref,
):
    b, f = place_ref[1], place_ref[3]
    count, rows, wide = k0_ref.shape
    width = wide // 3
    features = n0_ref.shape[2]
    grads = []
    for keep_ref, recv_ref, n_ref in ((k0_ref, r0_ref, n0_ref), (k1_ref, r1_ref, n1_ref)):
        fill_pairs(d_ref, keep_ref, recv_ref)
        tokens = n_ref[...].reshape(2 * rows * count, features)
        grad = lax.dot_general(tokens, d_ref[...], FIRST, preferred_element_type=F32)
        if not grads:
            total_ref[...] = grad
        else:
            total_ref[...] += grad
        grads.append(keep_ref)
    held = features // (8 * count)
    block = 3 * held
    bottom = block * 2 * count
    own_ref[bottom:, :] = stat_ref[...]
    for k in range(3):
        send_ref[k, bottom:, :] = spread_digits(stat_ref[...])
    for k, (i, j) in enumerate(FLIPS):
        for s, (da, dc) in enumerate(itertools.product(range(count), range(2))):
            piece = total_ref[rows_at(device_row(da, b ^ i, dc, f ^ j), held), :]
            for part in range(3):
                lanes = piece[:, part * width : (part + 1) * width]
                there = slice(s * block + part * held, s * block + (part + 1) * held)
                if k == 0:
                    own_ref[there, :] = lanes
                else:
                    send_ref[k - 1, there, :] = lanes.astype(BF16)


def qkv_sum_kernel(
    place_ref, own_ref, r1_ref, r2_ref, r3_ref, k0_ref, v0_ref, k1_ref, v1_ref, out_ref
):
    a, c = place_ref[0], place_ref[2]
    parts, rows, width = out_ref.shape
    count, length, _ = k0_ref.shape
    block = rows - 16 - 2 * length
    bottom = parts * block
    received = (r1_ref, r2_ref, r3_ref)
    stats = own_ref[bottom:, :]
    for ref in received:
        stats = stats + add_digits(ref[bottom:, :])
    digits = spread_digits(stats)
    for p in range(parts):
        here = slice(p * block, (p + 1) * block)
        total = own_ref[here, :]
        for ref in received:
            total = total + ref[here, :].astype(F32)
        out_ref[p, :block, :] = total.astype(BF16)
        out_ref[p, block : block + 16, :] = digits
    base = block + 16
    for c_flip, pair in enumerate(((k0_ref, v0_ref), (k1_ref, v1_ref))):
        for step in range(count):
            p = (a ^ step) * 2 + (c ^ c_flip)
            for r, ref in enumerate(pair):
                there = slice(base + r * length, base + (r + 1) * length)
                out_ref[p, there, :] = ref[step, :, 2 * width :]


def out_grads_kernel(place_ref, o_ref, da_ref, own_ref, send_ref, total_ref):
    c = place_ref[2]
    total_ref[...] = lax.dot_general(o_ref[...], da_ref[...], FIRST, preferred_element_type=F32)
    groups, two, held, _ = own_ref.shape
    for g in range(groups):
        for k in range(two):
            own_ref[g, k] = total_ref[rows_at((g * 2 + c) * 2 + k, held), :]
            send_ref[g, k] = total_ref[rows_at((g * 2 + (1 - c)) * 2 + k, held), :].astype(BF16)


def out_grads_core_kernel(own_ref, recv_ref, out_ref):
    groups, two, _, _ = own_ref.shape
    for g in range(groups):
        for k in range(two):
            total = own_ref[g, k] + recv_ref[g, k].astype(F32)
            out_ref[g * two + k] = total.astype(BF16)


def out_grads_sum_kernel(part_ref, out_ref):
    total = part_ref[0].astype(F32)
    for k in range(1, part_ref.shape[0]):
        total = total + part_ref[k].astype(F32)
    out_ref[...] = total


def finish_out_kernel(h_ref, ffn_ref, r1_ref, r2_ref, r3_ref, sum_ref, out_ref, total_ref):
    branch = ffn_ref[...]
    for ref in (r1_ref, r2_ref, r3_ref):
        branch = branch + ref[...].astype(F32)
    out_ref[...] = (h_ref[...] + branch).astype(BF16)
    squares = jnp.sum(branch * branch, 0, keepdims=True)
    lanes = lax.broadcasted_iota(jnp.int32, total_ref.shape, 1)
    totals = jnp.zeros(total_ref.shape, F32)
    for k in range(3):
        values = squares if k == 2 else sum_ref[k : k + 1, :]
        totals = jnp.where(lanes == k, jnp.sum(values, -1, keepdims=True), totals)
    total_ref[...] = totals


def finish_kernel(
    entries, place_ref, part_ref, w_ref, gain_ref, out_ref, gain_grad_ref, stat_ref, first_ref
):
    parts, _, width = part_ref.shape
    base = 3 * out_ref.shape[0]
    rows = first_ref.shape[1]
    stats = 0.0
    for p in range(parts):
        stats = stats + add_digits(part_ref[p, base : base + 16, :])
        for r in range(2):
            start = base + 16 + r * rows
            first_ref[place_ref[1] ^ r, :, p * width : (p + 1) * width] = part_ref[
                p, start : start + rows, :
            ].astype(F32)
    stat_ref[...] = jnp.sqrt(stats[:8] / entries)
    held = out_ref.shape[0]
    features = parts * width
    total = 0.0
    for part in range(3):
        for p in range(parts):
            grad = part_ref[p, part * held : (part + 1) * held, :].astype(F32)
            lanes = slice(part * features + p * width, part * features + (p + 1) * width)
            out_ref[:, lanes] = grad
            total = total + jnp.sum(w_ref[:, lanes].astype(F32) * grad, -1, keepdims=True)
    gain_grad_ref[...] = total / gain_ref[...]


def tokens_back_kernel(place_ref, p0, p1, p2, p3, x_ref, gain_ref, dh_ref, out_ref):
    b = place_ref[1]
    rows = out_ref.shape[1]
    for r in range(2):
        here = slice(r * rows, (r + 1) * rows)
        normed_grad = (
            p0[here, :] + p1[here, :].astype(F32) + p2[here, :].astype(F32) + p3[here, :].astype(F32)
        )
        row = b ^ r
        values = x_ref[row].astype(F32)
        out_ref[row] = dh_ref[row] + norm_back(values, gain_ref[0:1, :], normed_grad)


def turn_tables(positions, width):
    quarter = HEAD_DIM // 2
    freqs = jnp.power(10000.0, -jnp.arange(quarter, dtype=F32) / quarter)
    freqs = jnp.tile(freqs, width // quarter)
    signs = jnp.where(jnp.arange(width) % HEAD_DIM < quarter, -1.0, 1.0)
    angles = positions.astype(F32)[..., None] * freqs
    return jnp.cos(angles), jnp.sin(angles) * signs


def grid_body(tokens, v_first, segments, grad_out, w_qkv, w_out, w_gate_up, w_down, gain_attn, gain_ffn):
    row_count, shard_len, features = tokens.shape[1:]
    a, b, c, f = [lax.axis_index(name) for name in GRID]
    na = lax.axis_size("a")
    nd = 8 * na
    width = features // (2 * na)
    held = features // nd
    hidden = w_down.shape[0]
    room = unit_room(hidden)
    padded = 2 * na * room
    wide = 2 * padded
    length = 4 * na * shard_len
    count = row_count * shard_len
    places = jnp.stack([a, b, c, f]).astype(jnp.int32)
    a_steps = range(1, na)

    def plane_hops(pieces, tag):
        return [hop(piece, tag, b=i, f=j) for piece, (i, j) in zip(pieces, FLIPS[1:])]

    def a_hops(value, tag):
        return [value] + [hop(value, tag, a=step) for step in a_steps]

    mine = tokens[0]
    turned, sent = call(
        prepare_kernel,
        "prepare",
        [like(count, features), like(2 * na, 3 * held + 16, width)],
        [places, mine, w_qkv, segments[0], jnp.stack([gain_attn, gain_ffn])],
    )

    token_parts = a_hops(turned, "tokens_a")
    sent = swap(sent, "qkv_ac", ("a", "c"))
    spread = call(spread_kernel, "spread", like(4, held, wide), [places, w_gate_up], [pltpu.VMEM((4, held, wide), BF16)])
    units = [spread[0]] + plane_hops([spread[k] for k in range(1, 4)], "units_bf")
    units = call(
        join_units_kernel, "join_units", like(6 * held, wide), [*units, w_down], scalars=0
    )
    sent = after(sent, *token_parts[1 : 1 + GATE], units)
    sent = jnp.broadcast_to(sent, (4,) + sent.shape)
    sent = swap(sent, "qkv_bf", ("b", "f"))
    units = lax.all_gather(after(units, sent), ("a", "c"), axis=0, tiled=False)

    group_tokens = jnp.stack(token_parts)
    other_tokens = hop(group_tokens, "tokens_c", c=1)
    qkv_weights, gains = call(
        assemble_kernel,
        "assemble",
        [like(features, 3 * width), like(8, features, dtype=F32)],
        [sent],
        scalars=0,
    )

    def pick(array, index, dim):
        return lax.dynamic_index_in_dim(array, index, dim, keepdims=False)

    digits = sent.reshape(2, 2, na, 2, 3 * held + 16, width)[..., 3 * held + 2 : 3 * held + 4, :]
    digits = pick(digits, f, 1).astype(jnp.int32)
    all_starts = (digits[..., 0, :] * 256 + digits[..., 1, :]).reshape(
        2, na, 2, row_count, shard_len
    )
    all_starts = jnp.moveaxis(all_starts, 0, 1)
    group_starts = pick(all_starts, b, 1)
    group_starts = jnp.where(b == 0, group_starts, group_starts[:, :, ::-1])
    order = jnp.arange(2 * na, dtype=jnp.int32).reshape(na, 2, 1, 1)
    offset = jnp.arange(shard_len, dtype=jnp.int32)
    block = (order // 2 * 2 + b) * 2 + order % 2
    positions = block * shard_len + offset - group_starts
    cosine, sine = turn_tables(positions.reshape(na, 2, count), width)
    keeps, sends, normed = [], [], []
    for flip, x in enumerate((group_tokens, other_tokens)):
        n_part, keep, send = project(places, flip, x, qkv_weights, gains, cosine, sine)
        normed.append(n_part)
        keeps.append(keep)
        sends.append(hop(send, "heads_b", b=1))

    first = call(
        by_heads_kernel,
        "by_heads",
        like(4 * na, shard_len, width),
        [after(v_first, sent)[0]],
        scalars=0,
    )
    first = swap(first, "first_abc", ("a", "b", "c")).reshape(length, width)

    row_starts = pick(all_starts, b, 3).reshape(length)
    heads, everything = call(
        attend_kernel,
        "attend",
        [like(length, width), like(length, 3 * width)],
        [places, *keeps, *sends, row_starts[:, None], first],
        flops=8 * length * length * width,
    )

    parts = jnp.stack(a_hops(after(w_out, normed[0]), "out_a"))
    parts = [parts] + plane_hops([parts] * 3, "out_bf")
    parts = jnp.stack(lax.optimization_barrier((*parts, heads))[:4])
    other_parts = hop(parts, "out_c", c=1)
    grads = after(grad_out, heads).reshape(count, features)
    plane = [grads] + plane_hops([grads] * 3, "grads_bf")

    heads = swap(heads.reshape(4 * na, shard_len, width), "heads_abc", ("a", "b", "c"))
    inputs = mine.reshape(count, features)
    attention, full_out, stream, normed_two, sums = call(
        out_kernel,
        "out_project",
        [
            like(count, features),
            like(features, features),
            like(count, features, dtype=F32),
            like(count, features),
            like(2, features, dtype=F32),
        ],
        [places, after(heads, *plane), parts, other_parts, inputs, gains],
        flops=2 * count * features * features,
    )
    group_two = [normed_two] + plane_hops([normed_two] * 3, "two_bf")

    act, units_grad, back0, back, full_down = call(
        feed_kernel,
        "feed",
        [
            like(4 * count, padded),
            like(4 * count, wide),
            like(count, features, dtype=F32),
            like(3, count, features),
            like(padded, features),
        ],
        [places, *group_two, *plane, units],
        scratch=[
            pltpu.VMEM((4 * count, features), BF16),
            pltpu.VMEM((4 * count, features), BF16),
            pltpu.VMEM((features, wide), BF16),
        ],
        flops=16 * count * features * padded * 3,
    )
    backs = plane_hops([back[k] for k in range(3)], "two_back_bf")
    units_part, ffn0, ffn = call(
        feed_grads_kernel,
        "feed_grads",
        [
            like(2 * na, 6 * held, wide),
            like(count, features, dtype=F32),
            like(3, count, features),
        ],
        [places, *group_two, *plane, act, units_grad, full_down],
        scratch=[
            pltpu.VMEM((4 * count, features), BF16),
            pltpu.VMEM((4 * count, features), BF16),
        ],
        flops=16 * count * features * padded * 2,
    )
    units_part = lax.psum_scatter(units_part, ("a", "c"), scatter_dimension=0, tiled=True)
    stream_grad, attn_grad, heads_grad = call(
        stream_back_kernel,
        "stream_back",
        [
            like(count, features, dtype=F32),
            like(count, features),
            like(4 * na, shard_len, width),
        ],
        [back0, *backs, stream, gains, grads, full_out],
        flops=2 * count * features * features,
        scalars=0,
    )
    heads_grad = swap(heads_grad, "heads_back_abc", ("a", "b", "c"))
    own, send = call(
        out_grads_kernel,
        "out_grads",
        [like(2 * na, 2, held, features, dtype=F32), like(2 * na, 2, held, features)],
        [places, attention, attn_grad],
        scratch=[pltpu.VMEM((features, features), F32)],
        flops=2 * count * features * features,
    )
    out_part = call(
        out_grads_core_kernel,
        "out_grads_core",
        like(4 * na, held, features),
        [own, hop(send, "out_back_c", c=1)],
        scalars=0,
    )
    out_sent = swap(after(out_part, heads_grad), "out_back_abf", ("a", "b", "f"))
    out, total = call(
        finish_out_kernel,
        "finish_out",
        [like(count, features), like(16, width, dtype=F32)],
        [stream, ffn0, *plane_hops([after(ffn, attn_grad)[k] for k in range(3)], "ffn_bf"), sums],
        scalars=0,
    )

    cosine, sine = turn_tables(
        after(jnp.arange(length, dtype=jnp.int32) - row_starts, everything), width
    )
    k0, k1, r0, r1 = call(
        attend_back_kernel,
        "attend_back",
        [like(na, shard_len, 3 * width)] * 4,
        [
            places,
            everything,
            row_starts[:, None],
            after(heads_grad.reshape(length, width), out_part, total),
            cosine,
            sine,
        ],
        scratch=[
            pltpu.VMEM((length, width), F32),
            pltpu.VMEM((length, width), F32),
            pltpu.VMEM((length, 3 * width), BF16),
        ],
        flops=20 * length * length * width,
    )
    r1, r0 = hop(r1, "back_b", b=1), hop(r0, "back_b", b=1)
    grad_out_weights = call(
        out_grads_sum_kernel,
        "out_grads_sum",
        like(held, features, dtype=F32),
        [out_sent],
        scalars=0,
    )

    units_part = units_part[0]
    rows = [units_part[k * held : (k + 1) * held] for k in range(4)]
    rows = [rows[0]] + plane_hops(rows[1:], "units_back_bf")
    grad_gate_up, ffn_gain_grad, grad_down = call(
        gather_units_kernel,
        "gather_units",
        [
            like(*w_gate_up.shape, dtype=F32),
            like(held, 1, dtype=F32),
            like(hidden, features, dtype=F32),
        ],
        [places, *rows, units_part[4 * held :], w_gate_up, gain_ffn.astype(F32)[:, None]],
        scratch=[pltpu.VMEM((4, held, wide), BF16)],
    )

    dn1 = call(
        unproject_other_kernel,
        "unproject_other",
        like(na, count, features),
        [k1, r1, qkv_weights],
        scratch=[pltpu.VMEM((na * count, 3 * width), BF16)],
        flops=2 * na * count * features * 3 * width,
        scalars=0,
    )
    dn1 = hop(dn1, "tokens_back_c", c=1)
    own, send = call(
        qkv_grads_kernel,
        "qkv_grads",
        [like(features * 3 // 4 + 16, width, dtype=F32), like(3, features * 3 // 4 + 16, width)],
        [places, k0, r0, normed[0], k1, r1, normed[1], total],
        scratch=[
            pltpu.VMEM((na * count, 3 * width), BF16),
            pltpu.VMEM((features, 3 * width), F32),
        ],
        flops=4 * na * count * features * 3 * width,
    )
    last = call(
        qkv_sum_kernel,
        "qkv_sum",
        like(2 * na, 3 * held + 16 + count, width),
        [places, after(own, out_sent), *plane_hops([send[k] for k in range(3)], "qkv_back_bf"), k0, r0, k1, r1],
    )
    last = swap(last, "qkv_back_ac", ("a", "c"))
    grad_qkv, attn_gain_grad, stats, grad_first = call(
        functools.partial(finish_kernel, float(count * features * nd)),
        "finish",
        [
            like(*w_qkv.shape, dtype=F32),
            like(held, 1, dtype=F32),
            like(8, width, dtype=F32),
            like(row_count, shard_len, features, dtype=F32),
        ],
        [places, last, w_qkv, gain_attn.astype(F32)[:, None]],
    )
    own, send = call(
        unproject_own_kernel,
        "unproject_own",
        [like(count, features, dtype=F32), like(na - 1, count, features)],
        [k0, r0, qkv_weights, dn1],
        scratch=[pltpu.VMEM((na * count, 3 * width), BF16)],
        flops=2 * na * count * features * 3 * width,
        scalars=0,
    )
    grad_tokens = call(
        tokens_back_kernel,
        "tokens_back",
        like(row_count, shard_len, features, dtype=F32),
        [
            places,
            after(own, grad_gate_up),
            *[hop(send[step - 1], "tokens_back_a", a=step) for step in a_steps],
            mine,
            gains,
            stream_grad.reshape(row_count, shard_len, features),
        ],
    )

    return (
        out.reshape(tokens.shape),
        grad_tokens[None],
        grad_first[None],
        grad_qkv,
        grad_out_weights,
        grad_gate_up,
        grad_down,
        attn_gain_grad[:, 0],
        ffn_gain_grad[:, 0],
        stats[0, :3],
    )


def fits(mesh):
    return mesh.shape["seq"] == 4 * NA and mesh.shape["fsdp"] == 2


def solution(mesh):
    if fits(mesh):
        grid = Mesh(mesh.devices.reshape(mesh.shape["seq"] // 4, 2, 2, 2), GRID)
        seq, every = ("a", "b", "c"), GRID
        body = grid_body
        fsdp = "f"
    else:
        grid, body = mesh, ring_body
        seq, every, fsdp = "seq", ("seq", "fsdp"), "fsdp"
    return jax.shard_map(
        body,
        mesh=grid,
        in_specs=(
            P(fsdp, None, seq, None),
            P(fsdp, None, seq, None),
            P(fsdp, None, seq),
            P(fsdp, None, seq, None),
            P(every, None),
            P(every, None),
            P(every, None),
            P(every, None),
            P(every),
            P(every),
        ),
        out_specs=(
            P(fsdp, None, seq, None),
            P(fsdp, None, seq, None),
            P(fsdp, None, seq, None),
            P(every, None),
            P(every, None),
            P(every, None),
            P(every, None),
            P(every),
            P(every),
            P(),
        ),
        check_vma=False,
    )
```

```python
import functools
import itertools
import math

import jax
import jax.numpy as jnp
from jax import lax
from jax.experimental import pallas as pl
from jax.experimental.pallas import tpu as pltpu
from jax.sharding import Mesh
from jax.sharding import PartitionSpec as P

HEADS = 16
HEAD_DIM = 64
FF = 2816
GRID = ("a", "b", "c", "f")
NA = 4


epsilon = 1e-06
masked_score = -1e30


def from_behind(value, axis, steps):
    count = lax.axis_size(axis)
    initial, last = (max(0, -steps), min(count, count - steps))
    return lax.ppermute(value, axis, [(source, source + steps) for source in range(initial, last)])


def shifted(shard, axis, by):
    size = lax.axis_size(axis)
    return lax.ppermute(shard, axis, [(i, (i + by) % size) for i in range(size)])


def rms_forward(values, gain):
    inverse_rms = lax.rsqrt(jnp.mean(values * values, -1, keepdims=True) + epsilon)
    return (values * inverse_rms * gain, inverse_rms)


def rms_backward(values, inverse_rms, gain, normed_grad):
    scaled = normed_grad * gain
    gain_grad = jnp.sum(normed_grad * values * inverse_rms, 0)
    input_grad = inverse_rms * scaled - values * (
        inverse_rms * inverse_rms * inverse_rms
    ) * jnp.mean(scaled * values, -1, keepdims=True)
    return (input_grad, gain_grad)


def rotation_tables(positions, head_dim):
    half_dim = head_dim // 2
    freqs = jnp.power(10000.0, -jnp.arange(half_dim, dtype=jnp.float32) / half_dim)
    angles = positions[..., None] * freqs
    return (jnp.cos(angles)[..., None, :], jnp.sin(angles)[..., None, :])


def rotate_forward(values, cosine, sine_part):
    half_dim = values.shape[-1] // 2
    first_half = values[..., :half_dim]
    second_half = values[..., half_dim:]
    return jnp.concatenate(
        [
            first_half * cosine - second_half * sine_part,
            second_half * cosine + first_half * sine_part,
        ],
        -1,
    )


def rotate_backward(values, cosine, sine_part):
    half_dim = values.shape[-1] // 2
    first_half = values[..., :half_dim]
    second_half = values[..., half_dim:]
    return jnp.concatenate(
        [
            first_half * cosine + second_half * sine_part,
            second_half * cosine - first_half * sine_part,
        ],
        -1,
    )


def over_blocks(visit, carried, members, block_rows):
    piece_rows = members[0].shape[1]
    splits = piece_rows // block_rows
    key_blocks = jnp.swapaxes(
        members[0].reshape(members[0].shape[0], splits, block_rows, members[0].shape[2]), 0, 1
    )
    value_blocks = jnp.swapaxes(
        members[1].reshape(members[1].shape[0], splits, block_rows, members[1].shape[2]), 0, 1
    )
    offsets = jnp.arange(splits, dtype=jnp.int32) * block_rows

    def advance(running, block_item):
        return (visit(running, block_item[0], block_item[1], block_item[2]), None)

    carried, unused = lax.scan(advance, carried, (key_blocks, value_blocks, offsets))
    return carried


def back_pair(
    query_heads,
    grad_heads,
    lse_part,
    delta_part,
    seg_part,
    index_part,
    key_heads,
    value_heads,
    key_start,
    score_scale,
):
    raw = (
        jnp.einsum("rqhd,rkhd->rhqk", query_heads, key_heads, preferred_element_type=jnp.float32)
        * score_scale
    )
    key_index = key_start + jnp.arange(key_heads.shape[1], dtype=jnp.int32)
    valid = (key_index[None, None, :] >= seg_part[:, :, None]) & (
        key_index[None, None, :] <= index_part[None, :, None]
    )
    valid = valid[:, None]
    scores = jnp.where(valid, raw, masked_score)
    weights = jnp.where(valid, jnp.exp(scores - lse_part[..., None]), 0.0)
    value_grad = jnp.einsum(
        "rhqk,rqhd->rkhd",
        weights.astype(jnp.bfloat16),
        grad_heads,
        preferred_element_type=jnp.float32,
    )
    weight_grad = jnp.einsum(
        "rqhd,rkhd->rhqk", grad_heads, value_heads, preferred_element_type=jnp.float32
    )
    score_grad = (weights * (weight_grad - delta_part[..., None])).astype(jnp.bfloat16)
    query_grad = (
        jnp.einsum("rhqk,rkhd->rqhd", score_grad, key_heads, preferred_element_type=jnp.float32)
        * score_scale
    )
    key_grad = (
        jnp.einsum("rhqk,rqhd->rkhd", score_grad, query_heads, preferred_element_type=jnp.float32)
        * score_scale
    )
    return (query_grad, key_grad, value_grad)


def ring_body(tokens, v_first, segments, grad_out, w_qkv, w_out, w_gate_up, w_down, gain_attn, gain_ffn):
    row_count = tokens.shape[1]
    shard_len = tokens.shape[2]
    features = tokens.shape[3]
    head_count = HEADS
    head_dim = HEAD_DIM
    score_scale = head_dim ** (-0.5)
    cycle_size = lax.axis_size("seq")
    device_index = lax.axis_index("seq")
    gathered = (
        lax.all_gather(w_qkv, ("seq", "fsdp"), axis=0, tiled=True),
        lax.all_gather(w_out, ("seq", "fsdp"), axis=0, tiled=True),
        lax.all_gather(w_gate_up, ("seq", "fsdp"), axis=0, tiled=True),
        lax.all_gather(w_down, ("seq", "fsdp"), axis=0, tiled=True),
        lax.all_gather(gain_attn, ("seq", "fsdp"), axis=0, tiled=True),
        lax.all_gather(gain_ffn, ("seq", "fsdp"), axis=0, tiled=True),
    )
    full_qkv, full_out, full_gate_up, full_down, full_gain_attn, full_gain_ffn = gathered
    attn_gain = full_gain_attn.astype(jnp.float32)
    ffn_gain = full_gain_ffn.astype(jnp.float32)
    inputs = tokens.reshape(-1, features).astype(jnp.float32)
    normed_one, inverse_one = rms_forward(inputs, attn_gain)
    normed_one_low = normed_one.astype(jnp.bfloat16)
    projected = jnp.dot(normed_one_low, full_qkv, preferred_element_type=jnp.float32)
    query_index = device_index * shard_len + jnp.arange(shard_len, dtype=jnp.int32)
    seg_rows = segments[0]
    positions = (query_index[None, :] - seg_rows).astype(jnp.float32)
    cosine, sine_part = rotation_tables(positions, head_dim)

    def split_heads(values):
        return values.reshape(row_count, -1, head_count, head_dim)

    queries = rotate_forward(split_heads(projected[:, :features]), cosine, sine_part).astype(
        jnp.bfloat16
    )
    keys_low = (
        rotate_forward(split_heads(projected[:, features : 2 * features]), cosine, sine_part)
        .astype(jnp.bfloat16)
        .reshape(row_count, shard_len, features)
    )
    mixed = (
        (
            0.5 * projected[:, 2 * features :]
            + 0.5 * v_first.reshape(-1, features).astype(jnp.float32)
        )
        .astype(jnp.bfloat16)
        .reshape(row_count, shard_len, features)
    )

    def scores_for(key_heads, key_start):
        raw = (
            jnp.einsum("rqhd,rkhd->rhqk", queries, key_heads, preferred_element_type=jnp.float32)
            * score_scale
        )
        key_index = key_start + jnp.arange(key_heads.shape[1], dtype=jnp.int32)
        valid = (key_index[None, None, :] >= seg_rows[:, :, None]) & (
            key_index[None, None, :] <= query_index[None, :, None]
        )
        valid = valid[:, None]
        return (jnp.where(valid, raw, masked_score), valid)

    def accumulate(carried, key_piece, value_piece, key_start):
        running_max, running_sum, weighted = carried
        key_heads = split_heads(key_piece)
        value_heads = split_heads(value_piece)
        scores, valid = scores_for(key_heads, key_start)
        new_max = jnp.maximum(running_max, jnp.max(scores, -1))
        weights = jnp.where(valid, jnp.exp(scores - new_max[..., None]), 0.0)
        factor = jnp.exp(running_max - new_max)
        running_sum = running_sum * factor + jnp.sum(weights, -1)
        weighted = weighted * jnp.transpose(factor, (0, 2, 1))[..., None] + jnp.einsum(
            "rhqk,rkhd->rqhd",
            weights.astype(jnp.bfloat16),
            value_heads,
            preferred_element_type=jnp.float32,
        )
        return (new_max, running_sum, weighted)

    def visit_forward(carried, key_piece, value_piece, key_start):
        return accumulate(carried, key_piece, value_piece, key_start)

    initial = (
        jnp.full((row_count, head_count, shard_len), masked_score, jnp.float32),
        jnp.zeros((row_count, head_count, shard_len), jnp.float32),
        jnp.zeros((row_count, shard_len, head_count, head_dim), jnp.float32),
    )
    running_max, running_sum, weighted = over_blocks(
        visit_forward,
        initial,
        (
            lax.all_gather(keys_low, "seq", axis=1, tiled=True),
            lax.all_gather(mixed, "seq", axis=1, tiled=True),
        ),
        shard_len,
    )
    attention = weighted / jnp.transpose(running_sum, (0, 2, 1))[..., None]
    log_total = running_max + jnp.log(running_sum)
    attn_low = attention.reshape(-1, features).astype(jnp.bfloat16)
    branch_attn = jnp.dot(attn_low, full_out, preferred_element_type=jnp.float32)
    stream = inputs + branch_attn
    normed_two, inverse_two = rms_forward(stream, ffn_gain)
    normed_two_low = normed_two.astype(jnp.bfloat16)
    gate_up = jnp.dot(normed_two_low, full_gate_up, preferred_element_type=jnp.float32)
    gate = gate_up[:, :FF]
    upward = gate_up[:, FF:]
    sigmoid_gate = jax.nn.sigmoid(gate)
    silu_gate = gate * sigmoid_gate
    hidden_low = (silu_gate * upward).astype(jnp.bfloat16)
    branch_ffn = jnp.dot(hidden_low, full_down, preferred_element_type=jnp.float32)
    output = stream + branch_ffn
    out_tokens = output.astype(jnp.bfloat16).reshape(tokens.shape)
    square_sums = jnp.stack(
        [
            jnp.sum(stream * stream),
            jnp.sum(branch_attn * branch_attn),
            jnp.sum(branch_ffn * branch_ffn),
        ]
    )
    square_totals = lax.psum(square_sums, ("seq", "fsdp"))
    stats = jnp.sqrt(square_totals / (stream.size * lax.axis_size(("seq", "fsdp"))))
    regathered = (
        lax.all_gather(w_qkv, ("seq", "fsdp"), axis=0, tiled=True),
        lax.all_gather(w_out, ("seq", "fsdp"), axis=0, tiled=True),
        lax.all_gather(w_gate_up, ("seq", "fsdp"), axis=0, tiled=True),
        lax.all_gather(w_down, ("seq", "fsdp"), axis=0, tiled=True),
        lax.all_gather(gain_attn, ("seq", "fsdp"), axis=0, tiled=True),
        lax.all_gather(gain_ffn, ("seq", "fsdp"), axis=0, tiled=True),
    )
    full_qkv, full_out, full_gate_up, full_down, full_gain_attn, full_gain_ffn = regathered
    attn_gain = full_gain_attn.astype(jnp.float32)
    ffn_gain = full_gain_ffn.astype(jnp.float32)
    ffn_grad_low = grad_out.reshape(-1, features)
    out_grad = ffn_grad_low.astype(jnp.float32)
    down_grad = jnp.dot(hidden_low.T, ffn_grad_low, preferred_element_type=jnp.float32)
    hidden_grad = jnp.dot(ffn_grad_low, full_down.T, preferred_element_type=jnp.float32)
    gate_grad = hidden_grad * upward * sigmoid_gate * (1.0 + gate * (1.0 - sigmoid_gate))
    upward_grad = hidden_grad * silu_gate
    gate_up_grad_low = jnp.concatenate([gate_grad, upward_grad], -1).astype(jnp.bfloat16)
    gate_up_weight_grad = jnp.dot(
        normed_two_low.T, gate_up_grad_low, preferred_element_type=jnp.float32
    )
    normed_two_grad = jnp.dot(gate_up_grad_low, full_gate_up.T, preferred_element_type=jnp.float32)
    stream_norm_grad, ffn_gain_grad = rms_backward(stream, inverse_two, ffn_gain, normed_two_grad)
    stream_grad = out_grad + stream_norm_grad
    attn_grad_low = stream_grad.astype(jnp.bfloat16)
    out_weight_grad = jnp.dot(attn_low.T, attn_grad_low, preferred_element_type=jnp.float32)
    attention_grad = (
        jnp.dot(attn_grad_low, full_out.T, preferred_element_type=jnp.float32)
        .astype(jnp.bfloat16)
        .reshape(row_count, shard_len, head_count, head_dim)
    )
    row_delta = jnp.einsum("rqhd,rqhd->rhq", attention_grad.astype(jnp.float32), attention)

    def back_visit(partials, query_part, key_heads, value_heads, key_start):
        query_heads, grad_heads, lse_part, delta_part, seg_part, index_part = query_part
        query_term, key_term, value_term = back_pair(
            query_heads,
            grad_heads,
            lse_part,
            delta_part,
            seg_part,
            index_part,
            key_heads,
            value_heads,
            key_start,
            score_scale,
        )
        return (
            partials[0] + query_term,
            partials[1] + key_term.reshape(partials[1].shape),
            partials[2] + value_term.reshape(partials[2].shape),
        )

    zero_rows = jnp.zeros((row_count, shard_len, features), jnp.float32)

    def back_turn(turn_index, running):
        key_piece, value_piece, key_grad, value_grad, query_grad = running
        source = (device_index - turn_index) % cycle_size
        query_grad, key_grad, value_grad = back_visit(
            (query_grad, key_grad, value_grad),
            (queries, attention_grad, log_total, row_delta, seg_rows, query_index),
            split_heads(key_piece),
            split_heads(value_piece),
            source * shard_len,
        )
        key_piece, value_piece = from_behind((key_piece, value_piece), "seq", 1)
        key_grad, value_grad = (
            shifted(key_grad.astype(jnp.bfloat16), "seq", 1).astype(key_grad.dtype),
            shifted(value_grad.astype(jnp.bfloat16), "seq", 1).astype(value_grad.dtype),
        )
        return (key_piece, value_piece, key_grad, value_grad, query_grad)

    start_state = (
        keys_low,
        mixed,
        zero_rows,
        zero_rows,
        jnp.zeros((row_count, shard_len, head_count, head_dim), jnp.float32),
    )
    final_state = lax.fori_loop(0, cycle_size, back_turn, start_state)
    key_grad_home = final_state[2]
    value_grad_home = final_state[3]
    query_grad_home = final_state[4]
    query_grad_rows = rotate_backward(query_grad_home, cosine, sine_part).reshape(-1, features)
    key_grad_rows = rotate_backward(split_heads(key_grad_home), cosine, sine_part).reshape(
        -1, features
    )
    mixed_grad = 0.5 * value_grad_home.reshape(-1, features)
    qkv_grad_low = jnp.concatenate([query_grad_rows, key_grad_rows, mixed_grad], -1).astype(
        jnp.bfloat16
    )
    qkv_weight_grad = jnp.dot(normed_one_low.T, qkv_grad_low, preferred_element_type=jnp.float32)
    normed_one_grad = jnp.dot(qkv_grad_low, full_qkv.T, preferred_element_type=jnp.float32)
    input_norm_grad, attn_gain_grad = rms_backward(inputs, inverse_one, attn_gain, normed_one_grad)
    input_grad = stream_grad + input_norm_grad
    owned = (
        lax.psum_scatter(qkv_weight_grad, ("seq", "fsdp"), scatter_dimension=0, tiled=True),
        lax.psum_scatter(out_weight_grad, ("seq", "fsdp"), scatter_dimension=0, tiled=True),
        lax.psum_scatter(gate_up_weight_grad, ("seq", "fsdp"), scatter_dimension=0, tiled=True),
        lax.psum_scatter(down_grad, ("seq", "fsdp"), scatter_dimension=0, tiled=True),
        lax.psum_scatter(attn_gain_grad, ("seq", "fsdp"), scatter_dimension=0, tiled=True),
        lax.psum_scatter(ffn_gain_grad, ("seq", "fsdp"), scatter_dimension=0, tiled=True),
    )
    return (
        out_tokens,
        input_grad.reshape(tokens.shape),
        mixed_grad.reshape(tokens.shape),
        owned[0],
        owned[1],
        owned[2],
        owned[3],
        owned[4],
        owned[5],
        stats,
    )


FLIPS = ((0, 0), (0, 1), (1, 0), (1, 1))
LAST = (((1,), (1,)), ((), ()))
FIRST = (((0,), (0,)), ((), ()))
BF16, F32 = jnp.bfloat16, jnp.float32


def hop(value, tag, **flips):
    with jax.named_scope(tag):
        return flip_over(value, **flips)


def swap(value, tag, axes):
    with jax.named_scope(tag):
        return lax.all_to_all(value, axes, 0, 0, tiled=True)


def flip_over(value, **flips):
    axes = tuple(name for name in GRID if flips.get(name, 0))
    sizes = [lax.axis_size(name) for name in axes]
    pairs = []
    for source in itertools.product(*[range(size) for size in sizes]):
        origin, target = 0, 0
        for name, size, place in zip(axes, sizes, source):
            origin = origin * size + place
            target = target * size + (place ^ flips[name])
        pairs.append((origin, target))
    return lax.ppermute(value, axes if len(axes) > 1 else axes[0], pairs)


def ordered(mine, other, place, dim):
    first = jnp.where(place == 0, mine, other)
    second = jnp.where(place == 0, other, mine)
    return jnp.stack([first, second], dim)


def after(value, *earlier):
    return lax.optimization_barrier((value,) + earlier)[0]


def call(kernel, name, out_shape, inputs, scratch=(), flops=0, scalars=1, limit=0):
    def whole(x):
        return pl.BlockSpec(x.shape, lambda _: (0,) * len(x.shape), pipeline_mode=pl.Buffered(1))

    smem = pl.BlockSpec(memory_space=pltpu.SMEM)
    shapes = jax.tree.leaves(out_shape)
    moved = sum(x.size * x.dtype.itemsize for x in list(inputs) + shapes)
    held = sum(math.prod(x.shape) * jnp.dtype(x.dtype).itemsize for x in scratch)
    return pl.pallas_call(
        kernel,
        grid=(1,),
        in_specs=[smem] * scalars + [whole(x) for x in inputs[scalars:]],
        out_specs=jax.tree.map(whole, out_shape),
        out_shape=out_shape,
        scratch_shapes=list(scratch),
        compiler_params=pltpu.CompilerParams(vmem_limit_bytes=limit or moved + held + 8 * 2**20),
        cost_estimate=pl.CostEstimate(flops=flops, bytes_accessed=moved, transcendentals=0),
        name=name,
    )(*inputs)


def like(*shape, dtype=BF16):
    return jax.ShapeDtypeStruct(shape, dtype)


def device_row(a, b, c, f):
    return ((a * 2 + b) * 2 + c) * 2 + f


def rows_at(index, count):
    return pl.ds(pl.multiple_of(index * count, count), count)


def half_swap(values):
    lanes = lax.broadcasted_iota(jnp.int32, values.shape, values.ndim - 1)
    quarter = HEAD_DIM // 2
    width = values.shape[-1]
    ahead = pltpu.roll(values, width - quarter, values.ndim - 1)
    behind = pltpu.roll(values, quarter, values.ndim - 1)
    return jnp.where(lanes % HEAD_DIM < quarter, ahead, behind)


def unit_room(hidden):
    return -(-hidden // 16) * 16


def prepare_kernel(place_ref, x_ref, w_ref, seg_ref, gain_ref, x_out_ref, out_ref):
    b, c, f = place_ref[1], place_ref[2], place_ref[3]
    rows = x_ref.shape[1]
    for r in range(2):
        x_out_ref[r * rows : (r + 1) * rows, :] = x_ref[b ^ r]
    held = w_ref.shape[0]
    parts, _, width = out_ref.shape
    features = parts * width
    lanes = lax.broadcasted_iota(jnp.int32, (1, width), 1)
    mine = lanes // held == c * 2 + f
    lines = []
    for k in range(2):
        gain = jnp.concatenate([gain_ref[k : k + 1, :].astype(F32)] * (width // held), 1)
        lines.append(jnp.where(mine, gain, 0.0))
    starts = jnp.concatenate([seg_ref[0:1, :], seg_ref[1:2, :]], 1)
    lines.append((starts >> 8).astype(F32))
    lines.append((starts & 255).astype(F32))
    row = lax.broadcasted_iota(jnp.int32, (16, width), 0)
    small = jnp.zeros((16, width), F32)
    for k, line in enumerate(lines):
        small = jnp.where(row == k, line, small)
    small = small.astype(BF16)
    for p in range(parts):
        for part in range(3):
            start = part * features + p * width
            out_ref[p, part * held : (part + 1) * held, :] = w_ref[:, start : start + width]
        out_ref[p, 3 * held :, :] = small


def by_heads_kernel(x_ref, out_ref):
    rows, width = out_ref.shape[1:]
    for p in range(x_ref.shape[2] // width):
        for r in range(2):
            out_ref[((p // 2) * 2 + r) * 2 + p % 2] = x_ref[r, :, p * width : (p + 1) * width]


def join_units_kernel(u0_ref, u1_ref, u2_ref, u3_ref, d_ref, out_ref):
    wide = out_ref.shape[1]
    hidden, features = d_ref.shape
    held = out_ref.shape[0] // 6
    fold = held * (wide - features) // features
    for k, ref in enumerate((u0_ref, u1_ref, u2_ref, u3_ref)):
        out_ref[k * held : (k + 1) * held, :features] = ref[:held, :]
        for part in range(features // (wide - features)):
            start = k * held + part * fold
            out_ref[start : start + fold, features:] = ref[
                held : held + fold, part * (wide - features) : (part + 1) * (wide - features)
            ]
    room = unit_room(hidden)
    lead = room * features // wide
    rest = room - lead
    base = 4 * held
    out_ref[base:, :features] = d_ref[:lead, :]
    gap = jnp.zeros((room - hidden, wide - features), BF16)
    for part in range(features // (wide - features)):
        lanes = slice(part * (wide - features), (part + 1) * (wide - features))
        here = slice(base + part * rest, base + (part + 1) * rest)
        out_ref[here, features:] = jnp.concatenate([d_ref[lead:, lanes], gap], 0)


def spread_digits(values):
    row = lax.broadcasted_iota(jnp.int32, values.shape, 0)
    first = values.astype(BF16).astype(F32)
    second = (values - first).astype(BF16).astype(F32)
    third = values - first - second
    picked = jnp.where(row == 0, first, jnp.where(row == 1, second, third))
    return jnp.where(row < 3, picked, 0.0).astype(BF16)


def add_digits(tile):
    return jnp.broadcast_to(jnp.sum(tile.astype(F32), 0, keepdims=True), tile.shape)


def spread_kernel(place_ref, w_ref, g_ref, o0_ref, o1_ref, o2_ref, o3_ref, all_ref):
    half = w_ref.shape[1] // 2
    wide = all_ref.shape[2] // 2
    na = NA
    hidden = half // (8 * na)
    room = unit_room(hidden)
    values = w_ref[...]
    gap = jnp.zeros((values.shape[0], room - hidden), values.dtype)
    for b, f in FLIPS:
        for side in range(2):
            parts = []
            for a, c in itertools.product(range(na), range(2)):
                start = side * half + hidden * device_row(a, b, c, f)
                parts += [values[:, start : start + hidden], gap]
            if wide > 2 * na * room:
                parts.append(jnp.zeros((values.shape[0], wide - 2 * na * room), values.dtype))
            all_ref[b * 2 + f, :, side * wide : (side + 1) * wide] = jnp.concatenate(parts, 1)
    held, features = w_ref.shape[0], g_ref.shape[1]
    rest = 2 * wide - features
    fold = held * rest // features
    for (i, j), ref in zip(FLIPS, (o0_ref, o1_ref, o2_ref, o3_ref)):
        block = all_ref[(place_ref[1] ^ i) * 2 + (place_ref[3] ^ j)]
        ref[:held, :] = block[:, :features]
        for part in range(features // rest):
            rows = block[part * fold : (part + 1) * fold, features:]
            ref[held : held + fold, part * rest : (part + 1) * rest] = rows
        ref[held + fold :, :] = g_ref[...]


def gather_units_kernel(
    place_ref, p0, p1, p2, p3, d_ref, w_ref, gain_ref,
    out_ref, gain_grad_ref, down_ref, outs_ref, part_ref,
):
    hidden, features = down_ref.shape
    room = unit_room(hidden)
    lead = d_ref.shape[0]
    rest = room - lead
    down_ref[:lead, :] = d_ref[:, :features].astype(F32)
    size = d_ref.shape[1] - features
    for part in range(features // size):
        block = d_ref[part * rest : (part + 1) * rest, features:].astype(F32)
        down_ref[lead:, part * size : (part + 1) * size] = block[: hidden - lead, :]
    b, f = place_ref[1], place_ref[3]
    columns = part_ref.shape[2]
    total = 0.0
    for (i, j), ref in zip(FLIPS, (p0, p1, p2, p3)):
        part_ref[(b ^ i) * 2 + (f ^ j)] = ref[:, :columns]
        total = total + ref[:, columns:].astype(F32)
    outs_ref[...] = total
    half = w_ref.shape[1] // 2
    wide = part_ref.shape[2] // 2
    na = NA
    hidden = half // (8 * na)
    room = unit_room(hidden)
    total = 0.0
    for side in range(2):
        parts = []
        for a, b, c, f in itertools.product(range(na), range(2), range(2), range(2)):
            start = side * wide + room * (a * 2 + c)
            parts.append(part_ref[b * 2 + f][:, start : start + hidden].astype(F32))
        grad = jnp.concatenate(parts, 1)
        out_ref[:, side * half : (side + 1) * half] = grad
        weights = w_ref[:, side * half : (side + 1) * half].astype(F32)
        total = total + jnp.sum(weights * grad, -1, keepdims=True)
    gain_grad_ref[...] = total / gain_ref[...]


def assemble_kernel(place_ref, p0_ref, p1_ref, p2_ref, p3_ref, w_ref, gain_ref):
    b, f = place_ref[1], place_ref[3]
    groups, _, width = p0_ref.shape
    held = w_ref.shape[0] // (4 * groups)
    pieces = (p0_ref, p1_ref, p2_ref, p3_ref)
    for (i, j), ref in zip(FLIPS, pieces):
        for a, c in itertools.product(range(groups // 2), range(2)):
            rows = rows_at(device_row(a, b ^ i, c, f ^ j), held)
            for part in range(3):
                w_ref[rows, part * width : (part + 1) * width] = ref[
                    a * 2 + c, part * held : (part + 1) * held, :
                ]
    for i in range(2):
        for a in range(groups // 2):
            total = 0.0
            for j, c in itertools.product(range(2), range(2)):
                total = total + pieces[i * 2 + j][a * 2 + c, 3 * held :, :].astype(F32)
            lanes = pl.ds(pl.multiple_of((a * 2 + (b ^ i)) * width, width), width)
            gain_ref[:, lanes] = total[:8]


def project_kernel(
    place_ref, x_ref, w_ref, gain_ref, cos_ref, sin_ref, n_ref, keep_ref, send_ref
):
    width = w_ref.shape[1] // 3
    rows = x_ref.shape[1] // 2
    values = x_ref[0].astype(F32)
    inverse = lax.rsqrt(jnp.mean(values * values, -1, keepdims=True) + epsilon)
    normed = (values * inverse * gain_ref[0:1, :]).astype(BF16)
    n_ref[0] = normed
    projected = jnp.dot(normed, w_ref[...], preferred_element_type=F32)
    cosine = cos_ref[0, 0]
    sine = sin_ref[0, 0]
    for part in range(2):
        block = projected[:, part * width : (part + 1) * width]
        turned = (block * cosine + half_swap(block) * sine).astype(BF16)
        keep_ref[0, :, part * width : (part + 1) * width] = turned[:rows]
        send_ref[0, :, part * width : (part + 1) * width] = turned[rows:]
    values = projected[:, 2 * width :].astype(BF16)
    keep_ref[0, :, 2 * width :] = values[:rows]
    send_ref[0, :, 2 * width :] = values[rows:]


def project(places, flip, x, weights, gains, cosine, sine):
    count, rows, features = x.shape
    wide = weights.shape[1]
    third = wide // 3

    def by_step(*block):
        return pl.BlockSpec((1,) + block, lambda step, place: (step, 0, 0))

    def table_map(step, place):
        return (step ^ place[0], place[2] ^ flip, 0, 0)

    def fixed(step, place):
        return (0, 0)

    table = pl.BlockSpec((1, 1, rows, third), table_map)
    return pl.pallas_call(
        project_kernel,
        grid_spec=pltpu.PrefetchScalarGridSpec(
            num_scalar_prefetch=1,
            grid=(count,),
            in_specs=[
                by_step(rows, features),
                pl.BlockSpec((features, wide), fixed),
                pl.BlockSpec((8, features), fixed),
                table,
                table,
            ],
            out_specs=[by_step(rows, features), by_step(rows // 2, wide), by_step(rows // 2, wide)],
        ),
        out_shape=[
            like(count, rows, features),
            like(count, rows // 2, wide),
            like(count, rows // 2, wide),
        ],
        compiler_params=pltpu.CompilerParams(vmem_limit_bytes=8 * 2**20),
        cost_estimate=pl.CostEstimate(
            flops=2 * count * rows * features * wide,
            bytes_accessed=count * rows * features * 4 + features * wide * 2,
            transcendentals=count * rows,
        ),
        name="project",
    )(places, x, weights, gains, cosine, sine)


def block_scores(head, query, keys, seg, start, scale):
    lanes = lax.broadcasted_iota(jnp.int32, query.shape, 1)
    masked = jnp.where(lanes // HEAD_DIM == head, query, jnp.zeros_like(query))
    raw = lax.dot_general(masked, keys, LAST, preferred_element_type=F32) * scale
    row = start + lax.broadcasted_iota(jnp.int32, raw.shape, 0)
    column = lax.broadcasted_iota(jnp.int32, raw.shape, 1)
    valid = (column >= seg) & (column <= row)
    scores = jnp.where(valid, raw, masked_score)
    top = jnp.max(scores, -1, keepdims=True)
    weights = jnp.exp(scores - top)
    total = jnp.sum(weights, -1, keepdims=True)
    return masked, weights * (1.0 / total)


def row_block(place_ref, step, b_flip, c_flip):
    a, b, c = place_ref[0] ^ step, place_ref[1] ^ b_flip, place_ref[2] ^ c_flip
    return (a * 2 + b) * 2 + c


def attend_kernel(
    place_ref, k0_ref, k1_ref, r0_ref, r1_ref, seg_ref, first_ref, o_ref, all_ref
):
    count, rows, wide = k0_ref.shape
    width = wide // 3
    length = all_ref.shape[0]
    for (b_flip, c_flip), ref in zip(FLIPS, (k0_ref, k1_ref, r0_ref, r1_ref)):
        for step in range(count):
            all_ref[rows_at(row_block(place_ref, step, b_flip, c_flip), rows), :] = ref[step]
    size = min(256, length)
    scale = HEAD_DIM ** (-0.5)
    for start in range(0, length, size):
        stop = start + size
        own = all_ref[start:stop, 2 * width :].astype(F32)
        first = first_ref[start:stop, :].astype(F32)
        all_ref[start:stop, 2 * width :] = (0.5 * own + 0.5 * first).astype(BF16)
        query = all_ref[start:stop, :width]
        keys = all_ref[:stop, width : 2 * width]
        values = all_ref[:stop, 2 * width :]
        seg = seg_ref[start:stop, :]

        def one(head):
            _, weights = block_scores(head, query, keys, seg, start, scale)
            return jnp.dot(weights.astype(BF16), values, preferred_element_type=F32)

        lanes = lax.broadcasted_iota(jnp.int32, (size, width), 1)
        result = one(0)
        for head in range(1, width // HEAD_DIM):
            result = jnp.where(lanes // HEAD_DIM == head, one(head), result)
        o_ref[start:stop, :] = result.astype(BF16)


def attend_back_kernel(
    place_ref, all_ref, seg_ref, do_ref, cos_ref, sin_ref, k_ref, r_ref, dk_ref, dv_ref, full_ref
):
    _, count, rows, wide = k_ref.shape
    width = wide // 3
    length = all_ref.shape[0]
    size = min(256, length)
    scale = HEAD_DIM ** (-0.5)
    dk_ref[...] = jnp.zeros_like(dk_ref)
    dv_ref[...] = jnp.zeros_like(dv_ref)
    for start in range(0, length, size):
        stop = start + size
        query = all_ref[start:stop, :width]
        keys = all_ref[:stop, width : 2 * width]
        values = all_ref[:stop, 2 * width :]
        seg = seg_ref[start:stop, :]
        out_grad = do_ref[start:stop, :]
        lanes = lax.broadcasted_iota(jnp.int32, (size, width), 1)

        def one(head):
            masked, weights = block_scores(head, query, keys, seg, start, scale)
            grad = jnp.where(lanes // HEAD_DIM == head, out_grad, jnp.zeros_like(out_grad))
            weight_grad = lax.dot_general(grad, values, LAST, preferred_element_type=F32)
            delta = jnp.sum(weights * weight_grad, -1, keepdims=True)
            score_grad = (weights * (weight_grad - delta)).astype(BF16)
            dv_ref[:stop, :] += lax.dot_general(
                weights.astype(BF16), grad, FIRST, preferred_element_type=F32
            )
            dk_ref[:stop, :] += lax.dot_general(
                score_grad, masked, FIRST, preferred_element_type=F32
            )
            return jnp.dot(score_grad, keys, preferred_element_type=F32)

        query_grad = one(0)
        for head in range(1, width // HEAD_DIM):
            query_grad = jnp.where(lanes // HEAD_DIM == head, one(head), query_grad)
        query_grad = query_grad * scale
        cosine = cos_ref[start:stop, :]
        sine = sin_ref[start:stop, :]
        full_ref[start:stop, :width] = (
            query_grad * cosine - half_swap(query_grad) * sine
        ).astype(BF16)
    for start in range(0, length, size):
        stop = start + size
        key_grad = dk_ref[start:stop, :] * scale
        cosine = cos_ref[start:stop, :]
        sine = sin_ref[start:stop, :]
        full_ref[start:stop, width : 2 * width] = (
            key_grad * cosine - half_swap(key_grad) * sine
        ).astype(BF16)
        full_ref[start:stop, 2 * width :] = (0.5 * dv_ref[start:stop, :]).astype(BF16)
    for b_flip, c_flip in FLIPS:
        ref = (k_ref, r_ref)[b_flip]
        for step in range(count):
            ref[c_flip, step] = full_ref[
                rows_at(row_block(place_ref, step, b_flip, c_flip), rows), :
            ]


def out_kernel(
    place_ref, heads_ref, own_ref, other_ref, x_ref, gain_ref,
    o_ref, w_ref, h_ref, n_ref, sum_ref,
):
    a, b, c, f = [place_ref[k] for k in range(4)]
    rows, width = heads_ref.shape[1:]
    na = NA
    held = other_ref.shape[2]
    for k, (i, j) in enumerate(FLIPS):
        for step in range(na):
            for c_flip, ref in enumerate((own_ref, other_ref)):
                row = device_row(a ^ step, b ^ i, c ^ c_flip, f ^ j)
                w_ref[rows_at(row, held), :] = ref[k, step]
    for p in range(o_ref.shape[1] // width):
        for r in range(2):
            o_ref[r * rows : (r + 1) * rows, p * width : (p + 1) * width] = heads_ref[
                ((p // 2) * 2 + r) * 2 + p % 2
            ]
    branch = jnp.dot(o_ref[...], w_ref[...], preferred_element_type=F32)
    stream = x_ref[...].astype(F32) + branch
    h_ref[...] = stream
    inverse = lax.rsqrt(jnp.mean(stream * stream, -1, keepdims=True) + epsilon)
    n_ref[...] = (stream * inverse * gain_ref[1:2, :]).astype(BF16)
    sum_ref[0:1, :] = jnp.sum(stream * stream, 0, keepdims=True)
    sum_ref[1:2, :] = jnp.sum(branch * branch, 0, keepdims=True)


def feed_kernel(
    place_ref, n0, n1, n2, n3, g0, g1, g2, g3, w_ref,
    act_ref, dgu_ref, b0_ref, b1_ref, b2_ref, b3_ref, down_ref, n_ref, g_ref, full_ref,
):
    a, b, c, f = [place_ref[k] for k in range(4)]
    na, wide = w_ref.shape[0] // 2, w_ref.shape[2]
    padded, features = down_ref.shape
    held = features // (8 * na)
    rows = n0.shape[0]
    room = padded // (2 * na)
    lead = room * features // wide
    rest = room - lead
    for s, (da, dc) in enumerate(itertools.product(range(na), range(2))):
        for k, (i, j) in enumerate(FLIPS):
            row = device_row(da, b ^ i, dc, f ^ j)
            full_ref[rows_at(row, held), :] = w_ref[s, k * held : (k + 1) * held, :]
        base = 4 * held
        start = s * room
        down_ref[start : start + lead, :] = w_ref[s, base:, :features]
        for part in range(features // (wide - features)):
            lanes = slice(part * (wide - features), (part + 1) * (wide - features))
            here = slice(base + part * rest, base + (part + 1) * rest)
            down_ref[start + lead : start + room, lanes] = w_ref[s, here, features:]
    for k, (n_part, g_part) in enumerate(zip((n0, n1, n2, n3), (g0, g1, g2, g3))):
        n_ref[k * rows : (k + 1) * rows, :] = n_part[...]
        g_ref[k * rows : (k + 1) * rows, :] = g_part[g_part.shape[0] - rows :, :]
    size = 256
    for start in range(0, padded, size):
        here = slice(start, start + size)
        there = slice(padded + start, padded + start + size)
        gate = jnp.dot(n_ref[...], full_ref[:, here], preferred_element_type=F32)
        upward = jnp.dot(n_ref[...], full_ref[:, there], preferred_element_type=F32)
        act_grad = lax.dot_general(g_ref[...], down_ref[here, :], LAST, preferred_element_type=F32)
        sigmoid_gate = jax.nn.sigmoid(gate)
        silu_gate = gate * sigmoid_gate
        act_ref[:, here] = (silu_gate * upward).astype(BF16)
        dgu_ref[:, here] = (
            act_grad * upward * sigmoid_gate * (1.0 + gate * (1.0 - sigmoid_gate))
        ).astype(BF16)
        dgu_ref[:, there] = (act_grad * silu_gate).astype(BF16)
    for k in range(4):
        back = lax.dot_general(
            dgu_ref[k * rows : (k + 1) * rows, :], full_ref[...], LAST, preferred_element_type=F32
        )
        ref = (b0_ref, b1_ref, b2_ref, b3_ref)[k]
        ref[...] = back.astype(ref.dtype)


def feed_grads_kernel(
    place_ref, n0, n1, n2, n3, g0, g1, g2, g3, act_ref, dgu_ref, down_ref,
    own_ref, send_ref, f0_ref, f1_ref, f2_ref, f3_ref, n_ref, g_ref, out_ref,
):
    b, c, f = place_ref[1], place_ref[2], place_ref[3]
    rows = n0.shape[0]
    for k, (n_part, g_part) in enumerate(zip((n0, n1, n2, n3), (g0, g1, g2, g3))):
        n_ref[k * rows : (k + 1) * rows, :] = n_part[...]
        g_ref[k * rows : (k + 1) * rows, :] = g_part[g_part.shape[0] - rows :, :]
    groups, _, wide = out_ref.shape
    padded, features = down_ref.shape
    held = features // (4 * groups)
    room = padded // groups
    size = 512
    for start in range(0, wide, size):
        here = slice(start, start + size)
        grad = lax.dot_general(
            n_ref[...], dgu_ref[:, here], FIRST, preferred_element_type=F32
        ).astype(BF16)
        for s, (da, dc) in enumerate(itertools.product(range(groups // 2), range(2))):
            for db, df in FLIPS:
                row = device_row(da, db, dc, df) * held
                k = (b ^ db) * 2 + (f ^ df)
                out_ref[s, rows_at(k, held), here] = grad[row : row + held, :]
    grad = lax.dot_general(act_ref[...], g_ref[...], FIRST, preferred_element_type=F32).astype(BF16)
    lead = room * features // wide
    rest = room - lead
    base = 4 * held
    for s in range(groups):
        block = grad[room * s : room * (s + 1), :]
        out_ref[s, base:, :features] = block[:lead, :]
        for part in range(features // (wide - features)):
            lanes = slice(part * (wide - features), (part + 1) * (wide - features))
            there = slice(base + part * rest, base + (part + 1) * rest)
            out_ref[s, there, features:] = block[lead:, lanes]
    for a in range(groups // 2):
        own_ref[a] = out_ref[a * 2 + c]
        send_ref[a] = out_ref[a * 2 + (1 - c)]
    for k in range(4):
        ffn = jnp.dot(
            act_ref[k * rows : (k + 1) * rows, :], down_ref[...], preferred_element_type=F32
        )
        ref = (f0_ref, f1_ref, f2_ref, f3_ref)[k]
        ref[...] = ffn.astype(ref.dtype)


def norm_back(values, gain, normed_grad):
    inverse = lax.rsqrt(jnp.mean(values * values, -1, keepdims=True) + epsilon)
    scaled = normed_grad * gain
    return inverse * scaled - values * (inverse * inverse * inverse) * jnp.mean(
        scaled * values, -1, keepdims=True
    )


def stream_back_kernel(
    place_ref, p0, p1, p2, p3, h_ref, gain_ref, g_ref, w_ref, o_ref, dh_ref, do_ref, own_ref, send_ref, out_ref
):
    normed_grad = p0[...] + p1[...].astype(F32) + p2[...].astype(F32) + p3[...].astype(F32)
    stream = h_ref[...]
    stream_grad = g_ref[...].astype(F32) + norm_back(stream, gain_ref[1:2, :], normed_grad)
    dh_ref[...] = stream_grad
    low = stream_grad.astype(BF16)
    heads = lax.dot_general(low, w_ref[...], LAST, preferred_element_type=F32).astype(BF16)
    rows, width = do_ref.shape[1:]
    for p in range(heads.shape[1] // width):
        for r in range(2):
            do_ref[((p // 2) * 2 + r) * 2 + p % 2] = heads[
                r * rows : (r + 1) * rows, p * width : (p + 1) * width
            ]
    total = lax.dot_general(o_ref[...], low, FIRST, preferred_element_type=F32).astype(BF16)
    b, f = place_ref[1], place_ref[3]
    groups = out_ref.shape[0]
    held = out_ref.shape[1] // 4
    for s, (da, dc) in enumerate(itertools.product(range(groups // 2), range(2))):
        for db, df in FLIPS:
            row = device_row(da, db, dc, df) * held
            k = (b ^ db) * 2 + (f ^ df)
            out_ref[s, rows_at(k, held), :] = total[row : row + held, :]
    c = place_ref[2]
    for a in range(groups // 2):
        own_ref[a] = out_ref[a * 2 + c]
        send_ref[a] = out_ref[a * 2 + (1 - c)]


def fill_pairs(d_ref, keep_ref, recv_ref, flip):
    _, count, rows, _ = keep_ref.shape
    for step in range(count):
        base = 2 * rows * step
        d_ref[base : base + rows, :] = keep_ref[flip, step]
        d_ref[base + rows : base + 2 * rows, :] = recv_ref[flip, step]


def unproject_other_kernel(keep_ref, recv_ref, w_ref, dn_ref, d_ref):
    fill_pairs(d_ref, keep_ref, recv_ref, 1)
    count, rows, _ = dn_ref.shape
    for step in range(count):
        back = lax.dot_general(
            d_ref[rows * step : rows * (step + 1), :], w_ref[...], LAST, preferred_element_type=F32
        )
        dn_ref[step] = back.astype(BF16)


def unproject_own_kernel(
    keep_ref, recv_ref, w_ref, other_ref, own_ref, s1_ref, s2_ref, s3_ref, d_ref
):
    fill_pairs(d_ref, keep_ref, recv_ref, 0)
    count, rows, _ = other_ref.shape
    for step in range(count):
        back = lax.dot_general(
            d_ref[rows * step : rows * (step + 1), :], w_ref[...], LAST, preferred_element_type=F32
        )
        back = back + other_ref[step].astype(F32)
        if step == 0:
            own_ref[...] = back
        else:
            (s1_ref, s2_ref, s3_ref)[step - 1][...] = back.astype(BF16)


def qkv_grads_kernel(
    place_ref, k_ref, r_ref, n0_ref, n1_ref, stat_ref,
    own_ref, send_ref, d_ref, total_ref,
):
    b, f = place_ref[1], place_ref[3]
    _, count, rows, wide = k_ref.shape
    width = wide // 3
    features = n0_ref.shape[2]
    for flip, n_ref in enumerate((n0_ref, n1_ref)):
        fill_pairs(d_ref, k_ref, r_ref, flip)
        tokens = n_ref[...].reshape(2 * rows * count, features)
        grad = lax.dot_general(tokens, d_ref[...], FIRST, preferred_element_type=F32)
        if flip == 0:
            total_ref[...] = grad
        else:
            total_ref[...] += grad
    held = features // (8 * count)
    block = 3 * held
    bottom = block * 2 * count
    own_ref[bottom:, :] = stat_ref[...]
    for k in range(3):
        send_ref[k, bottom:, :] = spread_digits(stat_ref[...])
    for k, (i, j) in enumerate(FLIPS):
        for s, (da, dc) in enumerate(itertools.product(range(count), range(2))):
            piece = total_ref[rows_at(device_row(da, b ^ i, dc, f ^ j), held), :]
            for part in range(3):
                lanes = piece[:, part * width : (part + 1) * width]
                there = slice(s * block + part * held, s * block + (part + 1) * held)
                if k == 0:
                    own_ref[there, :] = lanes
                else:
                    send_ref[k - 1, there, :] = lanes.astype(BF16)


def qkv_sum_kernel(
    place_ref, own_ref, r1_ref, r2_ref, r3_ref, kept_ref, moved_ref, out_ref
):
    a, c = place_ref[0], place_ref[2]
    parts, rows, width = out_ref.shape
    _, count, length, _ = kept_ref.shape
    block = rows - 16 - 2 * length
    bottom = parts * block
    received = (r1_ref, r2_ref, r3_ref)
    stats = own_ref[bottom:, :]
    for ref in received:
        stats = stats + add_digits(ref[bottom:, :])
    digits = spread_digits(stats)
    for p in range(parts):
        here = slice(p * block, (p + 1) * block)
        total = own_ref[here, :]
        for ref in received:
            total = total + ref[here, :].astype(F32)
        out_ref[p, :block, :] = total.astype(BF16)
        out_ref[p, block : block + 16, :] = digits
    base = block + 16
    for c_flip in range(2):
        for step in range(count):
            p = (a ^ step) * 2 + (c ^ c_flip)
            for r, ref in enumerate((kept_ref, moved_ref)):
                there = slice(base + r * length, base + (r + 1) * length)
                out_ref[p, there, :] = ref[c_flip, step, :, 2 * width :]


def join_grads_kernel(units_ref, outs_ref, out_ref):
    held = out_ref.shape[1]
    wide = units_ref.shape[1]
    for k in range(4):
        here = slice(k * held, (k + 1) * held)
        out_ref[k, :, :wide] = units_ref[here, :]
        out_ref[k, :, wide:] = outs_ref[here, :]


def finish_out_kernel(h_ref, ffn_ref, r1_ref, r2_ref, r3_ref, sum_ref, out_ref, total_ref):
    branch = ffn_ref[...]
    for ref in (r1_ref, r2_ref, r3_ref):
        branch = branch + ref[...].astype(F32)
    out_ref[...] = (h_ref[...] + branch).astype(BF16)
    squares = jnp.sum(branch * branch, 0, keepdims=True)
    lanes = lax.broadcasted_iota(jnp.int32, total_ref.shape, 1)
    totals = jnp.zeros(total_ref.shape, F32)
    for k in range(3):
        values = squares if k == 2 else sum_ref[k : k + 1, :]
        totals = jnp.where(lanes == k, jnp.sum(values, -1, keepdims=True), totals)
    total_ref[...] = totals


def finish_kernel(
    entries, place_ref, part_ref, w_ref, gain_ref, out_ref, gain_grad_ref, stat_ref, first_ref
):
    parts, _, width = part_ref.shape
    base = 3 * out_ref.shape[0]
    rows = first_ref.shape[1]
    stats = 0.0
    for p in range(parts):
        stats = stats + add_digits(part_ref[p, base : base + 16, :])
        for r in range(2):
            start = base + 16 + r * rows
            first_ref[place_ref[1] ^ r, :, p * width : (p + 1) * width] = part_ref[
                p, start : start + rows, :
            ].astype(F32)
    stat_ref[...] = jnp.sqrt(stats[:8] / entries)
    held = out_ref.shape[0]
    features = parts * width
    total = 0.0
    for part in range(3):
        for p in range(parts):
            grad = part_ref[p, part * held : (part + 1) * held, :].astype(F32)
            lanes = slice(part * features + p * width, part * features + (p + 1) * width)
            out_ref[:, lanes] = grad
            total = total + jnp.sum(w_ref[:, lanes].astype(F32) * grad, -1, keepdims=True)
    gain_grad_ref[...] = total / gain_ref[...]


def tokens_back_kernel(place_ref, p0, p1, p2, p3, x_ref, gain_ref, dh_ref, out_ref):
    b = place_ref[1]
    rows = out_ref.shape[1]
    for r in range(2):
        here = slice(r * rows, (r + 1) * rows)
        normed_grad = (
            p0[here, :] + p1[here, :].astype(F32) + p2[here, :].astype(F32) + p3[here, :].astype(F32)
        )
        row = b ^ r
        values = x_ref[row].astype(F32)
        out_ref[row] = dh_ref[row] + norm_back(values, gain_ref[0:1, :], normed_grad)


def turn_tables(positions, width):
    quarter = HEAD_DIM // 2
    freqs = jnp.power(10000.0, -jnp.arange(quarter, dtype=F32) / quarter)
    freqs = jnp.tile(freqs, width // quarter)
    signs = jnp.where(jnp.arange(width) % HEAD_DIM < quarter, -1.0, 1.0)
    angles = positions.astype(F32)[..., None] * freqs
    return jnp.cos(angles), jnp.sin(angles) * signs


def grid_body(tokens, v_first, segments, grad_out, w_qkv, w_out, w_gate_up, w_down, gain_attn, gain_ffn):
    row_count, shard_len, features = tokens.shape[1:]
    a, b, c, f = [lax.axis_index(name) for name in GRID]
    na = lax.axis_size("a")
    nd = 8 * na
    width = features // (2 * na)
    held = features // nd
    hidden = w_down.shape[0]
    room = unit_room(hidden)
    padded = 2 * na * room
    wide = 2 * padded
    length = 4 * na * shard_len
    count = row_count * shard_len
    places = jnp.stack([a, b, c, f]).astype(jnp.int32)
    a_steps = range(1, na)

    def plane_hops(pieces, tag):
        return [hop(piece, tag, b=i, f=j) for piece, (i, j) in zip(pieces, FLIPS[1:])]

    def a_hops(value, tag):
        return [value] + [hop(value, tag, a=step) for step in a_steps]

    mine = tokens[0]
    parts = a_hops(w_out, "out_a")
    turned, sent = call(
        prepare_kernel,
        "prepare",
        [like(count, features), like(2 * na, 3 * held + 16, width)],
        [places, after(mine, *parts), w_qkv, segments[0], jnp.stack([gain_attn, gain_ffn])],
        limit=60 * 2**20,
    )

    token_parts = a_hops(turned, "tokens_a")
    sent = swap(sent, "qkv_ac", ("a", "c"))
    grads = grad_out.reshape(count, features)
    tall = held * wide // features + count
    plane = call(
        spread_kernel,
        "spread",
        [like(tall, features)] * 4,
        [places, w_gate_up, grads],
        scratch=[pltpu.VMEM((4, held, wide), BF16)],
        limit=60 * 2**20,
    )
    plane = [plane[0]] + plane_hops(plane[1:], "units_bf")
    units = call(
        join_units_kernel, "join_units", like(6 * held, wide), [*plane, w_down], scalars=0
    )
    near = sent
    sent = after(sent, *token_parts[1:], units)
    first = call(
        by_heads_kernel, "by_heads", like(4 * na, shard_len, width), [v_first[0]], scalars=0
    )
    first = swap(after(first, sent), "first_abc", ("a", "b", "c")).reshape(length, width)
    pieces = [sent] + plane_hops([sent] * 3, "qkv_bf")
    sent = after(pieces[0], first, *pieces[1:])
    units = lax.all_gather(after(units, sent), ("a", "c"), axis=0, tiled=False)

    group_tokens = jnp.stack(token_parts)
    other_tokens = hop(group_tokens, "tokens_c", c=1)
    qkv_weights, gains = call(
        assemble_kernel,
        "assemble",
        [like(features, 3 * width), like(8, features, dtype=F32)],
        [places, sent, *pieces[1:]],
        limit=60 * 2**20,
    )

    def pick(array, index, dim):
        return lax.dynamic_index_in_dim(array, index, dim, keepdims=False)

    def starts_of(small):
        digits = small[..., 3 * held + 2 : 3 * held + 4, :].astype(jnp.int32)
        digits = digits[..., 0, :] * 256 + digits[..., 1, :]
        return digits.reshape(na, 2, row_count, shard_len)

    group_starts = starts_of(near)
    all_starts = ordered(group_starts, starts_of(pieces[2]), b, 1)
    group_starts = jnp.where(b == 0, group_starts, group_starts[:, :, ::-1])
    order = jnp.arange(2 * na, dtype=jnp.int32).reshape(na, 2, 1, 1)
    offset = jnp.arange(shard_len, dtype=jnp.int32)
    block = (order // 2 * 2 + b) * 2 + order % 2
    positions = block * shard_len + offset - group_starts
    cosine, sine = turn_tables(positions.reshape(na, 2, count), width)
    keeps, sends, normed = [], [], []
    for flip, x in enumerate((group_tokens, other_tokens)):
        n_part, keep, send = project(places, flip, x, qkv_weights, gains, cosine, sine)
        normed.append(n_part)
        keeps.append(keep)
        sends.append(hop(send, "heads_b", b=1))

    parts = jnp.stack(lax.optimization_barrier((*parts, *keeps))[:na])
    parts = [parts] + plane_hops([parts] * 3, "out_bf")
    row_starts = pick(all_starts, b, 3).reshape(length)
    heads, everything = call(
        attend_kernel,
        "attend",
        [like(length, width), like(length, 3 * width)],
        [places, *keeps, *sends, row_starts[:, None], first],
        flops=8 * length * length * width,
    )

    parts = jnp.stack(lax.optimization_barrier((*parts, heads))[:4])
    other_parts = hop(parts, "out_c", c=1)

    heads = swap(heads.reshape(4 * na, shard_len, width), "heads_abc", ("a", "b", "c"))
    inputs = mine.reshape(count, features)
    attention, full_out, stream, normed_two, sums = call(
        out_kernel,
        "out_project",
        [
            like(count, features),
            like(features, features),
            like(count, features, dtype=F32),
            like(count, features),
            like(2, features, dtype=F32),
        ],
        [places, heads, parts, other_parts, inputs, gains],
        flops=2 * count * features * features,
    )
    group_two = [normed_two] + plane_hops([normed_two] * 3, "two_bf")

    act, units_grad, back0, *backs, full_down = call(
        feed_kernel,
        "feed",
        [
            like(4 * count, padded),
            like(4 * count, wide),
            like(count, features, dtype=F32),
            *[like(count, features)] * 3,
            like(padded, features),
        ],
        [places, *group_two, *plane, units],
        scratch=[
            pltpu.VMEM((4 * count, features), BF16),
            pltpu.VMEM((4 * count, features), BF16),
            pltpu.VMEM((features, wide), BF16),
        ],
        flops=16 * count * features * padded * 3,
        limit=60 * 2**20,
    )
    backs = plane_hops(backs, "two_back_bf")
    units_own, units_send, ffn0, *ffn = call(
        feed_grads_kernel,
        "feed_grads",
        [like(na, 6 * held, wide)] * 2
        + [like(count, features, dtype=F32)]
        + [like(count, features)] * 3,
        [places, *group_two, *plane, act, units_grad, full_down],
        scratch=[
            pltpu.VMEM((4 * count, features), BF16),
            pltpu.VMEM((4 * count, features), BF16),
            pltpu.VMEM((2 * na, 6 * held, wide), BF16),
        ],
        flops=16 * count * features * padded * 2,
        limit=60 * 2**20,
    )

    def add_c(own, send, tag, *earlier):
        send = after(hop(send, tag, c=1), *earlier)
        return (own.astype(F32) + send.astype(F32)).astype(BF16)

    units_part = add_c(units_own, units_send, "units_back_c")
    back0 = after(back0, units_part)
    units_part = lax.psum_scatter(units_part, "a", scatter_dimension=0, tiled=True)
    units_rs = units_part

    stream_grad, heads_grad, out_own, out_send = call(
        stream_back_kernel,
        "stream_back",
        [
            like(count, features, dtype=F32),
            like(4 * na, shard_len, width),
            *[like(na, 4 * held, features)] * 2,
        ],
        [places, back0, *backs, stream, gains, grads, full_out, attention],
        scratch=[pltpu.VMEM((2 * na, 4 * held, features), BF16)],
        flops=4 * count * features * features,
        limit=60 * 2**20,
    )

    heads_grad = swap(heads_grad, "heads_back_abc", ("a", "b", "c"))
    ffn = plane_hops(ffn, "ffn_bf")

    cosine, sine = turn_tables(
        after(jnp.arange(length, dtype=jnp.int32) - row_starts, everything), width
    )
    kept, moved = call(
        attend_back_kernel,
        "attend_back",
        [like(2, na, shard_len, 3 * width)] * 2,
        [
            places,
            everything,
            row_starts[:, None],
            after(heads_grad.reshape(length, width), *ffn),
            cosine,
            sine,
        ],
        scratch=[
            pltpu.VMEM((length, width), F32),
            pltpu.VMEM((length, width), F32),
            pltpu.VMEM((length, 3 * width), BF16),
        ],
        flops=20 * length,
    )
    moved = hop(moved, "back_b", b=1)
    out_part = add_c(out_own, after(out_send, ffn[0]), "out_back_c")
    out_part = lax.psum_scatter(out_part, "a", scatter_dimension=0, tiled=True)
    out, total = call(
        finish_out_kernel,
        "finish_out",
        [like(count, features), like(16, width, dtype=F32)],
        [stream, after(ffn0, kept), *ffn, sums],
        scalars=0,
    )

    dn1 = call(
        unproject_other_kernel,
        "unproject_other",
        like(na, count, features),
        [kept, moved, qkv_weights],
        scratch=[pltpu.VMEM((na * count, 3 * width), BF16)],
        flops=2 * na * count * features * 3 * width,
        scalars=0,
    )
    dn1 = hop(dn1, "tokens_back_c", c=1)
    own, send = call(
        qkv_grads_kernel,
        "qkv_grads",
        [like(features * 3 // 4 + 16, width, dtype=F32), like(3, features * 3 // 4 + 16, width)],
        [places, kept, moved, normed[0], normed[1], total],
        scratch=[
            pltpu.VMEM((na * count, 3 * width), BF16),
            pltpu.VMEM((features, 3 * width), F32),
        ],
        flops=4 * na * count * features * 3 * width,
    )
    own_tokens, *send_tokens = call(
        unproject_own_kernel,
        "unproject_own",
        [like(count, features, dtype=F32)] + [like(count, features)] * 3,
        [kept, moved, qkv_weights, dn1],
        scratch=[pltpu.VMEM((na * count, 3 * width), BF16)],
        flops=2 * na * count * features * 3 * width,
        scalars=0,
    )
    token_grads = [hop(send_tokens[step - 1], "tokens_back_a", a=step) for step in a_steps]
    units_part = units_part[0]
    units_part = after(units_part, token_grads[0])
    rows = call(
        join_grads_kernel,
        "join_grads",
        like(4, held, wide + features),
        [units_part, out_part[0]],
        scalars=0,
    )
    rows = [rows[0]] + plane_hops([rows[k] for k in range(1, 4)], "units_back_bf")
    grad_gate_up, ffn_gain_grad, grad_down, grad_out_weights = call(
        gather_units_kernel,
        "gather_units",
        [
            like(*w_gate_up.shape, dtype=F32),
            like(held, 1, dtype=F32),
            like(hidden, features, dtype=F32),
            like(held, features, dtype=F32),
        ],
        [places, *rows, units_part[4 * held :], w_gate_up, gain_ffn.astype(F32)[:, None]],
        scratch=[pltpu.VMEM((4, held, wide), BF16)],
    )

    last = call(
        qkv_sum_kernel,
        "qkv_sum",
        like(2 * na, 3 * held + 16 + count, width),
        [places, after(own, own_tokens, units_rs), *plane_hops([send[k] for k in range(3)], "qkv_back_bf"), kept, moved],
    )
    last = swap(last, "qkv_back_ac", ("a", "c"))
    grad_qkv, attn_gain_grad, stats, grad_first = call(
        functools.partial(finish_kernel, float(count * features * nd)),
        "finish",
        [
            like(*w_qkv.shape, dtype=F32),
            like(held, 1, dtype=F32),
            like(8, width, dtype=F32),
            like(row_count, shard_len, features, dtype=F32),
        ],
        [places, last, w_qkv, gain_attn.astype(F32)[:, None]],
    )
    grad_tokens = call(
        tokens_back_kernel,
        "tokens_back",
        like(row_count, shard_len, features, dtype=F32),
        [
            places,
            after(own_tokens, grad_gate_up),
            *token_grads,
            mine,
            gains,
            stream_grad.reshape(row_count, shard_len, features),
        ],
    )

    return (
        out.reshape(tokens.shape),
        grad_tokens[None],
        grad_first[None],
        grad_qkv,
        grad_out_weights,
        grad_gate_up,
        grad_down,
        attn_gain_grad[:, 0],
        ffn_gain_grad[:, 0],
        stats[0, :3],
    )


def fits(mesh):
    return mesh.shape["seq"] == 4 * NA and mesh.shape["fsdp"] == 2


def solution(mesh):
    if fits(mesh):
        grid = Mesh(mesh.devices.reshape(mesh.shape["seq"] // 4, 2, 2, 2), GRID)
        seq, every = ("a", "b", "c"), GRID
        body = grid_body
        fsdp = "f"
    else:
        grid, body = mesh, ring_body
        seq, every, fsdp = "seq", ("seq", "fsdp"), "fsdp"
    return jax.shard_map(
        body,
        mesh=grid,
        in_specs=(
            P(fsdp, None, seq, None),
            P(fsdp, None, seq, None),
            P(fsdp, None, seq),
            P(fsdp, None, seq, None),
            P(every, None),
            P(every, None),
            P(every, None),
            P(every, None),
            P(every),
            P(every),
        ),
        out_specs=(
            P(fsdp, None, seq, None),
            P(fsdp, None, seq, None),
            P(fsdp, None, seq, None),
            P(every, None),
            P(every, None),
            P(every, None),
            P(every, None),
            P(every),
            P(every),
            P(),
        ),
        check_vma=False,
    )
```

```python
import functools
import itertools
import math

import jax
import jax.numpy as jnp
from jax import lax
from jax.experimental import pallas as pl
from jax.experimental.pallas import tpu as pltpu
from jax.sharding import Mesh
from jax.sharding import PartitionSpec as P

HEADS = 16
HEAD_DIM = 64
FF = 2816
GRID = ("a", "b", "c", "f")
NA = 4


epsilon = 1e-06
masked_score = -1e30


def from_behind(value, axis, steps):
    count = lax.axis_size(axis)
    initial, last = (max(0, -steps), min(count, count - steps))
    return lax.ppermute(value, axis, [(source, source + steps) for source in range(initial, last)])


def shifted(shard, axis, by):
    size = lax.axis_size(axis)
    return lax.ppermute(shard, axis, [(i, (i + by) % size) for i in range(size)])


def rms_forward(values, gain):
    inverse_rms = lax.rsqrt(jnp.mean(values * values, -1, keepdims=True) + epsilon)
    return (values * inverse_rms * gain, inverse_rms)


def rms_backward(values, inverse_rms, gain, normed_grad):
    scaled = normed_grad * gain
    gain_grad = jnp.sum(normed_grad * values * inverse_rms, 0)
    input_grad = inverse_rms * scaled - values * (
        inverse_rms * inverse_rms * inverse_rms
    ) * jnp.mean(scaled * values, -1, keepdims=True)
    return (input_grad, gain_grad)


def rotation_tables(positions, head_dim):
    half_dim = head_dim // 2
    freqs = jnp.power(10000.0, -jnp.arange(half_dim, dtype=jnp.float32) / half_dim)
    angles = positions[..., None] * freqs
    return (jnp.cos(angles)[..., None, :], jnp.sin(angles)[..., None, :])


def rotate_forward(values, cosine, sine_part):
    half_dim = values.shape[-1] // 2
    first_half = values[..., :half_dim]
    second_half = values[..., half_dim:]
    return jnp.concatenate(
        [
            first_half * cosine - second_half * sine_part,
            second_half * cosine + first_half * sine_part,
        ],
        -1,
    )


def rotate_backward(values, cosine, sine_part):
    half_dim = values.shape[-1] // 2
    first_half = values[..., :half_dim]
    second_half = values[..., half_dim:]
    return jnp.concatenate(
        [
            first_half * cosine + second_half * sine_part,
            second_half * cosine - first_half * sine_part,
        ],
        -1,
    )


def over_blocks(visit, carried, members, block_rows):
    piece_rows = members[0].shape[1]
    splits = piece_rows // block_rows
    key_blocks = jnp.swapaxes(
        members[0].reshape(members[0].shape[0], splits, block_rows, members[0].shape[2]), 0, 1
    )
    value_blocks = jnp.swapaxes(
        members[1].reshape(members[1].shape[0], splits, block_rows, members[1].shape[2]), 0, 1
    )
    offsets = jnp.arange(splits, dtype=jnp.int32) * block_rows

    def advance(running, block_item):
        return (visit(running, block_item[0], block_item[1], block_item[2]), None)

    carried, unused = lax.scan(advance, carried, (key_blocks, value_blocks, offsets))
    return carried


def back_pair(
    query_heads,
    grad_heads,
    lse_part,
    delta_part,
    seg_part,
    index_part,
    key_heads,
    value_heads,
    key_start,
    score_scale,
):
    raw = (
        jnp.einsum("rqhd,rkhd->rhqk", query_heads, key_heads, preferred_element_type=jnp.float32)
        * score_scale
    )
    key_index = key_start + jnp.arange(key_heads.shape[1], dtype=jnp.int32)
    valid = (key_index[None, None, :] >= seg_part[:, :, None]) & (
        key_index[None, None, :] <= index_part[None, :, None]
    )
    valid = valid[:, None]
    scores = jnp.where(valid, raw, masked_score)
    weights = jnp.where(valid, jnp.exp(scores - lse_part[..., None]), 0.0)
    value_grad = jnp.einsum(
        "rhqk,rqhd->rkhd",
        weights.astype(jnp.bfloat16),
        grad_heads,
        preferred_element_type=jnp.float32,
    )
    weight_grad = jnp.einsum(
        "rqhd,rkhd->rhqk", grad_heads, value_heads, preferred_element_type=jnp.float32
    )
    score_grad = (weights * (weight_grad - delta_part[..., None])).astype(jnp.bfloat16)
    query_grad = (
        jnp.einsum("rhqk,rkhd->rqhd", score_grad, key_heads, preferred_element_type=jnp.float32)
        * score_scale
    )
    key_grad = (
        jnp.einsum("rhqk,rqhd->rkhd", score_grad, query_heads, preferred_element_type=jnp.float32)
        * score_scale
    )
    return (query_grad, key_grad, value_grad)


def ring_body(tokens, v_first, segments, grad_out, w_qkv, w_out, w_gate_up, w_down, gain_attn, gain_ffn):
    row_count = tokens.shape[1]
    shard_len = tokens.shape[2]
    features = tokens.shape[3]
    head_count = HEADS
    head_dim = HEAD_DIM
    score_scale = head_dim ** (-0.5)
    cycle_size = lax.axis_size("seq")
    device_index = lax.axis_index("seq")
    gathered = (
        lax.all_gather(w_qkv, ("seq", "fsdp"), axis=0, tiled=True),
        lax.all_gather(w_out, ("seq", "fsdp"), axis=0, tiled=True),
        lax.all_gather(w_gate_up, ("seq", "fsdp"), axis=0, tiled=True),
        lax.all_gather(w_down, ("seq", "fsdp"), axis=0, tiled=True),
        lax.all_gather(gain_attn, ("seq", "fsdp"), axis=0, tiled=True),
        lax.all_gather(gain_ffn, ("seq", "fsdp"), axis=0, tiled=True),
    )
    full_qkv, full_out, full_gate_up, full_down, full_gain_attn, full_gain_ffn = gathered
    attn_gain = full_gain_attn.astype(jnp.float32)
    ffn_gain = full_gain_ffn.astype(jnp.float32)
    inputs = tokens.reshape(-1, features).astype(jnp.float32)
    normed_one, inverse_one = rms_forward(inputs, attn_gain)
    normed_one_low = normed_one.astype(jnp.bfloat16)
    projected = jnp.dot(normed_one_low, full_qkv, preferred_element_type=jnp.float32)
    query_index = device_index * shard_len + jnp.arange(shard_len, dtype=jnp.int32)
    seg_rows = segments[0]
    positions = (query_index[None, :] - seg_rows).astype(jnp.float32)
    cosine, sine_part = rotation_tables(positions, head_dim)

    def split_heads(values):
        return values.reshape(row_count, -1, head_count, head_dim)

    queries = rotate_forward(split_heads(projected[:, :features]), cosine, sine_part).astype(
        jnp.bfloat16
    )
    keys_low = (
        rotate_forward(split_heads(projected[:, features : 2 * features]), cosine, sine_part)
        .astype(jnp.bfloat16)
        .reshape(row_count, shard_len, features)
    )
    mixed = (
        (
            0.5 * projected[:, 2 * features :]
            + 0.5 * v_first.reshape(-1, features).astype(jnp.float32)
        )
        .astype(jnp.bfloat16)
        .reshape(row_count, shard_len, features)
    )

    def scores_for(key_heads, key_start):
        raw = (
            jnp.einsum("rqhd,rkhd->rhqk", queries, key_heads, preferred_element_type=jnp.float32)
            * score_scale
        )
        key_index = key_start + jnp.arange(key_heads.shape[1], dtype=jnp.int32)
        valid = (key_index[None, None, :] >= seg_rows[:, :, None]) & (
            key_index[None, None, :] <= query_index[None, :, None]
        )
        valid = valid[:, None]
        return (jnp.where(valid, raw, masked_score), valid)

    def accumulate(carried, key_piece, value_piece, key_start):
        running_max, running_sum, weighted = carried
        key_heads = split_heads(key_piece)
        value_heads = split_heads(value_piece)
        scores, valid = scores_for(key_heads, key_start)
        new_max = jnp.maximum(running_max, jnp.max(scores, -1))
        weights = jnp.where(valid, jnp.exp(scores - new_max[..., None]), 0.0)
        factor = jnp.exp(running_max - new_max)
        running_sum = running_sum * factor + jnp.sum(weights, -1)
        weighted = weighted * jnp.transpose(factor, (0, 2, 1))[..., None] + jnp.einsum(
            "rhqk,rkhd->rqhd",
            weights.astype(jnp.bfloat16),
            value_heads,
            preferred_element_type=jnp.float32,
        )
        return (new_max, running_sum, weighted)

    def visit_forward(carried, key_piece, value_piece, key_start):
        return accumulate(carried, key_piece, value_piece, key_start)

    initial = (
        jnp.full((row_count, head_count, shard_len), masked_score, jnp.float32),
        jnp.zeros((row_count, head_count, shard_len), jnp.float32),
        jnp.zeros((row_count, shard_len, head_count, head_dim), jnp.float32),
    )
    running_max, running_sum, weighted = over_blocks(
        visit_forward,
        initial,
        (
            lax.all_gather(keys_low, "seq", axis=1, tiled=True),
            lax.all_gather(mixed, "seq", axis=1, tiled=True),
        ),
        shard_len,
    )
    attention = weighted / jnp.transpose(running_sum, (0, 2, 1))[..., None]
    log_total = running_max + jnp.log(running_sum)
    attn_low = attention.reshape(-1, features).astype(jnp.bfloat16)
    branch_attn = jnp.dot(attn_low, full_out, preferred_element_type=jnp.float32)
    stream = inputs + branch_attn
    normed_two, inverse_two = rms_forward(stream, ffn_gain)
    normed_two_low = normed_two.astype(jnp.bfloat16)
    gate_up = jnp.dot(normed_two_low, full_gate_up, preferred_element_type=jnp.float32)
    gate = gate_up[:, :FF]
    upward = gate_up[:, FF:]
    sigmoid_gate = jax.nn.sigmoid(gate)
    silu_gate = gate * sigmoid_gate
    hidden_low = (silu_gate * upward).astype(jnp.bfloat16)
    branch_ffn = jnp.dot(hidden_low, full_down, preferred_element_type=jnp.float32)
    output = stream + branch_ffn
    out_tokens = output.astype(jnp.bfloat16).reshape(tokens.shape)
    square_sums = jnp.stack(
        [
            jnp.sum(stream * stream),
            jnp.sum(branch_attn * branch_attn),
            jnp.sum(branch_ffn * branch_ffn),
        ]
    )
    square_totals = lax.psum(square_sums, ("seq", "fsdp"))
    stats = jnp.sqrt(square_totals / (stream.size * lax.axis_size(("seq", "fsdp"))))
    regathered = (
        lax.all_gather(w_qkv, ("seq", "fsdp"), axis=0, tiled=True),
        lax.all_gather(w_out, ("seq", "fsdp"), axis=0, tiled=True),
        lax.all_gather(w_gate_up, ("seq", "fsdp"), axis=0, tiled=True),
        lax.all_gather(w_down, ("seq", "fsdp"), axis=0, tiled=True),
        lax.all_gather(gain_attn, ("seq", "fsdp"), axis=0, tiled=True),
        lax.all_gather(gain_ffn, ("seq", "fsdp"), axis=0, tiled=True),
    )
    full_qkv, full_out, full_gate_up, full_down, full_gain_attn, full_gain_ffn = regathered
    attn_gain = full_gain_attn.astype(jnp.float32)
    ffn_gain = full_gain_ffn.astype(jnp.float32)
    ffn_grad_low = grad_out.reshape(-1, features)
    out_grad = ffn_grad_low.astype(jnp.float32)
    down_grad = jnp.dot(hidden_low.T, ffn_grad_low, preferred_element_type=jnp.float32)
    hidden_grad = jnp.dot(ffn_grad_low, full_down.T, preferred_element_type=jnp.float32)
    gate_grad = hidden_grad * upward * sigmoid_gate * (1.0 + gate * (1.0 - sigmoid_gate))
    upward_grad = hidden_grad * silu_gate
    gate_up_grad_low = jnp.concatenate([gate_grad, upward_grad], -1).astype(jnp.bfloat16)
    gate_up_weight_grad = jnp.dot(
        normed_two_low.T, gate_up_grad_low, preferred_element_type=jnp.float32
    )
    normed_two_grad = jnp.dot(gate_up_grad_low, full_gate_up.T, preferred_element_type=jnp.float32)
    stream_norm_grad, ffn_gain_grad = rms_backward(stream, inverse_two, ffn_gain, normed_two_grad)
    stream_grad = out_grad + stream_norm_grad
    attn_grad_low = stream_grad.astype(jnp.bfloat16)
    out_weight_grad = jnp.dot(attn_low.T, attn_grad_low, preferred_element_type=jnp.float32)
    attention_grad = (
        jnp.dot(attn_grad_low, full_out.T, preferred_element_type=jnp.float32)
        .astype(jnp.bfloat16)
        .reshape(row_count, shard_len, head_count, head_dim)
    )
    row_delta = jnp.einsum("rqhd,rqhd->rhq", attention_grad.astype(jnp.float32), attention)

    def back_visit(partials, query_part, key_heads, value_heads, key_start):
        query_heads, grad_heads, lse_part, delta_part, seg_part, index_part = query_part
        query_term, key_term, value_term = back_pair(
            query_heads,
            grad_heads,
            lse_part,
            delta_part,
            seg_part,
            index_part,
            key_heads,
            value_heads,
            key_start,
            score_scale,
        )
        return (
            partials[0] + query_term,
            partials[1] + key_term.reshape(partials[1].shape),
            partials[2] + value_term.reshape(partials[2].shape),
        )

    zero_rows = jnp.zeros((row_count, shard_len, features), jnp.float32)

    def back_turn(turn_index, running):
        key_piece, value_piece, key_grad, value_grad, query_grad = running
        source = (device_index - turn_index) % cycle_size
        query_grad, key_grad, value_grad = back_visit(
            (query_grad, key_grad, value_grad),
            (queries, attention_grad, log_total, row_delta, seg_rows, query_index),
            split_heads(key_piece),
            split_heads(value_piece),
            source * shard_len,
        )
        key_piece, value_piece = from_behind((key_piece, value_piece), "seq", 1)
        key_grad, value_grad = (
            shifted(key_grad.astype(jnp.bfloat16), "seq", 1).astype(key_grad.dtype),
            shifted(value_grad.astype(jnp.bfloat16), "seq", 1).astype(value_grad.dtype),
        )
        return (key_piece, value_piece, key_grad, value_grad, query_grad)

    start_state = (
        keys_low,
        mixed,
        zero_rows,
        zero_rows,
        jnp.zeros((row_count, shard_len, head_count, head_dim), jnp.float32),
    )
    final_state = lax.fori_loop(0, cycle_size, back_turn, start_state)
    key_grad_home = final_state[2]
    value_grad_home = final_state[3]
    query_grad_home = final_state[4]
    query_grad_rows = rotate_backward(query_grad_home, cosine, sine_part).reshape(-1, features)
    key_grad_rows = rotate_backward(split_heads(key_grad_home), cosine, sine_part).reshape(
        -1, features
    )
    mixed_grad = 0.5 * value_grad_home.reshape(-1, features)
    qkv_grad_low = jnp.concatenate([query_grad_rows, key_grad_rows, mixed_grad], -1).astype(
        jnp.bfloat16
    )
    qkv_weight_grad = jnp.dot(normed_one_low.T, qkv_grad_low, preferred_element_type=jnp.float32)
    normed_one_grad = jnp.dot(qkv_grad_low, full_qkv.T, preferred_element_type=jnp.float32)
    input_norm_grad, attn_gain_grad = rms_backward(inputs, inverse_one, attn_gain, normed_one_grad)
    input_grad = stream_grad + input_norm_grad
    owned = (
        lax.psum_scatter(qkv_weight_grad, ("seq", "fsdp"), scatter_dimension=0, tiled=True),
        lax.psum_scatter(out_weight_grad, ("seq", "fsdp"), scatter_dimension=0, tiled=True),
        lax.psum_scatter(gate_up_weight_grad, ("seq", "fsdp"), scatter_dimension=0, tiled=True),
        lax.psum_scatter(down_grad, ("seq", "fsdp"), scatter_dimension=0, tiled=True),
        lax.psum_scatter(attn_gain_grad, ("seq", "fsdp"), scatter_dimension=0, tiled=True),
        lax.psum_scatter(ffn_gain_grad, ("seq", "fsdp"), scatter_dimension=0, tiled=True),
    )
    return (
        out_tokens,
        input_grad.reshape(tokens.shape),
        mixed_grad.reshape(tokens.shape),
        owned[0],
        owned[1],
        owned[2],
        owned[3],
        owned[4],
        owned[5],
        stats,
    )


FLIPS = ((0, 0), (0, 1), (1, 0), (1, 1))
LAST = (((1,), (1,)), ((), ()))
FIRST = (((0,), (0,)), ((), ()))
BF16, F32 = jnp.bfloat16, jnp.float32


def hop(value, tag, **flips):
    with jax.named_scope(tag):
        return flip_over(value, **flips)


def swap(value, tag, axes):
    with jax.named_scope(tag):
        return lax.all_to_all(value, axes, 0, 0, tiled=True)


def flip_over(value, **flips):
    axes = tuple(name for name in GRID if flips.get(name, 0))
    sizes = [lax.axis_size(name) for name in axes]
    pairs = []
    for source in itertools.product(*[range(size) for size in sizes]):
        origin, target = 0, 0
        for name, size, place in zip(axes, sizes, source):
            origin = origin * size + place
            target = target * size + (place ^ flips[name])
        pairs.append((origin, target))
    return lax.ppermute(value, axes if len(axes) > 1 else axes[0], pairs)


def ordered(mine, other, place, dim):
    first = jnp.where(place == 0, mine, other)
    second = jnp.where(place == 0, other, mine)
    return jnp.stack([first, second], dim)


def after(value, *earlier):
    return lax.optimization_barrier((value,) + earlier)[0]


def call(kernel, name, out_shape, inputs, scratch=(), flops=0, scalars=1, limit=0):
    def whole(x):
        return pl.BlockSpec(x.shape, lambda _: (0,) * len(x.shape), pipeline_mode=pl.Buffered(1))

    smem = pl.BlockSpec(memory_space=pltpu.SMEM)
    shapes = jax.tree.leaves(out_shape)
    moved = sum(x.size * x.dtype.itemsize for x in list(inputs) + shapes)
    held = sum(math.prod(x.shape) * jnp.dtype(x.dtype).itemsize for x in scratch)
    return pl.pallas_call(
        kernel,
        grid=(1,),
        in_specs=[smem] * scalars + [whole(x) for x in inputs[scalars:]],
        out_specs=jax.tree.map(whole, out_shape),
        out_shape=out_shape,
        scratch_shapes=list(scratch),
        compiler_params=pltpu.CompilerParams(vmem_limit_bytes=limit or moved + held + 8 * 2**20),
        cost_estimate=pl.CostEstimate(flops=flops, bytes_accessed=moved, transcendentals=0),
        name=name,
    )(*inputs)


def like(*shape, dtype=BF16):
    return jax.ShapeDtypeStruct(shape, dtype)


def device_row(a, b, c, f):
    return ((a * 2 + b) * 2 + c) * 2 + f


def rows_at(index, count):
    return pl.ds(pl.multiple_of(index * count, count), count)


def half_swap(values):
    lanes = lax.broadcasted_iota(jnp.int32, values.shape, values.ndim - 1)
    quarter = HEAD_DIM // 2
    width = values.shape[-1]
    ahead = pltpu.roll(values, width - quarter, values.ndim - 1)
    behind = pltpu.roll(values, quarter, values.ndim - 1)
    return jnp.where(lanes % HEAD_DIM < quarter, ahead, behind)


def unit_room(hidden):
    return -(-hidden // 16) * 16


def prepare_kernel(place_ref, x_ref, w_ref, seg_ref, g0_ref, g1_ref, x_out_ref, out_ref):
    b, c, f = place_ref[1], place_ref[2], place_ref[3]
    rows = x_ref.shape[1]
    for r in range(2):
        x_out_ref[r * rows : (r + 1) * rows, :] = x_ref[b ^ r]
    held = w_ref.shape[0]
    parts, _, width = out_ref.shape
    features = parts * width
    lanes = lax.broadcasted_iota(jnp.int32, (1, width), 1)
    mine = lanes // held == c * 2 + f
    lines = []
    for ref in (g0_ref, g1_ref):
        gain = jnp.concatenate([ref[...].astype(F32)] * (width // held), 1)
        lines.append(jnp.where(mine, gain, 0.0))
    starts = jnp.concatenate([seg_ref[0:1, :], seg_ref[1:2, :]], 1)
    lines.append((starts >> 8).astype(F32))
    lines.append((starts & 255).astype(F32))
    row = lax.broadcasted_iota(jnp.int32, (16, width), 0)
    small = jnp.zeros((16, width), F32)
    for k, line in enumerate(lines):
        small = jnp.where(row == k, line, small)
    small = small.astype(BF16)
    for p in range(parts):
        for part in range(3):
            start = part * features + p * width
            out_ref[p, part * held : (part + 1) * held, :] = w_ref[:, start : start + width]
        out_ref[p, 3 * held :, :] = small


def by_heads_kernel(x_ref, out_ref):
    rows, width = out_ref.shape[1:]
    for p in range(x_ref.shape[2] // width):
        for r in range(2):
            out_ref[((p // 2) * 2 + r) * 2 + p % 2] = x_ref[r, :, p * width : (p + 1) * width]


def join_units_kernel(u0_ref, u1_ref, u2_ref, u3_ref, d_ref, out_ref):
    wide = out_ref.shape[1]
    hidden, features = d_ref.shape
    held = out_ref.shape[0] // 6
    fold = held * (wide - features) // features
    for k, ref in enumerate((u0_ref, u1_ref, u2_ref, u3_ref)):
        out_ref[k * held : (k + 1) * held, :features] = ref[:held, :]
        for part in range(features // (wide - features)):
            start = k * held + part * fold
            out_ref[start : start + fold, features:] = ref[
                held : held + fold, part * (wide - features) : (part + 1) * (wide - features)
            ]
    room = unit_room(hidden)
    lead = room * features // wide
    rest = room - lead
    base = 4 * held
    out_ref[base:, :features] = d_ref[:lead, :]
    gap = jnp.zeros((room - hidden, wide - features), BF16)
    for part in range(features // (wide - features)):
        lanes = slice(part * (wide - features), (part + 1) * (wide - features))
        here = slice(base + part * rest, base + (part + 1) * rest)
        out_ref[here, features:] = jnp.concatenate([d_ref[lead:, lanes], gap], 0)


def spread_digits(values):
    row = lax.broadcasted_iota(jnp.int32, values.shape, 0)
    first = values.astype(BF16).astype(F32)
    second = (values - first).astype(BF16).astype(F32)
    third = values - first - second
    picked = jnp.where(row == 0, first, jnp.where(row == 1, second, third))
    return jnp.where(row < 3, picked, 0.0).astype(BF16)


def add_digits(tile):
    return jnp.broadcast_to(jnp.sum(tile.astype(F32), 0, keepdims=True), tile.shape)


def spread_kernel(place_ref, w_ref, g_ref, o0_ref, o1_ref, o2_ref, o3_ref, all_ref):
    half = w_ref.shape[1] // 2
    wide = all_ref.shape[2] // 2
    na = NA
    hidden = half // (8 * na)
    room = unit_room(hidden)
    values = w_ref[...]
    gap = jnp.zeros((values.shape[0], room - hidden), values.dtype)
    for b, f in FLIPS:
        for side in range(2):
            parts = []
            for a, c in itertools.product(range(na), range(2)):
                start = side * half + hidden * device_row(a, b, c, f)
                parts += [values[:, start : start + hidden], gap]
            if wide > 2 * na * room:
                parts.append(jnp.zeros((values.shape[0], wide - 2 * na * room), values.dtype))
            all_ref[b * 2 + f, :, side * wide : (side + 1) * wide] = jnp.concatenate(parts, 1)
    held, features = w_ref.shape[0], g_ref.shape[1]
    rest = 2 * wide - features
    fold = held * rest // features
    for (i, j), ref in zip(FLIPS, (o0_ref, o1_ref, o2_ref, o3_ref)):
        block = all_ref[(place_ref[1] ^ i) * 2 + (place_ref[3] ^ j)]
        ref[:held, :] = block[:, :features]
        for part in range(features // rest):
            rows = block[part * fold : (part + 1) * fold, features:]
            ref[held : held + fold, part * rest : (part + 1) * rest] = rows
        ref[held + fold :, :] = g_ref[...]


def gather_units_kernel(
    place_ref, p0, p1, p2, p3, d_ref, w_ref, gain_ref,
    out_ref, gain_grad_ref, down_ref, outs_ref, part_ref,
):
    hidden, features = down_ref.shape
    room = unit_room(hidden)
    lead = d_ref.shape[0]
    rest = room - lead
    down_ref[:lead, :] = d_ref[:, :features].astype(F32)
    size = d_ref.shape[1] - features
    for part in range(features // size):
        block = d_ref[part * rest : (part + 1) * rest, features:].astype(F32)
        down_ref[lead:, part * size : (part + 1) * size] = block[: hidden - lead, :]
    b, f = place_ref[1], place_ref[3]
    columns = part_ref.shape[2]
    total = 0.0
    for (i, j), ref in zip(FLIPS, (p0, p1, p2, p3)):
        part_ref[(b ^ i) * 2 + (f ^ j)] = ref[:, :columns]
        total = total + ref[:, columns:].astype(F32)
    outs_ref[...] = total
    half = w_ref.shape[1] // 2
    wide = part_ref.shape[2] // 2
    na = NA
    hidden = half // (8 * na)
    room = unit_room(hidden)
    total = 0.0
    for side in range(2):
        parts = []
        for a, b, c, f in itertools.product(range(na), range(2), range(2), range(2)):
            start = side * wide + room * (a * 2 + c)
            parts.append(part_ref[b * 2 + f][:, start : start + hidden].astype(F32))
        grad = jnp.concatenate(parts, 1)
        out_ref[:, side * half : (side + 1) * half] = grad
        weights = w_ref[:, side * half : (side + 1) * half].astype(F32)
        total = total + jnp.sum(weights * grad, -1, keepdims=True)
    gain_grad_ref[...] = total / gain_ref[...]


def assemble(place_ref, p0_ref, p1_ref, p2_ref, p3_ref, w_ref, gain_ref):
    b, f = place_ref[1], place_ref[3]
    groups, _, width = p0_ref.shape
    held = w_ref.shape[0] // (4 * groups)
    pieces = (p0_ref, p1_ref, p2_ref, p3_ref)
    for (i, j), ref in zip(FLIPS, pieces):
        for a, c in itertools.product(range(groups // 2), range(2)):
            rows = rows_at(device_row(a, b ^ i, c, f ^ j), held)
            for part in range(3):
                w_ref[rows, part * width : (part + 1) * width] = ref[
                    a * 2 + c, part * held : (part + 1) * held, :
                ]
    for i in range(2):
        for a in range(groups // 2):
            total = 0.0
            for j, c in itertools.product(range(2), range(2)):
                total = total + pieces[i * 2 + j][a * 2 + c, 3 * held :, :].astype(F32)
            lanes = pl.ds(pl.multiple_of((a * 2 + (b ^ i)) * width, width), width)
            gain_ref[:, lanes] = total[:8]


def project_kernel(
    place_ref, x_ref, w_ref, gain_ref, cos_ref, sin_ref, n_ref, keep_ref, send_ref
):
    project_block(x_ref, w_ref, gain_ref, cos_ref, sin_ref, n_ref, keep_ref, send_ref)


def project_first_kernel(
    place_ref, x_ref, p0_ref, p1_ref, p2_ref, p3_ref, cos_ref, sin_ref,
    n_ref, keep_ref, send_ref, w_ref, gain_ref,
):
    @pl.when(pl.program_id(0) == 0)
    def _():
        assemble(place_ref, p0_ref, p1_ref, p2_ref, p3_ref, w_ref, gain_ref)

    project_block(x_ref, w_ref, gain_ref, cos_ref, sin_ref, n_ref, keep_ref, send_ref)


def project_block(x_ref, w_ref, gain_ref, cos_ref, sin_ref, n_ref, keep_ref, send_ref):
    width = w_ref.shape[1] // 3
    rows = x_ref.shape[1] // 2
    values = x_ref[0].astype(F32)
    inverse = lax.rsqrt(jnp.mean(values * values, -1, keepdims=True) + epsilon)
    normed = (values * inverse * gain_ref[0:1, :]).astype(BF16)
    n_ref[0] = normed
    projected = jnp.dot(normed, w_ref[...], preferred_element_type=F32)
    cosine = cos_ref[0, 0]
    sine = sin_ref[0, 0]
    for part in range(2):
        block = projected[:, part * width : (part + 1) * width]
        turned = (block * cosine + half_swap(block) * sine).astype(BF16)
        keep_ref[0, :, part * width : (part + 1) * width] = turned[:rows]
        send_ref[0, :, part * width : (part + 1) * width] = turned[rows:]
    values = projected[:, 2 * width :].astype(BF16)
    keep_ref[0, :, 2 * width :] = values[:rows]
    send_ref[0, :, 2 * width :] = values[rows:]


def project(places, flip, x, weights, cosine, sine):
    count, rows, features = x.shape
    third = cosine.shape[3]
    wide = 3 * third

    def by_step(*block):
        return pl.BlockSpec((1,) + block, lambda step, place: (step, 0, 0))

    def table_map(step, place):
        return (step ^ place[0], place[2] ^ flip, 0, 0)

    def fixed(*block):
        return pl.BlockSpec(block, lambda step, place: (0,) * len(block))

    table = pl.BlockSpec((1, 1, rows, third), table_map)
    first = len(weights) > 2
    shapes = [
        like(count, rows, features),
        like(count, rows // 2, wide),
        like(count, rows // 2, wide),
    ]
    specs = [by_step(rows, features), by_step(rows // 2, wide), by_step(rows // 2, wide)]
    if first:
        shapes += [like(features, wide), like(8, features, dtype=F32)]
        specs += [fixed(features, wide), fixed(8, features)]
    return pl.pallas_call(
        project_first_kernel if first else project_kernel,
        grid_spec=pltpu.PrefetchScalarGridSpec(
            num_scalar_prefetch=1,
            grid=(count,),
            in_specs=[
                by_step(rows, features),
                *[fixed(*weight.shape) for weight in weights],
                table,
                table,
            ],
            out_specs=specs,
        ),
        out_shape=shapes,
        compiler_params=pltpu.CompilerParams(
            vmem_limit_bytes=16 * 2**20 if first else 8 * 2**20
        ),
        cost_estimate=pl.CostEstimate(
            flops=2 * count * rows * features * wide,
            bytes_accessed=count * rows * features * 4 + features * wide * 2,
            transcendentals=count * rows,
        ),
        name="project_first" if first else "project",
    )(places, x, *weights, cosine, sine)


def block_scores(head, query, keys, seg, start, scale):
    lanes = lax.broadcasted_iota(jnp.int32, query.shape, 1)
    masked = jnp.where(lanes // HEAD_DIM == head, query, jnp.zeros_like(query))
    raw = lax.dot_general(masked, keys, LAST, preferred_element_type=F32) * scale
    row = start + lax.broadcasted_iota(jnp.int32, raw.shape, 0)
    column = lax.broadcasted_iota(jnp.int32, raw.shape, 1)
    valid = (column >= seg) & (column <= row)
    scores = jnp.where(valid, raw, masked_score)
    top = jnp.max(scores, -1, keepdims=True)
    weights = jnp.exp(scores - top)
    total = jnp.sum(weights, -1, keepdims=True)
    return masked, weights * (1.0 / total)


def row_block(place_ref, step, b_flip, c_flip):
    a, b, c = place_ref[0] ^ step, place_ref[1] ^ b_flip, place_ref[2] ^ c_flip
    return (a * 2 + b) * 2 + c


def attend_kernel(
    place_ref, k0_ref, k1_ref, r0_ref, r1_ref, seg_ref, first_ref, o_ref, all_ref
):
    count, rows, wide = k0_ref.shape
    width = wide // 3
    length = all_ref.shape[0]
    for (b_flip, c_flip), ref in zip(FLIPS, (k0_ref, k1_ref, r0_ref, r1_ref)):
        for step in range(count):
            all_ref[rows_at(row_block(place_ref, step, b_flip, c_flip), rows), :] = ref[step]
    size = min(256, length)
    scale = HEAD_DIM ** (-0.5)
    for start in range(0, length, size):
        stop = start + size
        own = all_ref[start:stop, 2 * width :].astype(F32)
        first = first_ref[start:stop, :].astype(F32)
        all_ref[start:stop, 2 * width :] = (0.5 * own + 0.5 * first).astype(BF16)
        query = all_ref[start:stop, :width]
        keys = all_ref[:stop, width : 2 * width]
        values = all_ref[:stop, 2 * width :]
        seg = seg_ref[start:stop, :]

        def one(head):
            _, weights = block_scores(head, query, keys, seg, start, scale)
            return jnp.dot(weights.astype(BF16), values, preferred_element_type=F32)

        lanes = lax.broadcasted_iota(jnp.int32, (size, width), 1)
        result = one(0)
        for head in range(1, width // HEAD_DIM):
            result = jnp.where(lanes // HEAD_DIM == head, one(head), result)
        o_ref[start:stop, :] = result.astype(BF16)


def attend_back_kernel(
    place_ref, all_ref, seg_ref, do_ref, cos_ref, sin_ref, k_ref, r_ref, dk_ref, dv_ref, full_ref
):
    _, count, rows, wide = k_ref.shape
    width = wide // 3
    length = all_ref.shape[0]
    size = min(256, length)
    scale = HEAD_DIM ** (-0.5)
    dk_ref[...] = jnp.zeros_like(dk_ref)
    dv_ref[...] = jnp.zeros_like(dv_ref)
    for start in range(0, length, size):
        stop = start + size
        query = all_ref[start:stop, :width]
        keys = all_ref[:stop, width : 2 * width]
        values = all_ref[:stop, 2 * width :]
        seg = seg_ref[start:stop, :]
        out_grad = do_ref[start:stop, :]
        lanes = lax.broadcasted_iota(jnp.int32, (size, width), 1)

        def one(head):
            masked, weights = block_scores(head, query, keys, seg, start, scale)
            grad = jnp.where(lanes // HEAD_DIM == head, out_grad, jnp.zeros_like(out_grad))
            weight_grad = lax.dot_general(grad, values, LAST, preferred_element_type=F32)
            delta = jnp.sum(weights * weight_grad, -1, keepdims=True)
            score_grad = (weights * (weight_grad - delta)).astype(BF16)
            dv_ref[:stop, :] += lax.dot_general(
                weights.astype(BF16), grad, FIRST, preferred_element_type=F32
            )
            dk_ref[:stop, :] += lax.dot_general(
                score_grad, masked, FIRST, preferred_element_type=F32
            )
            return jnp.dot(score_grad, keys, preferred_element_type=F32)

        query_grad = one(0)
        for head in range(1, width // HEAD_DIM):
            query_grad = jnp.where(lanes // HEAD_DIM == head, one(head), query_grad)
        query_grad = query_grad * scale
        cosine = cos_ref[start:stop, :]
        sine = sin_ref[start:stop, :]
        full_ref[start:stop, :width] = (
            query_grad * cosine - half_swap(query_grad) * sine
        ).astype(BF16)
    for start in range(0, length, size):
        stop = start + size
        key_grad = dk_ref[start:stop, :] * scale
        cosine = cos_ref[start:stop, :]
        sine = sin_ref[start:stop, :]
        full_ref[start:stop, width : 2 * width] = (
            key_grad * cosine - half_swap(key_grad) * sine
        ).astype(BF16)
        full_ref[start:stop, 2 * width :] = (0.5 * dv_ref[start:stop, :]).astype(BF16)
    for b_flip, c_flip in FLIPS:
        ref = (k_ref, r_ref)[b_flip]
        for step in range(count):
            ref[c_flip, step] = full_ref[
                rows_at(row_block(place_ref, step, b_flip, c_flip), rows), :
            ]


def assemble_out(place_ref, own_ref, other_ref, w_ref):
    a, b, c, f = [place_ref[k] for k in range(4)]
    na = own_ref.shape[1]
    held = other_ref.shape[2]
    for k, (i, j) in enumerate(FLIPS):
        for step in range(na):
            for c_flip, ref in enumerate((own_ref, other_ref)):
                row = device_row(a ^ step, b ^ i, c ^ c_flip, f ^ j)
                w_ref[rows_at(row, held), :] = ref[k, step]


def out_kernel(
    place_ref, heads_ref, own_ref, other_ref, x_ref, gain_ref,
    o_ref, h_ref, n_ref, sum_ref, w_ref,
):
    rows, width = heads_ref.shape[1:]
    assemble_out(place_ref, own_ref, other_ref, w_ref)
    for p in range(o_ref.shape[1] // width):
        for r in range(2):
            o_ref[r * rows : (r + 1) * rows, p * width : (p + 1) * width] = heads_ref[
                ((p // 2) * 2 + r) * 2 + p % 2
            ]
    branch = jnp.dot(o_ref[...], w_ref[...], preferred_element_type=F32)
    stream = x_ref[...].astype(F32) + branch
    h_ref[...] = stream
    inverse = lax.rsqrt(jnp.mean(stream * stream, -1, keepdims=True) + epsilon)
    n_ref[...] = (stream * inverse * gain_ref[1:2, :]).astype(BF16)
    sum_ref[0:1, :] = jnp.sum(stream * stream, 0, keepdims=True)
    sum_ref[1:2, :] = jnp.sum(branch * branch, 0, keepdims=True)


def feed_kernel(
    place_ref, n0, n1, n2, n3, g0, g1, g2, g3, w_ref,
    act_ref, dgu_ref, b0_ref, b1_ref, b2_ref, b3_ref, down_ref, n_ref, g_ref, full_ref,
):
    a, b, c, f = [place_ref[k] for k in range(4)]
    na, wide = w_ref.shape[0] // 2, w_ref.shape[2]
    padded, features = down_ref.shape
    held = features // (8 * na)
    rows = n0.shape[0]
    room = padded // (2 * na)
    lead = room * features // wide
    rest = room - lead
    for s, (da, dc) in enumerate(itertools.product(range(na), range(2))):
        for k, (i, j) in enumerate(FLIPS):
            row = device_row(da, b ^ i, dc, f ^ j)
            full_ref[rows_at(row, held), :] = w_ref[s, k * held : (k + 1) * held, :]
        base = 4 * held
        start = s * room
        down_ref[start : start + lead, :] = w_ref[s, base:, :features]
        for part in range(features // (wide - features)):
            lanes = slice(part * (wide - features), (part + 1) * (wide - features))
            here = slice(base + part * rest, base + (part + 1) * rest)
            down_ref[start + lead : start + room, lanes] = w_ref[s, here, features:]
    for k, (n_part, g_part) in enumerate(zip((n0, n1, n2, n3), (g0, g1, g2, g3))):
        n_ref[k * rows : (k + 1) * rows, :] = n_part[...]
        g_ref[k * rows : (k + 1) * rows, :] = g_part[g_part.shape[0] - rows :, :]
    size = 256
    for start in range(0, padded, size):
        here = slice(start, start + size)
        there = slice(padded + start, padded + start + size)
        gate = jnp.dot(n_ref[...], full_ref[:, here], preferred_element_type=F32)
        upward = jnp.dot(n_ref[...], full_ref[:, there], preferred_element_type=F32)
        act_grad = lax.dot_general(g_ref[...], down_ref[here, :], LAST, preferred_element_type=F32)
        sigmoid_gate = jax.nn.sigmoid(gate)
        silu_gate = gate * sigmoid_gate
        act_ref[:, here] = (silu_gate * upward).astype(BF16)
        dgu_ref[:, here] = (
            act_grad * upward * sigmoid_gate * (1.0 + gate * (1.0 - sigmoid_gate))
        ).astype(BF16)
        dgu_ref[:, there] = (act_grad * silu_gate).astype(BF16)
    for k in range(4):
        back = lax.dot_general(
            dgu_ref[k * rows : (k + 1) * rows, :], full_ref[...], LAST, preferred_element_type=F32
        )
        ref = (b0_ref, b1_ref, b2_ref, b3_ref)[k]
        ref[...] = back.astype(ref.dtype)


def feed_grads_kernel(
    place_ref, n0, n1, n2, n3, g0, g1, g2, g3, act_ref, dgu_ref,
    own_ref, send_ref, n_ref, g_ref, out_ref,
):
    b, c, f = place_ref[1], place_ref[2], place_ref[3]
    rows = n0.shape[0]
    for k, (n_part, g_part) in enumerate(zip((n0, n1, n2, n3), (g0, g1, g2, g3))):
        n_ref[k * rows : (k + 1) * rows, :] = n_part[...]
        g_ref[k * rows : (k + 1) * rows, :] = g_part[g_part.shape[0] - rows :, :]
    groups, _, wide = out_ref.shape
    padded, features = act_ref.shape[1], g_ref.shape[1]
    held = features // (4 * groups)
    room = padded // groups
    size = 512
    for start in range(0, wide, size):
        here = slice(start, start + size)
        grad = lax.dot_general(
            n_ref[...], dgu_ref[:, here], FIRST, preferred_element_type=F32
        ).astype(BF16)
        for s, (da, dc) in enumerate(itertools.product(range(groups // 2), range(2))):
            for db, df in FLIPS:
                row = device_row(da, db, dc, df) * held
                k = (b ^ db) * 2 + (f ^ df)
                out_ref[s, rows_at(k, held), here] = grad[row : row + held, :]
    grad = lax.dot_general(act_ref[...], g_ref[...], FIRST, preferred_element_type=F32).astype(BF16)
    lead = room * features // wide
    rest = room - lead
    base = 4 * held
    for s in range(groups):
        block = grad[room * s : room * (s + 1), :]
        out_ref[s, base:, :features] = block[:lead, :]
        for part in range(features // (wide - features)):
            lanes = slice(part * (wide - features), (part + 1) * (wide - features))
            there = slice(base + part * rest, base + (part + 1) * rest)
            out_ref[s, there, features:] = block[lead:, lanes]
    for a in range(groups // 2):
        own_ref[a] = out_ref[a * 2 + c]
        send_ref[a] = out_ref[a * 2 + (1 - c)]


def feed_branch_kernel(act_ref, down_ref, f0_ref, f1_ref, f2_ref, f3_ref):
    rows = f0_ref.shape[0]
    for k, ref in enumerate((f0_ref, f1_ref, f2_ref, f3_ref)):
        ffn = jnp.dot(
            act_ref[k * rows : (k + 1) * rows, :], down_ref[...], preferred_element_type=F32
        )
        ref[...] = ffn.astype(ref.dtype)


def norm_back(values, gain, normed_grad):
    inverse = lax.rsqrt(jnp.mean(values * values, -1, keepdims=True) + epsilon)
    scaled = normed_grad * gain
    return inverse * scaled - values * (inverse * inverse * inverse) * jnp.mean(
        scaled * values, -1, keepdims=True
    )


def stream_back_kernel(
    place_ref, p0, p1, p2, p3, h_ref, gain_ref, g_ref, w0_ref, w1_ref, o_ref,
    dh_ref, do_ref, own_ref, send_ref, out_ref, w_ref,
):
    assemble_out(place_ref, w0_ref, w1_ref, w_ref)
    normed_grad = p0[...] + p1[...].astype(F32) + p2[...].astype(F32) + p3[...].astype(F32)
    stream = h_ref[...]
    stream_grad = g_ref[...].astype(F32) + norm_back(stream, gain_ref[1:2, :], normed_grad)
    dh_ref[...] = stream_grad
    low = stream_grad.astype(BF16)
    heads = lax.dot_general(low, w_ref[...], LAST, preferred_element_type=F32).astype(BF16)
    rows, width = do_ref.shape[1:]
    for p in range(heads.shape[1] // width):
        for r in range(2):
            do_ref[((p // 2) * 2 + r) * 2 + p % 2] = heads[
                r * rows : (r + 1) * rows, p * width : (p + 1) * width
            ]
    total = lax.dot_general(o_ref[...], low, FIRST, preferred_element_type=F32).astype(BF16)
    b, f = place_ref[1], place_ref[3]
    groups = out_ref.shape[0]
    held = out_ref.shape[1] // 4
    for s, (da, dc) in enumerate(itertools.product(range(groups // 2), range(2))):
        for db, df in FLIPS:
            row = device_row(da, db, dc, df) * held
            k = (b ^ db) * 2 + (f ^ df)
            out_ref[s, rows_at(k, held), :] = total[row : row + held, :]
    c = place_ref[2]
    for a in range(groups // 2):
        own_ref[a] = out_ref[a * 2 + c]
        send_ref[a] = out_ref[a * 2 + (1 - c)]


def fill_pairs(d_ref, keep_ref, recv_ref, flip):
    _, count, rows, _ = keep_ref.shape
    for step in range(count):
        base = 2 * rows * step
        d_ref[base : base + rows, :] = keep_ref[flip, step]
        d_ref[base + rows : base + 2 * rows, :] = recv_ref[flip, step]


def unproject_other_kernel(keep_ref, recv_ref, w_ref, dn_ref, d_ref):
    fill_pairs(d_ref, keep_ref, recv_ref, 1)
    count, rows, _ = dn_ref.shape
    for step in range(count):
        back = lax.dot_general(
            d_ref[rows * step : rows * (step + 1), :], w_ref[...], LAST, preferred_element_type=F32
        )
        dn_ref[step] = back.astype(BF16)


def unproject_own_kernel(
    keep_ref, recv_ref, w_ref, other_ref, own_ref, s1_ref, s2_ref, s3_ref, d_ref
):
    fill_pairs(d_ref, keep_ref, recv_ref, 0)
    count, rows, _ = other_ref.shape
    for step in range(count):
        back = lax.dot_general(
            d_ref[rows * step : rows * (step + 1), :], w_ref[...], LAST, preferred_element_type=F32
        )
        back = back + other_ref[step].astype(F32)
        if step == 0:
            own_ref[...] = back
        else:
            (s1_ref, s2_ref, s3_ref)[step - 1][...] = back.astype(BF16)


def qkv_grads_kernel(
    place_ref, k_ref, r_ref, n0_ref, n1_ref, stat_ref,
    own_ref, send_ref, d_ref, total_ref,
):
    b, f = place_ref[1], place_ref[3]
    _, count, rows, wide = k_ref.shape
    width = wide // 3
    features = n0_ref.shape[2]
    for flip, n_ref in enumerate((n0_ref, n1_ref)):
        fill_pairs(d_ref, k_ref, r_ref, flip)
        tokens = n_ref[...].reshape(2 * rows * count, features)
        grad = lax.dot_general(tokens, d_ref[...], FIRST, preferred_element_type=F32)
        if flip == 0:
            total_ref[...] = grad
        else:
            total_ref[...] += grad
    held = features // (8 * count)
    block = 3 * held
    bottom = block * 2 * count
    own_ref[bottom:, :] = stat_ref[...]
    for k in range(3):
        send_ref[k, bottom:, :] = spread_digits(stat_ref[...])
    for k, (i, j) in enumerate(FLIPS):
        for s, (da, dc) in enumerate(itertools.product(range(count), range(2))):
            piece = total_ref[rows_at(device_row(da, b ^ i, dc, f ^ j), held), :]
            for part in range(3):
                lanes = piece[:, part * width : (part + 1) * width]
                there = slice(s * block + part * held, s * block + (part + 1) * held)
                if k == 0:
                    own_ref[there, :] = lanes
                else:
                    send_ref[k - 1, there, :] = lanes.astype(BF16)


def qkv_sum_kernel(
    place_ref, own_ref, r1_ref, r2_ref, r3_ref, kept_ref, moved_ref, out_ref
):
    a, c = place_ref[0], place_ref[2]
    parts, rows, width = out_ref.shape
    _, count, length, _ = kept_ref.shape
    block = rows - 16 - 2 * length
    bottom = parts * block
    received = (r1_ref, r2_ref, r3_ref)
    stats = own_ref[bottom:, :]
    for ref in received:
        stats = stats + add_digits(ref[bottom:, :])
    digits = spread_digits(stats)
    for p in range(parts):
        here = slice(p * block, (p + 1) * block)
        total = own_ref[here, :]
        for ref in received:
            total = total + ref[here, :].astype(F32)
        out_ref[p, :block, :] = total.astype(BF16)
        out_ref[p, block : block + 16, :] = digits
    base = block + 16
    for c_flip in range(2):
        for step in range(count):
            p = (a ^ step) * 2 + (c ^ c_flip)
            for r, ref in enumerate((kept_ref, moved_ref)):
                there = slice(base + r * length, base + (r + 1) * length)
                out_ref[p, there, :] = ref[c_flip, step, :, 2 * width :]


def join_grads_kernel(units_ref, outs_ref, out_ref):
    held = out_ref.shape[1]
    wide = units_ref.shape[1]
    for k in range(4):
        here = slice(k * held, (k + 1) * held)
        out_ref[k, :, :wide] = units_ref[here, :]
        out_ref[k, :, wide:] = outs_ref[here, :]


def finish_out_kernel(h_ref, ffn_ref, r1_ref, r2_ref, r3_ref, sum_ref, out_ref, total_ref):
    branch = ffn_ref[...]
    for ref in (r1_ref, r2_ref, r3_ref):
        branch = branch + ref[...].astype(F32)
    out_ref[...] = (h_ref[...] + branch).astype(BF16)
    squares = jnp.sum(branch * branch, 0, keepdims=True)
    lanes = lax.broadcasted_iota(jnp.int32, total_ref.shape, 1)
    totals = jnp.zeros(total_ref.shape, F32)
    for k in range(3):
        values = squares if k == 2 else sum_ref[k : k + 1, :]
        totals = jnp.where(lanes == k, jnp.sum(values, -1, keepdims=True), totals)
    total_ref[...] = totals


def finish_kernel(
    entries, place_ref, part_ref, w_ref, gain_ref, out_ref, gain_grad_ref, stat_ref, first_ref
):
    parts, _, width = part_ref.shape
    base = 3 * out_ref.shape[0]
    rows = first_ref.shape[1]
    stats = 0.0
    for p in range(parts):
        stats = stats + add_digits(part_ref[p, base : base + 16, :])
        for r in range(2):
            start = base + 16 + r * rows
            first_ref[place_ref[1] ^ r, :, p * width : (p + 1) * width] = part_ref[
                p, start : start + rows, :
            ].astype(F32)
    stat_ref[...] = jnp.sqrt(stats[:8] / entries)
    held = out_ref.shape[0]
    features = parts * width
    total = 0.0
    for part in range(3):
        for p in range(parts):
            grad = part_ref[p, part * held : (part + 1) * held, :].astype(F32)
            lanes = slice(part * features + p * width, part * features + (p + 1) * width)
            out_ref[:, lanes] = grad
            total = total + jnp.sum(w_ref[:, lanes].astype(F32) * grad, -1, keepdims=True)
    gain_grad_ref[...] = total / gain_ref[...]


def tokens_back_kernel(place_ref, p0, p1, p2, p3, x_ref, gain_ref, dh_ref, out_ref):
    b = place_ref[1]
    rows = out_ref.shape[1]
    for r in range(2):
        here = slice(r * rows, (r + 1) * rows)
        normed_grad = (
            p0[here, :] + p1[here, :].astype(F32) + p2[here, :].astype(F32) + p3[here, :].astype(F32)
        )
        row = b ^ r
        values = x_ref[row].astype(F32)
        out_ref[row] = dh_ref[row] + norm_back(values, gain_ref[0:1, :], normed_grad)


def turn_tables(positions, width):
    quarter = HEAD_DIM // 2
    freqs = jnp.power(10000.0, -jnp.arange(quarter, dtype=F32) / quarter)
    freqs = jnp.tile(freqs, width // quarter)
    signs = jnp.where(jnp.arange(width) % HEAD_DIM < quarter, -1.0, 1.0)
    angles = positions.astype(F32)[..., None] * freqs
    return jnp.cos(angles), jnp.sin(angles) * signs


def grid_body(tokens, v_first, segments, grad_out, w_qkv, w_out, w_gate_up, w_down, gain_attn, gain_ffn):
    row_count, shard_len, features = tokens.shape[1:]
    a, b, c, f = [lax.axis_index(name) for name in GRID]
    na = lax.axis_size("a")
    nd = 8 * na
    width = features // (2 * na)
    held = features // nd
    hidden = w_down.shape[0]
    room = unit_room(hidden)
    padded = 2 * na * room
    wide = 2 * padded
    length = 4 * na * shard_len
    count = row_count * shard_len
    places = jnp.stack([a, b, c, f]).astype(jnp.int32)
    a_steps = range(1, na)

    def plane_hops(pieces, tag):
        return [hop(piece, tag, b=i, f=j) for piece, (i, j) in zip(pieces, FLIPS[1:])]

    def a_hops(value, tag):
        return [value] + [hop(value, tag, a=step) for step in a_steps]

    mine = tokens[0]
    parts = a_hops(w_out, "out_a")
    turned, sent = call(
        prepare_kernel,
        "prepare",
        [like(count, features), like(2 * na, 3 * held + 16, width)],
        [places, after(mine, *parts), w_qkv, segments[0], gain_attn[None], gain_ffn[None]],
        limit=60 * 2**20,
    )

    token_parts = a_hops(turned, "tokens_a")
    sent = swap(sent, "qkv_ac", ("a", "c"))
    grads = grad_out.reshape(count, features)
    tall = held * wide // features + count
    plane = call(
        spread_kernel,
        "spread",
        [like(tall, features)] * 4,
        [places, w_gate_up, grads],
        scratch=[pltpu.VMEM((4, held, wide), BF16)],
        limit=60 * 2**20,
    )
    plane = lax.optimization_barrier((*plane, turned))[:4]
    plane = [plane[0]] + plane_hops(plane[1:], "units_bf")
    units = call(
        join_units_kernel, "join_units", like(6 * held, wide), [*plane, w_down], scalars=0
    )
    near = sent
    sent = after(sent, *token_parts[1:], units)
    first = call(
        by_heads_kernel, "by_heads", like(4 * na, shard_len, width), [v_first[0]], scalars=0
    )
    first = swap(after(first, sent), "first_abc", ("a", "b", "c")).reshape(length, width)
    pieces = [sent] + plane_hops([sent] * 3, "qkv_bf")
    sent = after(pieces[0], first, *pieces[1:])
    units = lax.all_gather(after(units, sent), ("a", "c"), axis=0, tiled=False)

    group_tokens = jnp.stack(token_parts)
    other_tokens = hop(group_tokens, "tokens_c", c=1)
    def pick(array, index, dim):
        return lax.dynamic_index_in_dim(array, index, dim, keepdims=False)

    def starts_of(small):
        digits = small[..., 3 * held + 2 : 3 * held + 4, :].astype(jnp.int32)
        digits = digits[..., 0, :] * 256 + digits[..., 1, :]
        return digits.reshape(na, 2, row_count, shard_len)

    group_starts = starts_of(near)
    all_starts = ordered(group_starts, starts_of(pieces[2]), b, 1)
    group_starts = jnp.where(b == 0, group_starts, group_starts[:, :, ::-1])
    order = jnp.arange(2 * na, dtype=jnp.int32).reshape(na, 2, 1, 1)
    offset = jnp.arange(shard_len, dtype=jnp.int32)
    block = (order // 2 * 2 + b) * 2 + order % 2
    positions = block * shard_len + offset - group_starts
    cosine, sine = turn_tables(positions.reshape(na, 2, count), width)
    n_part, keep, send, *qkv = project(
        places, 0, group_tokens, [sent, *pieces[1:]], cosine, sine
    )
    qkv_weights, gains = qkv
    normed, keeps, sends = [n_part], [keep], [hop(send, "heads_b", b=1)]
    n_part, keep, send = project(places, 1, other_tokens, qkv, cosine, sine)
    normed.append(n_part)
    keeps.append(keep)
    sends.append(hop(send, "heads_b", b=1))

    parts = jnp.stack(lax.optimization_barrier((*parts, *keeps))[:na])
    parts = [parts] + plane_hops([parts] * 3, "out_bf")
    row_starts = pick(all_starts, b, 3).reshape(length)
    heads, everything = call(
        attend_kernel,
        "attend",
        [like(length, width), like(length, 3 * width)],
        [places, *keeps, *sends, row_starts[:, None], first],
        flops=8 * length * length * width,
    )

    parts = jnp.stack(lax.optimization_barrier((*parts, heads))[:4])
    other_parts = hop(parts, "out_c", c=1)

    heads = swap(heads.reshape(4 * na, shard_len, width), "heads_abc", ("a", "b", "c"))
    inputs = mine.reshape(count, features)
    attention, stream, normed_two, sums = call(
        out_kernel,
        "out_project",
        [
            like(count, features),
            like(count, features, dtype=F32),
            like(count, features),
            like(2, features, dtype=F32),
        ],
        [places, heads, parts, other_parts, inputs, gains],
        scratch=[pltpu.VMEM((features, features), BF16)],
        flops=2 * count * features * features,
    )
    group_two = [normed_two] + plane_hops([normed_two] * 3, "two_bf")

    act, units_grad, back0, *backs, full_down = call(
        feed_kernel,
        "feed",
        [
            like(4 * count, padded),
            like(4 * count, wide),
            like(count, features, dtype=F32),
            *[like(count, features)] * 3,
            like(padded, features),
        ],
        [places, *group_two, *plane, units],
        scratch=[
            pltpu.VMEM((4 * count, features), BF16),
            pltpu.VMEM((4 * count, features), BF16),
            pltpu.VMEM((features, wide), BF16),
        ],
        flops=16 * count * features * padded * 3,
        limit=60 * 2**20,
    )
    backs = plane_hops(backs, "two_back_bf")
    units_own, units_send = call(
        feed_grads_kernel,
        "feed_grads",
        [like(na, 6 * held, wide)] * 2,
        [places, *group_two, *plane, act, units_grad],
        scratch=[
            pltpu.VMEM((4 * count, features), BF16),
            pltpu.VMEM((4 * count, features), BF16),
            pltpu.VMEM((2 * na, 6 * held, wide), BF16),
        ],
        flops=16 * count * features * padded * 2,
        limit=60 * 2**20,
    )

    ffn0, *ffn = call(
        feed_branch_kernel,
        "feed_branch",
        [like(count, features, dtype=F32)] + [like(count, features)] * 3,
        [act, full_down],
        flops=8 * count * features * padded,
        scalars=0,
        limit=60 * 2**20,
    )

    def add_c(own, send, tag, *earlier):
        send = after(hop(send, tag, c=1), *earlier)
        return (own.astype(F32) + send.astype(F32)).astype(BF16)

    units_part = add_c(units_own, units_send, "units_back_c")
    back0 = after(back0, units_part)
    units_part = lax.psum_scatter(units_part, "a", scatter_dimension=0, tiled=True)
    units_rs = units_part

    stream_grad, heads_grad, out_own, out_send = call(
        stream_back_kernel,
        "stream_back",
        [
            like(count, features, dtype=F32),
            like(4 * na, shard_len, width),
            *[like(na, 4 * held, features)] * 2,
        ],
        [places, back0, *backs, stream, gains, grads, parts, other_parts, attention],
        scratch=[
            pltpu.VMEM((2 * na, 4 * held, features), BF16),
            pltpu.VMEM((features, features), BF16),
        ],
        flops=4 * count * features * features,
        limit=60 * 2**20,
    )

    heads_grad = swap(heads_grad, "heads_back_abc", ("a", "b", "c"))
    ffn = plane_hops(ffn, "ffn_bf")

    cosine, sine = turn_tables(
        after(jnp.arange(length, dtype=jnp.int32) - row_starts, everything), width
    )
    kept, moved = call(
        attend_back_kernel,
        "attend_back",
        [like(2, na, shard_len, 3 * width)] * 2,
        [
            places,
            everything,
            row_starts[:, None],
            after(heads_grad.reshape(length, width), *ffn),
            cosine,
            sine,
        ],
        scratch=[
            pltpu.VMEM((length, width), F32),
            pltpu.VMEM((length, width), F32),
            pltpu.VMEM((length, 3 * width), BF16),
        ],
        flops=20 * length,
    )
    moved = hop(moved, "back_b", b=1)
    out_part = add_c(out_own, after(out_send, ffn[0]), "out_back_c")
    out_part = lax.psum_scatter(out_part, "a", scatter_dimension=0, tiled=True)
    out, total = call(
        finish_out_kernel,
        "finish_out",
        [like(count, features), like(16, width, dtype=F32)],
        [stream, after(ffn0, kept), *ffn, sums],
        scalars=0,
    )

    dn1 = call(
        unproject_other_kernel,
        "unproject_other",
        like(na, count, features),
        [kept, moved, qkv_weights],
        scratch=[pltpu.VMEM((na * count, 3 * width), BF16)],
        flops=2 * na * count * features * 3 * width,
        scalars=0,
    )
    dn1 = hop(dn1, "tokens_back_c", c=1)
    own, send = call(
        qkv_grads_kernel,
        "qkv_grads",
        [like(features * 3 // 4 + 16, width, dtype=F32), like(3, features * 3 // 4 + 16, width)],
        [places, kept, moved, normed[0], normed[1], total],
        scratch=[
            pltpu.VMEM((na * count, 3 * width), BF16),
            pltpu.VMEM((features, 3 * width), F32),
        ],
        flops=4 * na * count * features * 3 * width,
    )
    own_tokens, *send_tokens = call(
        unproject_own_kernel,
        "unproject_own",
        [like(count, features, dtype=F32)] + [like(count, features)] * 3,
        [kept, moved, qkv_weights, dn1],
        scratch=[pltpu.VMEM((na * count, 3 * width), BF16)],
        flops=2 * na * count * features * 3 * width,
        scalars=0,
    )
    token_grads = [hop(send_tokens[step - 1], "tokens_back_a", a=step) for step in a_steps]
    units_part = units_part[0]
    units_part = after(units_part, token_grads[0])
    rows = call(
        join_grads_kernel,
        "join_grads",
        like(4, held, wide + features),
        [units_part, out_part[0]],
        scalars=0,
    )
    rows = [rows[0]] + plane_hops([rows[k] for k in range(1, 4)], "units_back_bf")
    grad_gate_up, ffn_gain_grad, grad_down, grad_out_weights = call(
        gather_units_kernel,
        "gather_units",
        [
            like(*w_gate_up.shape, dtype=F32),
            like(held, 1, dtype=F32),
            like(hidden, features, dtype=F32),
            like(held, features, dtype=F32),
        ],
        [places, *rows, units_part[4 * held :], w_gate_up, gain_ffn.astype(F32)[:, None]],
        scratch=[pltpu.VMEM((4, held, wide), BF16)],
    )

    last = call(
        qkv_sum_kernel,
        "qkv_sum",
        like(2 * na, 3 * held + 16 + count, width),
        [places, after(own, own_tokens, units_rs), *plane_hops([send[k] for k in range(3)], "qkv_back_bf"), kept, moved],
    )
    last = swap(last, "qkv_back_ac", ("a", "c"))
    grad_qkv, attn_gain_grad, stats, grad_first = call(
        functools.partial(finish_kernel, float(count * features * nd)),
        "finish",
        [
            like(*w_qkv.shape, dtype=F32),
            like(held, 1, dtype=F32),
            like(8, width, dtype=F32),
            like(row_count, shard_len, features, dtype=F32),
        ],
        [places, last, w_qkv, gain_attn.astype(F32)[:, None]],
    )
    grad_tokens = call(
        tokens_back_kernel,
        "tokens_back",
        like(row_count, shard_len, features, dtype=F32),
        [
            places,
            after(own_tokens, grad_gate_up),
            *token_grads,
            mine,
            gains,
            stream_grad.reshape(row_count, shard_len, features),
        ],
    )

    return (
        out.reshape(tokens.shape),
        grad_tokens[None],
        grad_first[None],
        grad_qkv,
        grad_out_weights,
        grad_gate_up,
        grad_down,
        attn_gain_grad[:, 0],
        ffn_gain_grad[:, 0],
        stats[0, :3],
    )


def fits(mesh):
    return mesh.shape["seq"] == 4 * NA and mesh.shape["fsdp"] == 2


def solution(mesh):
    if fits(mesh):
        grid = Mesh(mesh.devices.reshape(mesh.shape["seq"] // 4, 2, 2, 2), GRID)
        seq, every = ("a", "b", "c"), GRID
        body = grid_body
        fsdp = "f"
    else:
        grid, body = mesh, ring_body
        seq, every, fsdp = "seq", ("seq", "fsdp"), "fsdp"
    return jax.shard_map(
        body,
        mesh=grid,
        in_specs=(
            P(fsdp, None, seq, None),
            P(fsdp, None, seq, None),
            P(fsdp, None, seq),
            P(fsdp, None, seq, None),
            P(every, None),
            P(every, None),
            P(every, None),
            P(every, None),
            P(every),
            P(every),
        ),
        out_specs=(
            P(fsdp, None, seq, None),
            P(fsdp, None, seq, None),
            P(fsdp, None, seq, None),
            P(every, None),
            P(every, None),
            P(every, None),
            P(every, None),
            P(every),
            P(every),
            P(),
        ),
        check_vma=False,
    )
```

```python
import functools
import itertools
import math

import jax
import jax.numpy as jnp
from jax import lax
from jax.experimental import pallas as pl
from jax.experimental.pallas import tpu as pltpu
from jax.sharding import Mesh
from jax.sharding import PartitionSpec as P

HEADS = 16
HEAD_DIM = 64
FF = 2816
GRID = ("a", "b", "c", "f")
NA = 4


epsilon = 1e-06
masked_score = -1e30


def from_behind(value, axis, steps):
    count = lax.axis_size(axis)
    initial, last = (max(0, -steps), min(count, count - steps))
    return lax.ppermute(value, axis, [(source, source + steps) for source in range(initial, last)])


def shifted(shard, axis, by):
    size = lax.axis_size(axis)
    return lax.ppermute(shard, axis, [(i, (i + by) % size) for i in range(size)])


def rms_forward(values, gain):
    inverse_rms = lax.rsqrt(jnp.mean(values * values, -1, keepdims=True) + epsilon)
    return (values * inverse_rms * gain, inverse_rms)


def rms_backward(values, inverse_rms, gain, normed_grad):
    scaled = normed_grad * gain
    gain_grad = jnp.sum(normed_grad * values * inverse_rms, 0)
    input_grad = inverse_rms * scaled - values * (
        inverse_rms * inverse_rms * inverse_rms
    ) * jnp.mean(scaled * values, -1, keepdims=True)
    return (input_grad, gain_grad)


def rotation_tables(positions, head_dim):
    half_dim = head_dim // 2
    freqs = jnp.power(10000.0, -jnp.arange(half_dim, dtype=jnp.float32) / half_dim)
    angles = positions[..., None] * freqs
    return (jnp.cos(angles)[..., None, :], jnp.sin(angles)[..., None, :])


def rotate_forward(values, cosine, sine_part):
    half_dim = values.shape[-1] // 2
    first_half = values[..., :half_dim]
    second_half = values[..., half_dim:]
    return jnp.concatenate(
        [
            first_half * cosine - second_half * sine_part,
            second_half * cosine + first_half * sine_part,
        ],
        -1,
    )


def rotate_backward(values, cosine, sine_part):
    half_dim = values.shape[-1] // 2
    first_half = values[..., :half_dim]
    second_half = values[..., half_dim:]
    return jnp.concatenate(
        [
            first_half * cosine + second_half * sine_part,
            second_half * cosine - first_half * sine_part,
        ],
        -1,
    )


def over_blocks(visit, carried, members, block_rows):
    piece_rows = members[0].shape[1]
    splits = piece_rows // block_rows
    key_blocks = jnp.swapaxes(
        members[0].reshape(members[0].shape[0], splits, block_rows, members[0].shape[2]), 0, 1
    )
    value_blocks = jnp.swapaxes(
        members[1].reshape(members[1].shape[0], splits, block_rows, members[1].shape[2]), 0, 1
    )
    offsets = jnp.arange(splits, dtype=jnp.int32) * block_rows

    def advance(running, block_item):
        return (visit(running, block_item[0], block_item[1], block_item[2]), None)

    carried, unused = lax.scan(advance, carried, (key_blocks, value_blocks, offsets))
    return carried


def back_pair(
    query_heads,
    grad_heads,
    lse_part,
    delta_part,
    seg_part,
    index_part,
    key_heads,
    value_heads,
    key_start,
    score_scale,
):
    raw = (
        jnp.einsum("rqhd,rkhd->rhqk", query_heads, key_heads, preferred_element_type=jnp.float32)
        * score_scale
    )
    key_index = key_start + jnp.arange(key_heads.shape[1], dtype=jnp.int32)
    valid = (key_index[None, None, :] >= seg_part[:, :, None]) & (
        key_index[None, None, :] <= index_part[None, :, None]
    )
    valid = valid[:, None]
    scores = jnp.where(valid, raw, masked_score)
    weights = jnp.where(valid, jnp.exp(scores - lse_part[..., None]), 0.0)
    value_grad = jnp.einsum(
        "rhqk,rqhd->rkhd",
        weights.astype(jnp.bfloat16),
        grad_heads,
        preferred_element_type=jnp.float32,
    )
    weight_grad = jnp.einsum(
        "rqhd,rkhd->rhqk", grad_heads, value_heads, preferred_element_type=jnp.float32
    )
    score_grad = (weights * (weight_grad - delta_part[..., None])).astype(jnp.bfloat16)
    query_grad = (
        jnp.einsum("rhqk,rkhd->rqhd", score_grad, key_heads, preferred_element_type=jnp.float32)
        * score_scale
    )
    key_grad = (
        jnp.einsum("rhqk,rqhd->rkhd", score_grad, query_heads, preferred_element_type=jnp.float32)
        * score_scale
    )
    return (query_grad, key_grad, value_grad)


def ring_body(tokens, v_first, segments, grad_out, w_qkv, w_out, w_gate_up, w_down, gain_attn, gain_ffn):
    row_count = tokens.shape[1]
    shard_len = tokens.shape[2]
    features = tokens.shape[3]
    head_count = HEADS
    head_dim = HEAD_DIM
    score_scale = head_dim ** (-0.5)
    cycle_size = lax.axis_size("seq")
    device_index = lax.axis_index("seq")
    gathered = (
        lax.all_gather(w_qkv, ("seq", "fsdp"), axis=0, tiled=True),
        lax.all_gather(w_out, ("seq", "fsdp"), axis=0, tiled=True),
        lax.all_gather(w_gate_up, ("seq", "fsdp"), axis=0, tiled=True),
        lax.all_gather(w_down, ("seq", "fsdp"), axis=0, tiled=True),
        lax.all_gather(gain_attn, ("seq", "fsdp"), axis=0, tiled=True),
        lax.all_gather(gain_ffn, ("seq", "fsdp"), axis=0, tiled=True),
    )
    full_qkv, full_out, full_gate_up, full_down, full_gain_attn, full_gain_ffn = gathered
    attn_gain = full_gain_attn.astype(jnp.float32)
    ffn_gain = full_gain_ffn.astype(jnp.float32)
    inputs = tokens.reshape(-1, features).astype(jnp.float32)
    normed_one, inverse_one = rms_forward(inputs, attn_gain)
    normed_one_low = normed_one.astype(jnp.bfloat16)
    projected = jnp.dot(normed_one_low, full_qkv, preferred_element_type=jnp.float32)
    query_index = device_index * shard_len + jnp.arange(shard_len, dtype=jnp.int32)
    seg_rows = segments[0]
    positions = (query_index[None, :] - seg_rows).astype(jnp.float32)
    cosine, sine_part = rotation_tables(positions, head_dim)

    def split_heads(values):
        return values.reshape(row_count, -1, head_count, head_dim)

    queries = rotate_forward(split_heads(projected[:, :features]), cosine, sine_part).astype(
        jnp.bfloat16
    )
    keys_low = (
        rotate_forward(split_heads(projected[:, features : 2 * features]), cosine, sine_part)
        .astype(jnp.bfloat16)
        .reshape(row_count, shard_len, features)
    )
    mixed = (
        (
            0.5 * projected[:, 2 * features :]
            + 0.5 * v_first.reshape(-1, features).astype(jnp.float32)
        )
        .astype(jnp.bfloat16)
        .reshape(row_count, shard_len, features)
    )

    def scores_for(key_heads, key_start):
        raw = (
            jnp.einsum("rqhd,rkhd->rhqk", queries, key_heads, preferred_element_type=jnp.float32)
            * score_scale
        )
        key_index = key_start + jnp.arange(key_heads.shape[1], dtype=jnp.int32)
        valid = (key_index[None, None, :] >= seg_rows[:, :, None]) & (
            key_index[None, None, :] <= query_index[None, :, None]
        )
        valid = valid[:, None]
        return (jnp.where(valid, raw, masked_score), valid)

    def accumulate(carried, key_piece, value_piece, key_start):
        running_max, running_sum, weighted = carried
        key_heads = split_heads(key_piece)
        value_heads = split_heads(value_piece)
        scores, valid = scores_for(key_heads, key_start)
        new_max = jnp.maximum(running_max, jnp.max(scores, -1))
        weights = jnp.where(valid, jnp.exp(scores - new_max[..., None]), 0.0)
        factor = jnp.exp(running_max - new_max)
        running_sum = running_sum * factor + jnp.sum(weights, -1)
        weighted = weighted * jnp.transpose(factor, (0, 2, 1))[..., None] + jnp.einsum(
            "rhqk,rkhd->rqhd",
            weights.astype(jnp.bfloat16),
            value_heads,
            preferred_element_type=jnp.float32,
        )
        return (new_max, running_sum, weighted)

    def visit_forward(carried, key_piece, value_piece, key_start):
        return accumulate(carried, key_piece, value_piece, key_start)

    initial = (
        jnp.full((row_count, head_count, shard_len), masked_score, jnp.float32),
        jnp.zeros((row_count, head_count, shard_len), jnp.float32),
        jnp.zeros((row_count, shard_len, head_count, head_dim), jnp.float32),
    )
    running_max, running_sum, weighted = over_blocks(
        visit_forward,
        initial,
        (
            lax.all_gather(keys_low, "seq", axis=1, tiled=True),
            lax.all_gather(mixed, "seq", axis=1, tiled=True),
        ),
        shard_len,
    )
    attention = weighted / jnp.transpose(running_sum, (0, 2, 1))[..., None]
    log_total = running_max + jnp.log(running_sum)
    attn_low = attention.reshape(-1, features).astype(jnp.bfloat16)
    branch_attn = jnp.dot(attn_low, full_out, preferred_element_type=jnp.float32)
    stream = inputs + branch_attn
    normed_two, inverse_two = rms_forward(stream, ffn_gain)
    normed_two_low = normed_two.astype(jnp.bfloat16)
    gate_up = jnp.dot(normed_two_low, full_gate_up, preferred_element_type=jnp.float32)
    gate = gate_up[:, :FF]
    upward = gate_up[:, FF:]
    sigmoid_gate = jax.nn.sigmoid(gate)
    silu_gate = gate * sigmoid_gate
    hidden_low = (silu_gate * upward).astype(jnp.bfloat16)
    branch_ffn = jnp.dot(hidden_low, full_down, preferred_element_type=jnp.float32)
    output = stream + branch_ffn
    out_tokens = output.astype(jnp.bfloat16).reshape(tokens.shape)
    square_sums = jnp.stack(
        [
            jnp.sum(stream * stream),
            jnp.sum(branch_attn * branch_attn),
            jnp.sum(branch_ffn * branch_ffn),
        ]
    )
    square_totals = lax.psum(square_sums, ("seq", "fsdp"))
    stats = jnp.sqrt(square_totals / (stream.size * lax.axis_size(("seq", "fsdp"))))
    regathered = (
        lax.all_gather(w_qkv, ("seq", "fsdp"), axis=0, tiled=True),
        lax.all_gather(w_out, ("seq", "fsdp"), axis=0, tiled=True),
        lax.all_gather(w_gate_up, ("seq", "fsdp"), axis=0, tiled=True),
        lax.all_gather(w_down, ("seq", "fsdp"), axis=0, tiled=True),
        lax.all_gather(gain_attn, ("seq", "fsdp"), axis=0, tiled=True),
        lax.all_gather(gain_ffn, ("seq", "fsdp"), axis=0, tiled=True),
    )
    full_qkv, full_out, full_gate_up, full_down, full_gain_attn, full_gain_ffn = regathered
    attn_gain = full_gain_attn.astype(jnp.float32)
    ffn_gain = full_gain_ffn.astype(jnp.float32)
    ffn_grad_low = grad_out.reshape(-1, features)
    out_grad = ffn_grad_low.astype(jnp.float32)
    down_grad = jnp.dot(hidden_low.T, ffn_grad_low, preferred_element_type=jnp.float32)
    hidden_grad = jnp.dot(ffn_grad_low, full_down.T, preferred_element_type=jnp.float32)
    gate_grad = hidden_grad * upward * sigmoid_gate * (1.0 + gate * (1.0 - sigmoid_gate))
    upward_grad = hidden_grad * silu_gate
    gate_up_grad_low = jnp.concatenate([gate_grad, upward_grad], -1).astype(jnp.bfloat16)
    gate_up_weight_grad = jnp.dot(
        normed_two_low.T, gate_up_grad_low, preferred_element_type=jnp.float32
    )
    normed_two_grad = jnp.dot(gate_up_grad_low, full_gate_up.T, preferred_element_type=jnp.float32)
    stream_norm_grad, ffn_gain_grad = rms_backward(stream, inverse_two, ffn_gain, normed_two_grad)
    stream_grad = out_grad + stream_norm_grad
    attn_grad_low = stream_grad.astype(jnp.bfloat16)
    out_weight_grad = jnp.dot(attn_low.T, attn_grad_low, preferred_element_type=jnp.float32)
    attention_grad = (
        jnp.dot(attn_grad_low, full_out.T, preferred_element_type=jnp.float32)
        .astype(jnp.bfloat16)
        .reshape(row_count, shard_len, head_count, head_dim)
    )
    row_delta = jnp.einsum("rqhd,rqhd->rhq", attention_grad.astype(jnp.float32), attention)

    def back_visit(partials, query_part, key_heads, value_heads, key_start):
        query_heads, grad_heads, lse_part, delta_part, seg_part, index_part = query_part
        query_term, key_term, value_term = back_pair(
            query_heads,
            grad_heads,
            lse_part,
            delta_part,
            seg_part,
            index_part,
            key_heads,
            value_heads,
            key_start,
            score_scale,
        )
        return (
            partials[0] + query_term,
            partials[1] + key_term.reshape(partials[1].shape),
            partials[2] + value_term.reshape(partials[2].shape),
        )

    zero_rows = jnp.zeros((row_count, shard_len, features), jnp.float32)

    def back_turn(turn_index, running):
        key_piece, value_piece, key_grad, value_grad, query_grad = running
        source = (device_index - turn_index) % cycle_size
        query_grad, key_grad, value_grad = back_visit(
            (query_grad, key_grad, value_grad),
            (queries, attention_grad, log_total, row_delta, seg_rows, query_index),
            split_heads(key_piece),
            split_heads(value_piece),
            source * shard_len,
        )
        key_piece, value_piece = from_behind((key_piece, value_piece), "seq", 1)
        key_grad, value_grad = (
            shifted(key_grad.astype(jnp.bfloat16), "seq", 1).astype(key_grad.dtype),
            shifted(value_grad.astype(jnp.bfloat16), "seq", 1).astype(value_grad.dtype),
        )
        return (key_piece, value_piece, key_grad, value_grad, query_grad)

    start_state = (
        keys_low,
        mixed,
        zero_rows,
        zero_rows,
        jnp.zeros((row_count, shard_len, head_count, head_dim), jnp.float32),
    )
    final_state = lax.fori_loop(0, cycle_size, back_turn, start_state)
    key_grad_home = final_state[2]
    value_grad_home = final_state[3]
    query_grad_home = final_state[4]
    query_grad_rows = rotate_backward(query_grad_home, cosine, sine_part).reshape(-1, features)
    key_grad_rows = rotate_backward(split_heads(key_grad_home), cosine, sine_part).reshape(
        -1, features
    )
    mixed_grad = 0.5 * value_grad_home.reshape(-1, features)
    qkv_grad_low = jnp.concatenate([query_grad_rows, key_grad_rows, mixed_grad], -1).astype(
        jnp.bfloat16
    )
    qkv_weight_grad = jnp.dot(normed_one_low.T, qkv_grad_low, preferred_element_type=jnp.float32)
    normed_one_grad = jnp.dot(qkv_grad_low, full_qkv.T, preferred_element_type=jnp.float32)
    input_norm_grad, attn_gain_grad = rms_backward(inputs, inverse_one, attn_gain, normed_one_grad)
    input_grad = stream_grad + input_norm_grad
    owned = (
        lax.psum_scatter(qkv_weight_grad, ("seq", "fsdp"), scatter_dimension=0, tiled=True),
        lax.psum_scatter(out_weight_grad, ("seq", "fsdp"), scatter_dimension=0, tiled=True),
        lax.psum_scatter(gate_up_weight_grad, ("seq", "fsdp"), scatter_dimension=0, tiled=True),
        lax.psum_scatter(down_grad, ("seq", "fsdp"), scatter_dimension=0, tiled=True),
        lax.psum_scatter(attn_gain_grad, ("seq", "fsdp"), scatter_dimension=0, tiled=True),
        lax.psum_scatter(ffn_gain_grad, ("seq", "fsdp"), scatter_dimension=0, tiled=True),
    )
    return (
        out_tokens,
        input_grad.reshape(tokens.shape),
        mixed_grad.reshape(tokens.shape),
        owned[0],
        owned[1],
        owned[2],
        owned[3],
        owned[4],
        owned[5],
        stats,
    )


FLIPS = ((0, 0), (0, 1), (1, 0), (1, 1))
LAST = (((1,), (1,)), ((), ()))
FIRST = (((0,), (0,)), ((), ()))
BF16, F32 = jnp.bfloat16, jnp.float32


def hop(value, tag, **flips):
    with jax.named_scope(tag):
        return flip_over(value, **flips)


def swap(value, tag, axes):
    with jax.named_scope(tag):
        return lax.all_to_all(value, axes, 0, 0, tiled=True)


def flip_over(value, **flips):
    axes = tuple(name for name in GRID if flips.get(name, 0))
    sizes = [lax.axis_size(name) for name in axes]
    pairs = []
    for source in itertools.product(*[range(size) for size in sizes]):
        origin, target = 0, 0
        for name, size, place in zip(axes, sizes, source):
            origin = origin * size + place
            target = target * size + (place ^ flips[name])
        pairs.append((origin, target))
    return lax.ppermute(value, axes if len(axes) > 1 else axes[0], pairs)


def ordered(mine, other, place, dim):
    first = jnp.where(place == 0, mine, other)
    second = jnp.where(place == 0, other, mine)
    return jnp.stack([first, second], dim)


def after(value, *earlier):
    return lax.optimization_barrier((value,) + earlier)[0]


def call(kernel, name, out_shape, inputs, scratch=(), flops=0, scalars=1, limit=0):
    def whole(x):
        return pl.BlockSpec(x.shape, lambda _: (0,) * len(x.shape), pipeline_mode=pl.Buffered(1))

    smem = pl.BlockSpec(memory_space=pltpu.SMEM)
    shapes = jax.tree.leaves(out_shape)
    moved = sum(x.size * x.dtype.itemsize for x in list(inputs) + shapes)
    held = sum(math.prod(x.shape) * jnp.dtype(x.dtype).itemsize for x in scratch)
    return pl.pallas_call(
        kernel,
        grid=(1,),
        in_specs=[smem] * scalars + [whole(x) for x in inputs[scalars:]],
        out_specs=jax.tree.map(whole, out_shape),
        out_shape=out_shape,
        scratch_shapes=list(scratch),
        compiler_params=pltpu.CompilerParams(vmem_limit_bytes=limit or moved + held + 8 * 2**20),
        cost_estimate=pl.CostEstimate(flops=flops, bytes_accessed=moved, transcendentals=0),
        name=name,
    )(*inputs)


def like(*shape, dtype=BF16):
    return jax.ShapeDtypeStruct(shape, dtype)


def device_row(a, b, c, f):
    return ((a * 2 + b) * 2 + c) * 2 + f


def rows_at(index, count):
    return pl.ds(pl.multiple_of(index * count, count), count)


def half_swap(values):
    lanes = lax.broadcasted_iota(jnp.int32, values.shape, values.ndim - 1)
    quarter = HEAD_DIM // 2
    width = values.shape[-1]
    ahead = pltpu.roll(values, width - quarter, values.ndim - 1)
    behind = pltpu.roll(values, quarter, values.ndim - 1)
    return jnp.where(lanes % HEAD_DIM < quarter, ahead, behind)


def unit_room(hidden):
    return -(-hidden // 16) * 16


def prepare_kernel(
    place_ref, x_ref, w_ref, seg_ref, g0_ref, g1_ref, v_ref, x_out_ref, out_ref
):
    b, c, f = place_ref[1], place_ref[2], place_ref[3]
    rows = x_ref.shape[1]
    for r in range(2):
        x_out_ref[r * rows : (r + 1) * rows, :] = x_ref[b ^ r]
    held = w_ref.shape[0]
    parts, _, width = out_ref.shape
    features = parts * width
    lanes = lax.broadcasted_iota(jnp.int32, (1, width), 1)
    mine = lanes // held == c * 2 + f
    lines = []
    for ref in (g0_ref, g1_ref):
        gain = jnp.concatenate([ref[...].astype(F32)] * (width // held), 1)
        lines.append(jnp.where(mine, gain, 0.0))
    starts = jnp.concatenate([seg_ref[0:1, :], seg_ref[1:2, :]], 1)
    lines.append((starts >> 8).astype(F32))
    lines.append((starts & 255).astype(F32))
    row = lax.broadcasted_iota(jnp.int32, (16, width), 0)
    small = jnp.zeros((16, width), F32)
    for k, line in enumerate(lines):
        small = jnp.where(row == k, line, small)
    small = small.astype(BF16)
    for p in range(parts):
        for part in range(3):
            start = part * features + p * width
            out_ref[p, part * held : (part + 1) * held, :] = w_ref[:, start : start + width]
        out_ref[p, 3 * held : 3 * held + 16, :] = small
        for r in range(2):
            start = 3 * held + 16 + r * rows
            out_ref[p, start : start + rows, :] = v_ref[b ^ r, :, p * width : (p + 1) * width]


def join_units_kernel(u0_ref, u1_ref, u2_ref, u3_ref, d_ref, out_ref):
    wide = out_ref.shape[1]
    hidden, features = d_ref.shape
    held = out_ref.shape[0] // 6
    fold = held * (wide - features) // features
    for k, ref in enumerate((u0_ref, u1_ref, u2_ref, u3_ref)):
        out_ref[k * held : (k + 1) * held, :features] = ref[:held, :]
        for part in range(features // (wide - features)):
            start = k * held + part * fold
            out_ref[start : start + fold, features:] = ref[
                held : held + fold, part * (wide - features) : (part + 1) * (wide - features)
            ]
    room = unit_room(hidden)
    lead = room * features // wide
    rest = room - lead
    base = 4 * held
    out_ref[base:, :features] = d_ref[:lead, :]
    gap = jnp.zeros((room - hidden, wide - features), BF16)
    for part in range(features // (wide - features)):
        lanes = slice(part * (wide - features), (part + 1) * (wide - features))
        here = slice(base + part * rest, base + (part + 1) * rest)
        out_ref[here, features:] = jnp.concatenate([d_ref[lead:, lanes], gap], 0)


def spread_digits(values):
    row = lax.broadcasted_iota(jnp.int32, values.shape, 0)
    first = values.astype(BF16).astype(F32)
    second = (values - first).astype(BF16).astype(F32)
    third = values - first - second
    picked = jnp.where(row == 0, first, jnp.where(row == 1, second, third))
    return jnp.where(row < 3, picked, 0.0).astype(BF16)


def add_digits(tile):
    return jnp.broadcast_to(jnp.sum(tile.astype(F32), 0, keepdims=True), tile.shape)


def spread_kernel(place_ref, w_ref, g_ref, o0_ref, o1_ref, o2_ref, o3_ref, all_ref):
    half = w_ref.shape[1] // 2
    wide = all_ref.shape[2] // 2
    na = NA
    hidden = half // (8 * na)
    room = unit_room(hidden)
    values = w_ref[...]
    gap = jnp.zeros((values.shape[0], room - hidden), values.dtype)
    for b, f in FLIPS:
        for side in range(2):
            parts = []
            for a, c in itertools.product(range(na), range(2)):
                start = side * half + hidden * device_row(a, b, c, f)
                parts += [values[:, start : start + hidden], gap]
            if wide > 2 * na * room:
                parts.append(jnp.zeros((values.shape[0], wide - 2 * na * room), values.dtype))
            all_ref[b * 2 + f, :, side * wide : (side + 1) * wide] = jnp.concatenate(parts, 1)
    held, features = w_ref.shape[0], g_ref.shape[1]
    rest = 2 * wide - features
    fold = held * rest // features
    for (i, j), ref in zip(FLIPS, (o0_ref, o1_ref, o2_ref, o3_ref)):
        block = all_ref[(place_ref[1] ^ i) * 2 + (place_ref[3] ^ j)]
        ref[:held, :] = block[:, :features]
        for part in range(features // rest):
            rows = block[part * fold : (part + 1) * fold, features:]
            ref[held : held + fold, part * rest : (part + 1) * rest] = rows
        ref[held + fold :, :] = g_ref[...]


def gather_units_kernel(
    place_ref, p0, p1, p2, p3, d_ref, w_ref, gain_ref,
    out_ref, gain_grad_ref, down_ref, outs_ref, part_ref,
):
    hidden, features = down_ref.shape
    room = unit_room(hidden)
    lead = d_ref.shape[0]
    rest = room - lead
    down_ref[:lead, :] = d_ref[:, :features].astype(F32)
    size = d_ref.shape[1] - features
    for part in range(features // size):
        block = d_ref[part * rest : (part + 1) * rest, features:].astype(F32)
        down_ref[lead:, part * size : (part + 1) * size] = block[: hidden - lead, :]
    b, f = place_ref[1], place_ref[3]
    columns = part_ref.shape[2]
    total = 0.0
    for (i, j), ref in zip(FLIPS, (p0, p1, p2, p3)):
        part_ref[(b ^ i) * 2 + (f ^ j)] = ref[:, :columns]
        total = total + ref[:, columns:].astype(F32)
    outs_ref[...] = total
    half = w_ref.shape[1] // 2
    wide = part_ref.shape[2] // 2
    na = NA
    hidden = half // (8 * na)
    room = unit_room(hidden)
    total = 0.0
    for side in range(2):
        parts = []
        for a, b, c, f in itertools.product(range(na), range(2), range(2), range(2)):
            start = side * wide + room * (a * 2 + c)
            parts.append(part_ref[b * 2 + f][:, start : start + hidden].astype(F32))
        grad = jnp.concatenate(parts, 1)
        out_ref[:, side * half : (side + 1) * half] = grad
        weights = w_ref[:, side * half : (side + 1) * half].astype(F32)
        total = total + jnp.sum(weights * grad, -1, keepdims=True)
    gain_grad_ref[...] = total / gain_ref[...]


def assemble(place_ref, p0_ref, p1_ref, p2_ref, p3_ref, w_ref, gain_ref):
    b, f = place_ref[1], place_ref[3]
    groups, _, width = p0_ref.shape
    held = w_ref.shape[0] // (4 * groups)
    pieces = (p0_ref, p1_ref, p2_ref, p3_ref)
    for (i, j), ref in zip(FLIPS, pieces):
        for a, c in itertools.product(range(groups // 2), range(2)):
            rows = rows_at(device_row(a, b ^ i, c, f ^ j), held)
            for part in range(3):
                w_ref[rows, part * width : (part + 1) * width] = ref[
                    a * 2 + c, part * held : (part + 1) * held, :
                ]
    for i in range(2):
        for a in range(groups // 2):
            total = 0.0
            for j, c in itertools.product(range(2), range(2)):
                total = total + pieces[i * 2 + j][a * 2 + c, 3 * held :, :].astype(F32)
            lanes = pl.ds(pl.multiple_of((a * 2 + (b ^ i)) * width, width), width)
            gain_ref[:, lanes] = total[:8]


def project_kernel(
    place_ref, x_ref, first_ref, w_ref, gain_ref, cos_ref, sin_ref, n_ref, keep_ref, send_ref
):
    project_block(x_ref, first_ref, w_ref, gain_ref, cos_ref, sin_ref, n_ref, keep_ref, send_ref)


def project_first_kernel(
    place_ref, x_ref, first_ref, p0_ref, p1_ref, p2_ref, p3_ref, cos_ref, sin_ref,
    n_ref, keep_ref, send_ref, w_ref, gain_ref,
):
    @pl.when(pl.program_id(0) == 0)
    def _():
        assemble(place_ref, p0_ref, p1_ref, p2_ref, p3_ref, w_ref, gain_ref)

    project_block(x_ref, first_ref, w_ref, gain_ref, cos_ref, sin_ref, n_ref, keep_ref, send_ref)


def project_block(
    x_ref, first_ref, w_ref, gain_ref, cos_ref, sin_ref, n_ref, keep_ref, send_ref
):
    width = w_ref.shape[1] // 3
    rows = x_ref.shape[1] // 2
    values = x_ref[0].astype(F32)
    inverse = lax.rsqrt(jnp.mean(values * values, -1, keepdims=True) + epsilon)
    normed = (values * inverse * gain_ref[0:1, :]).astype(BF16)
    n_ref[0] = normed
    projected = jnp.dot(normed, w_ref[...], preferred_element_type=F32)
    cosine = cos_ref[0, 0]
    sine = sin_ref[0, 0]
    for part in range(2):
        block = projected[:, part * width : (part + 1) * width]
        turned = (block * cosine + half_swap(block) * sine).astype(BF16)
        keep_ref[0, :, part * width : (part + 1) * width] = turned[:rows]
        send_ref[0, :, part * width : (part + 1) * width] = turned[rows:]
    values = (0.5 * projected[:, 2 * width :] + 0.5 * first_ref[0].astype(F32)).astype(BF16)
    keep_ref[0, :, 2 * width :] = values[:rows]
    send_ref[0, :, 2 * width :] = values[rows:]


def project(places, flip, x, first_values, weights, cosine, sine):
    count, rows, features = x.shape
    third = cosine.shape[3]
    wide = 3 * third

    def by_step(*block):
        return pl.BlockSpec((1,) + block, lambda step, place: (step, 0, 0))

    def first_map(step, place):
        return ((step ^ place[0]) * 2 + (place[2] ^ flip), 0, 0)

    def table_map(step, place):
        return (step ^ place[0], place[2] ^ flip, 0, 0)

    def fixed(*block):
        return pl.BlockSpec(block, lambda step, place: (0,) * len(block))

    table = pl.BlockSpec((1, 1, rows, third), table_map)
    first = len(weights) > 2
    shapes = [
        like(count, rows, features),
        like(count, rows // 2, wide),
        like(count, rows // 2, wide),
    ]
    specs = [by_step(rows, features), by_step(rows // 2, wide), by_step(rows // 2, wide)]
    if first:
        shapes += [like(features, wide), like(8, features, dtype=F32)]
        specs += [fixed(features, wide), fixed(8, features)]
    return pl.pallas_call(
        project_first_kernel if first else project_kernel,
        grid_spec=pltpu.PrefetchScalarGridSpec(
            num_scalar_prefetch=1,
            grid=(count,),
            in_specs=[
                by_step(rows, features),
                pl.BlockSpec((1, rows, third), first_map),
                *[fixed(*weight.shape) for weight in weights],
                table,
                table,
            ],
            out_specs=specs,
        ),
        out_shape=shapes,
        compiler_params=pltpu.CompilerParams(
            vmem_limit_bytes=16 * 2**20 if first else 8 * 2**20
        ),
        cost_estimate=pl.CostEstimate(
            flops=2 * count * rows * features * wide,
            bytes_accessed=count * rows * features * 4 + features * wide * 2,
            transcendentals=count * rows,
        ),
        name="project_first" if first else "project",
    )(places, x, first_values, *weights, cosine, sine)


def block_scores(head, query, keys, seg, start, scale):
    lanes = lax.broadcasted_iota(jnp.int32, query.shape, 1)
    masked = jnp.where(lanes // HEAD_DIM == head, query, jnp.zeros_like(query))
    raw = lax.dot_general(masked, keys, LAST, preferred_element_type=F32) * scale
    row = start + lax.broadcasted_iota(jnp.int32, raw.shape, 0)
    column = lax.broadcasted_iota(jnp.int32, raw.shape, 1)
    valid = (column >= seg) & (column <= row)
    scores = jnp.where(valid, raw, masked_score)
    top = jnp.max(scores, -1, keepdims=True)
    weights = jnp.exp(scores - top)
    total = jnp.sum(weights, -1, keepdims=True)
    return masked, weights * (1.0 / total)


def row_block(place_ref, step, b_flip, c_flip):
    a, b, c = place_ref[0] ^ step, place_ref[1] ^ b_flip, place_ref[2] ^ c_flip
    return (a * 2 + b) * 2 + c


def attend_kernel(
    place_ref, k0_ref, k1_ref, r0_ref, r1_ref, seg_ref, o_ref, all_ref
):
    count, rows, wide = k0_ref.shape
    width = wide // 3
    length = all_ref.shape[0]
    for (b_flip, c_flip), ref in zip(FLIPS, (k0_ref, k1_ref, r0_ref, r1_ref)):
        for step in range(count):
            all_ref[rows_at(row_block(place_ref, step, b_flip, c_flip), rows), :] = ref[step]
    size = min(256, length)
    scale = HEAD_DIM ** (-0.5)
    for start in range(0, length, size):
        stop = start + size
        query = all_ref[start:stop, :width]
        keys = all_ref[:stop, width : 2 * width]
        values = all_ref[:stop, 2 * width :]
        seg = seg_ref[start:stop, :]

        def one(head):
            _, weights = block_scores(head, query, keys, seg, start, scale)
            return jnp.dot(weights.astype(BF16), values, preferred_element_type=F32)

        lanes = lax.broadcasted_iota(jnp.int32, (size, width), 1)
        result = one(0)
        for head in range(1, width // HEAD_DIM):
            result = jnp.where(lanes // HEAD_DIM == head, one(head), result)
        o_ref[start:stop, :] = result.astype(BF16)


def attend_back_kernel(
    place_ref, all_ref, seg_ref, do_ref, cos_ref, sin_ref, k_ref, r_ref, dk_ref, dv_ref, full_ref
):
    _, count, rows, wide = k_ref.shape
    width = wide // 3
    length = all_ref.shape[0]
    size = min(256, length)
    scale = HEAD_DIM ** (-0.5)
    dk_ref[...] = jnp.zeros_like(dk_ref)
    dv_ref[...] = jnp.zeros_like(dv_ref)
    for start in range(0, length, size):
        stop = start + size
        query = all_ref[start:stop, :width]
        keys = all_ref[:stop, width : 2 * width]
        values = all_ref[:stop, 2 * width :]
        seg = seg_ref[start:stop, :]
        out_grad = do_ref[start:stop, :]
        lanes = lax.broadcasted_iota(jnp.int32, (size, width), 1)

        def one(head):
            masked, weights = block_scores(head, query, keys, seg, start, scale)
            grad = jnp.where(lanes // HEAD_DIM == head, out_grad, jnp.zeros_like(out_grad))
            weight_grad = lax.dot_general(grad, values, LAST, preferred_element_type=F32)
            delta = jnp.sum(weights * weight_grad, -1, keepdims=True)
            score_grad = (weights * (weight_grad - delta)).astype(BF16)
            dv_ref[:stop, :] += lax.dot_general(
                weights.astype(BF16), grad, FIRST, preferred_element_type=F32
            )
            dk_ref[:stop, :] += lax.dot_general(
                score_grad, masked, FIRST, preferred_element_type=F32
            )
            return jnp.dot(score_grad, keys, preferred_element_type=F32)

        query_grad = one(0)
        for head in range(1, width // HEAD_DIM):
            query_grad = jnp.where(lanes // HEAD_DIM == head, one(head), query_grad)
        query_grad = query_grad * scale
        cosine = cos_ref[start:stop, :]
        sine = sin_ref[start:stop, :]
        full_ref[start:stop, :width] = (
            query_grad * cosine - half_swap(query_grad) * sine
        ).astype(BF16)
    for start in range(0, length, size):
        stop = start + size
        key_grad = dk_ref[start:stop, :] * scale
        cosine = cos_ref[start:stop, :]
        sine = sin_ref[start:stop, :]
        full_ref[start:stop, width : 2 * width] = (
            key_grad * cosine - half_swap(key_grad) * sine
        ).astype(BF16)
        full_ref[start:stop, 2 * width :] = (0.5 * dv_ref[start:stop, :]).astype(BF16)
    for b_flip, c_flip in FLIPS:
        ref = (k_ref, r_ref)[b_flip]
        for step in range(count):
            ref[c_flip, step] = full_ref[
                rows_at(row_block(place_ref, step, b_flip, c_flip), rows), :
            ]


def assemble_out(place_ref, own_ref, other_ref, w_ref):
    a, b, c, f = [place_ref[k] for k in range(4)]
    na = own_ref.shape[1]
    held = other_ref.shape[2]
    for k, (i, j) in enumerate(FLIPS):
        for step in range(na):
            for c_flip, ref in enumerate((own_ref, other_ref)):
                row = device_row(a ^ step, b ^ i, c ^ c_flip, f ^ j)
                w_ref[rows_at(row, held), :] = ref[k, step]


def out_kernel(
    place_ref, heads_ref, own_ref, other_ref, x_ref, gain_ref,
    o_ref, h_ref, n_ref, sum_ref, w_ref,
):
    rows, width = heads_ref.shape[1:]
    assemble_out(place_ref, own_ref, other_ref, w_ref)
    for p in range(o_ref.shape[1] // width):
        for r in range(2):
            o_ref[r * rows : (r + 1) * rows, p * width : (p + 1) * width] = heads_ref[
                ((p // 2) * 2 + r) * 2 + p % 2
            ]
    branch = jnp.dot(o_ref[...], w_ref[...], preferred_element_type=F32)
    stream = x_ref[...].astype(F32) + branch
    h_ref[...] = stream
    inverse = lax.rsqrt(jnp.mean(stream * stream, -1, keepdims=True) + epsilon)
    n_ref[...] = (stream * inverse * gain_ref[1:2, :]).astype(BF16)
    sum_ref[0:1, :] = jnp.sum(stream * stream, 0, keepdims=True)
    sum_ref[1:2, :] = jnp.sum(branch * branch, 0, keepdims=True)


def feed_kernel(
    place_ref, n0, n1, n2, n3, g0, g1, g2, g3, w_ref,
    act_ref, dgu_ref, b0_ref, b1_ref, b2_ref, b3_ref, down_ref, n_ref, g_ref, full_ref,
):
    a, b, c, f = [place_ref[k] for k in range(4)]
    na, wide = w_ref.shape[0] // 2, w_ref.shape[2]
    padded, features = down_ref.shape
    held = features // (8 * na)
    rows = n0.shape[0]
    room = padded // (2 * na)
    lead = room * features // wide
    rest = room - lead
    for s, (da, dc) in enumerate(itertools.product(range(na), range(2))):
        for k, (i, j) in enumerate(FLIPS):
            row = device_row(da, b ^ i, dc, f ^ j)
            full_ref[rows_at(row, held), :] = w_ref[s, k * held : (k + 1) * held, :]
        base = 4 * held
        start = s * room
        down_ref[start : start + lead, :] = w_ref[s, base:, :features]
        for part in range(features // (wide - features)):
            lanes = slice(part * (wide - features), (part + 1) * (wide - features))
            here = slice(base + part * rest, base + (part + 1) * rest)
            down_ref[start + lead : start + room, lanes] = w_ref[s, here, features:]
    for k, (n_part, g_part) in enumerate(zip((n0, n1, n2, n3), (g0, g1, g2, g3))):
        n_ref[k * rows : (k + 1) * rows, :] = n_part[...]
        g_ref[k * rows : (k + 1) * rows, :] = g_part[g_part.shape[0] - rows :, :]
    size = 256
    for start in range(0, padded, size):
        here = slice(start, start + size)
        there = slice(padded + start, padded + start + size)
        gate = jnp.dot(n_ref[...], full_ref[:, here], preferred_element_type=F32)
        upward = jnp.dot(n_ref[...], full_ref[:, there], preferred_element_type=F32)
        act_grad = lax.dot_general(g_ref[...], down_ref[here, :], LAST, preferred_element_type=F32)
        sigmoid_gate = jax.nn.sigmoid(gate)
        silu_gate = gate * sigmoid_gate
        act_ref[:, here] = (silu_gate * upward).astype(BF16)
        dgu_ref[:, here] = (
            act_grad * upward * sigmoid_gate * (1.0 + gate * (1.0 - sigmoid_gate))
        ).astype(BF16)
        dgu_ref[:, there] = (act_grad * silu_gate).astype(BF16)
    for k in range(4):
        back = lax.dot_general(
            dgu_ref[k * rows : (k + 1) * rows, :], full_ref[...], LAST, preferred_element_type=F32
        )
        ref = (b0_ref, b1_ref, b2_ref, b3_ref)[k]
        ref[...] = back.astype(ref.dtype)


def feed_grads_kernel(
    place_ref, n0, n1, n2, n3, g0, g1, g2, g3, act_ref, dgu_ref,
    own_ref, send_ref, n_ref, g_ref, out_ref,
):
    b, c, f = place_ref[1], place_ref[2], place_ref[3]
    rows = n0.shape[0]
    for k, (n_part, g_part) in enumerate(zip((n0, n1, n2, n3), (g0, g1, g2, g3))):
        n_ref[k * rows : (k + 1) * rows, :] = n_part[...]
        g_ref[k * rows : (k + 1) * rows, :] = g_part[g_part.shape[0] - rows :, :]
    groups, _, wide = out_ref.shape
    padded, features = act_ref.shape[1], g_ref.shape[1]
    held = features // (4 * groups)
    room = padded // groups
    size = 512
    for start in range(0, wide, size):
        here = slice(start, start + size)
        grad = lax.dot_general(
            n_ref[...], dgu_ref[:, here], FIRST, preferred_element_type=F32
        ).astype(BF16)
        for s, (da, dc) in enumerate(itertools.product(range(groups // 2), range(2))):
            for db, df in FLIPS:
                row = device_row(da, db, dc, df) * held
                k = (b ^ db) * 2 + (f ^ df)
                out_ref[s, rows_at(k, held), here] = grad[row : row + held, :]
    grad = lax.dot_general(act_ref[...], g_ref[...], FIRST, preferred_element_type=F32).astype(BF16)
    lead = room * features // wide
    rest = room - lead
    base = 4 * held
    for s in range(groups):
        block = grad[room * s : room * (s + 1), :]
        out_ref[s, base:, :features] = block[:lead, :]
        for part in range(features // (wide - features)):
            lanes = slice(part * (wide - features), (part + 1) * (wide - features))
            there = slice(base + part * rest, base + (part + 1) * rest)
            out_ref[s, there, features:] = block[lead:, lanes]
    for a in range(groups // 2):
        own_ref[a] = out_ref[a * 2 + c]
        send_ref[a] = out_ref[a * 2 + (1 - c)]


def feed_branch_kernel(act_ref, down_ref, f0_ref, f1_ref, f2_ref, f3_ref):
    rows = f0_ref.shape[0]
    for k, ref in enumerate((f0_ref, f1_ref, f2_ref, f3_ref)):
        ffn = jnp.dot(
            act_ref[k * rows : (k + 1) * rows, :], down_ref[...], preferred_element_type=F32
        )
        ref[...] = ffn.astype(ref.dtype)


def norm_back(values, gain, normed_grad):
    inverse = lax.rsqrt(jnp.mean(values * values, -1, keepdims=True) + epsilon)
    scaled = normed_grad * gain
    return inverse * scaled - values * (inverse * inverse * inverse) * jnp.mean(
        scaled * values, -1, keepdims=True
    )


def stream_back_kernel(
    place_ref, p0, p1, p2, p3, h_ref, gain_ref, g_ref, w0_ref, w1_ref, o_ref,
    dh_ref, do_ref, own_ref, send_ref, out_ref, w_ref,
):
    assemble_out(place_ref, w0_ref, w1_ref, w_ref)
    normed_grad = p0[...] + p1[...].astype(F32) + p2[...].astype(F32) + p3[...].astype(F32)
    stream = h_ref[...]
    stream_grad = g_ref[...].astype(F32) + norm_back(stream, gain_ref[1:2, :], normed_grad)
    dh_ref[...] = stream_grad
    low = stream_grad.astype(BF16)
    heads = lax.dot_general(low, w_ref[...], LAST, preferred_element_type=F32).astype(BF16)
    rows, width = do_ref.shape[1:]
    for p in range(heads.shape[1] // width):
        for r in range(2):
            do_ref[((p // 2) * 2 + r) * 2 + p % 2] = heads[
                r * rows : (r + 1) * rows, p * width : (p + 1) * width
            ]
    total = lax.dot_general(o_ref[...], low, FIRST, preferred_element_type=F32).astype(BF16)
    b, f = place_ref[1], place_ref[3]
    groups = out_ref.shape[0]
    held = out_ref.shape[1] // 4
    for s, (da, dc) in enumerate(itertools.product(range(groups // 2), range(2))):
        for db, df in FLIPS:
            row = device_row(da, db, dc, df) * held
            k = (b ^ db) * 2 + (f ^ df)
            out_ref[s, rows_at(k, held), :] = total[row : row + held, :]
    c = place_ref[2]
    for a in range(groups // 2):
        own_ref[a] = out_ref[a * 2 + c]
        send_ref[a] = out_ref[a * 2 + (1 - c)]


def fill_pairs(d_ref, keep_ref, recv_ref, flip):
    _, count, rows, _ = keep_ref.shape
    for step in range(count):
        base = 2 * rows * step
        d_ref[base : base + rows, :] = keep_ref[flip, step]
        d_ref[base + rows : base + 2 * rows, :] = recv_ref[flip, step]


def unproject_other_kernel(keep_ref, recv_ref, w_ref, dn_ref, d_ref):
    fill_pairs(d_ref, keep_ref, recv_ref, 1)
    count, rows, _ = dn_ref.shape
    for step in range(count):
        back = lax.dot_general(
            d_ref[rows * step : rows * (step + 1), :], w_ref[...], LAST, preferred_element_type=F32
        )
        dn_ref[step] = back.astype(BF16)


def unproject_own_kernel(
    keep_ref, recv_ref, w_ref, other_ref, own_ref, s1_ref, s2_ref, s3_ref, d_ref
):
    fill_pairs(d_ref, keep_ref, recv_ref, 0)
    count, rows, _ = other_ref.shape
    for step in range(count):
        back = lax.dot_general(
            d_ref[rows * step : rows * (step + 1), :], w_ref[...], LAST, preferred_element_type=F32
        )
        back = back + other_ref[step].astype(F32)
        if step == 0:
            own_ref[...] = back
        else:
            (s1_ref, s2_ref, s3_ref)[step - 1][...] = back.astype(BF16)


def qkv_grads_kernel(
    place_ref, k_ref, r_ref, n0_ref, n1_ref, stat_ref,
    own_ref, send_ref, d_ref, total_ref,
):
    b, f = place_ref[1], place_ref[3]
    _, count, rows, wide = k_ref.shape
    width = wide // 3
    features = n0_ref.shape[2]
    for flip, n_ref in enumerate((n0_ref, n1_ref)):
        fill_pairs(d_ref, k_ref, r_ref, flip)
        tokens = n_ref[...].reshape(2 * rows * count, features)
        grad = lax.dot_general(tokens, d_ref[...], FIRST, preferred_element_type=F32)
        if flip == 0:
            total_ref[...] = grad
        else:
            total_ref[...] += grad
    held = features // (8 * count)
    block = 3 * held
    bottom = block * 2 * count
    own_ref[bottom:, :] = stat_ref[...]
    for k in range(3):
        send_ref[k, bottom:, :] = spread_digits(stat_ref[...])
    for k, (i, j) in enumerate(FLIPS):
        for s, (da, dc) in enumerate(itertools.product(range(count), range(2))):
            piece = total_ref[rows_at(device_row(da, b ^ i, dc, f ^ j), held), :]
            for part in range(3):
                lanes = piece[:, part * width : (part + 1) * width]
                there = slice(s * block + part * held, s * block + (part + 1) * held)
                if k == 0:
                    own_ref[there, :] = lanes
                else:
                    send_ref[k - 1, there, :] = lanes.astype(BF16)


def qkv_sum_kernel(
    place_ref, own_ref, r1_ref, r2_ref, r3_ref, kept_ref, moved_ref, out_ref
):
    a, c = place_ref[0], place_ref[2]
    parts, rows, width = out_ref.shape
    _, count, length, _ = kept_ref.shape
    block = rows - 16 - 2 * length
    bottom = parts * block
    received = (r1_ref, r2_ref, r3_ref)
    stats = own_ref[bottom:, :]
    for ref in received:
        stats = stats + add_digits(ref[bottom:, :])
    digits = spread_digits(stats)
    for p in range(parts):
        here = slice(p * block, (p + 1) * block)
        total = own_ref[here, :]
        for ref in received:
            total = total + ref[here, :].astype(F32)
        out_ref[p, :block, :] = total.astype(BF16)
        out_ref[p, block : block + 16, :] = digits
    base = block + 16
    for c_flip in range(2):
        for step in range(count):
            p = (a ^ step) * 2 + (c ^ c_flip)
            for r, ref in enumerate((kept_ref, moved_ref)):
                there = slice(base + r * length, base + (r + 1) * length)
                out_ref[p, there, :] = ref[c_flip, step, :, 2 * width :]


def join_grads_kernel(units_ref, outs_ref, out_ref):
    held = out_ref.shape[1]
    wide = units_ref.shape[1]
    for k in range(4):
        here = slice(k * held, (k + 1) * held)
        out_ref[k, :, :wide] = units_ref[here, :]
        out_ref[k, :, wide:] = outs_ref[here, :]


def finish_out_kernel(h_ref, ffn_ref, r1_ref, r2_ref, r3_ref, sum_ref, out_ref, total_ref):
    branch = ffn_ref[...]
    for ref in (r1_ref, r2_ref, r3_ref):
        branch = branch + ref[...].astype(F32)
    out_ref[...] = (h_ref[...] + branch).astype(BF16)
    squares = jnp.sum(branch * branch, 0, keepdims=True)
    lanes = lax.broadcasted_iota(jnp.int32, total_ref.shape, 1)
    totals = jnp.zeros(total_ref.shape, F32)
    for k in range(3):
        values = squares if k == 2 else sum_ref[k : k + 1, :]
        totals = jnp.where(lanes == k, jnp.sum(values, -1, keepdims=True), totals)
    total_ref[...] = totals


def finish_kernel(
    entries, place_ref, part_ref, w_ref, gain_ref, out_ref, gain_grad_ref, stat_ref, first_ref
):
    parts, _, width = part_ref.shape
    base = 3 * out_ref.shape[0]
    rows = first_ref.shape[1]
    stats = 0.0
    for p in range(parts):
        stats = stats + add_digits(part_ref[p, base : base + 16, :])
        for r in range(2):
            start = base + 16 + r * rows
            first_ref[place_ref[1] ^ r, :, p * width : (p + 1) * width] = part_ref[
                p, start : start + rows, :
            ].astype(F32)
    stat_ref[...] = jnp.sqrt(stats[:8] / entries)
    held = out_ref.shape[0]
    features = parts * width
    total = 0.0
    for part in range(3):
        for p in range(parts):
            grad = part_ref[p, part * held : (part + 1) * held, :].astype(F32)
            lanes = slice(part * features + p * width, part * features + (p + 1) * width)
            out_ref[:, lanes] = grad
            total = total + jnp.sum(w_ref[:, lanes].astype(F32) * grad, -1, keepdims=True)
    gain_grad_ref[...] = total / gain_ref[...]


def tokens_back_kernel(place_ref, p0, p1, p2, p3, x_ref, gain_ref, dh_ref, out_ref):
    b = place_ref[1]
    rows = out_ref.shape[1]
    for r in range(2):
        here = slice(r * rows, (r + 1) * rows)
        normed_grad = (
            p0[here, :] + p1[here, :].astype(F32) + p2[here, :].astype(F32) + p3[here, :].astype(F32)
        )
        row = b ^ r
        values = x_ref[row].astype(F32)
        out_ref[row] = dh_ref[row] + norm_back(values, gain_ref[0:1, :], normed_grad)


def turn_tables(positions, width):
    quarter = HEAD_DIM // 2
    freqs = jnp.power(10000.0, -jnp.arange(quarter, dtype=F32) / quarter)
    freqs = jnp.tile(freqs, width // quarter)
    signs = jnp.where(jnp.arange(width) % HEAD_DIM < quarter, -1.0, 1.0)
    angles = positions.astype(F32)[..., None] * freqs
    return jnp.cos(angles), jnp.sin(angles) * signs


def grid_body(tokens, v_first, segments, grad_out, w_qkv, w_out, w_gate_up, w_down, gain_attn, gain_ffn):
    row_count, shard_len, features = tokens.shape[1:]
    a, b, c, f = [lax.axis_index(name) for name in GRID]
    na = lax.axis_size("a")
    nd = 8 * na
    width = features // (2 * na)
    held = features // nd
    hidden = w_down.shape[0]
    room = unit_room(hidden)
    padded = 2 * na * room
    wide = 2 * padded
    length = 4 * na * shard_len
    count = row_count * shard_len
    places = jnp.stack([a, b, c, f]).astype(jnp.int32)
    a_steps = range(1, na)

    def plane_hops(pieces, tag):
        return [hop(piece, tag, b=i, f=j) for piece, (i, j) in zip(pieces, FLIPS[1:])]

    def a_hops(value, tag):
        return [value] + [hop(value, tag, a=step) for step in a_steps]

    mine = tokens[0]
    parts = a_hops(w_out, "out_a")
    turned, sent = call(
        prepare_kernel,
        "prepare",
        [like(count, features), like(2 * na, 3 * held + 16 + count, width)],
        [places, after(mine, *parts), w_qkv, segments[0], gain_attn[None], gain_ffn[None], v_first[0]],
        limit=60 * 2**20,
    )

    token_parts = a_hops(turned, "tokens_a")
    sent = swap(sent, "qkv_ac", ("a", "c"))
    grads = grad_out.reshape(count, features)
    tall = held * wide // features + count
    plane = call(
        spread_kernel,
        "spread",
        [like(tall, features)] * 4,
        [places, w_gate_up, grads],
        scratch=[pltpu.VMEM((4, held, wide), BF16)],
        limit=60 * 2**20,
    )
    plane = lax.optimization_barrier((*plane, turned))[:4]
    plane = [plane[0]] + plane_hops(plane[1:], "units_bf")
    units = call(
        join_units_kernel, "join_units", like(6 * held, wide), [*plane, w_down], scalars=0
    )
    first = sent[:, 3 * held + 16 :]
    sent = sent[:, : 3 * held + 16]
    near = sent
    sent = after(sent, *token_parts[1:], units)
    pieces = [sent] + plane_hops([sent] * 3, "qkv_bf")
    sent = after(*pieces)
    units = lax.all_gather(after(units, sent), ("a", "c"), axis=0, tiled=False)

    group_tokens = jnp.stack(token_parts)
    other_tokens = hop(group_tokens, "tokens_c", c=1)
    def pick(array, index, dim):
        return lax.dynamic_index_in_dim(array, index, dim, keepdims=False)

    def starts_of(small):
        digits = small[..., 3 * held + 2 : 3 * held + 4, :].astype(jnp.int32)
        digits = digits[..., 0, :] * 256 + digits[..., 1, :]
        return digits.reshape(na, 2, row_count, shard_len)

    group_starts = starts_of(near)
    all_starts = ordered(group_starts, starts_of(pieces[2]), b, 1)
    group_starts = jnp.where(b == 0, group_starts, group_starts[:, :, ::-1])
    order = jnp.arange(2 * na, dtype=jnp.int32).reshape(na, 2, 1, 1)
    offset = jnp.arange(shard_len, dtype=jnp.int32)
    block = (order // 2 * 2 + b) * 2 + order % 2
    positions = block * shard_len + offset - group_starts
    cosine, sine = turn_tables(positions.reshape(na, 2, count), width)
    n_part, keep, send, *qkv = project(
        places, 0, group_tokens, first, [sent, *pieces[1:]], cosine, sine
    )
    qkv_weights, gains = qkv
    normed, keeps, sends = [n_part], [keep], [hop(send, "heads_b", b=1)]
    n_part, keep, send = project(places, 1, other_tokens, first, qkv, cosine, sine)
    normed.append(n_part)
    keeps.append(keep)
    sends.append(hop(send, "heads_b", b=1))

    parts = jnp.stack(lax.optimization_barrier((*parts, *keeps))[:na])
    parts = [parts] + plane_hops([parts] * 3, "out_bf")
    row_starts = pick(all_starts, b, 3).reshape(length)
    heads, everything = call(
        attend_kernel,
        "attend",
        [like(length, width), like(length, 3 * width)],
        [places, *keeps, *sends, row_starts[:, None]],
        flops=8 * length * length * width,
    )

    parts = jnp.stack(lax.optimization_barrier((*parts, heads))[:4])
    other_parts = hop(parts, "out_c", c=1)

    heads = swap(heads.reshape(4 * na, shard_len, width), "heads_abc", ("a", "b", "c"))
    inputs = mine.reshape(count, features)
    attention, stream, normed_two, sums = call(
        out_kernel,
        "out_project",
        [
            like(count, features),
            like(count, features, dtype=F32),
            like(count, features),
            like(2, features, dtype=F32),
        ],
        [places, heads, parts, other_parts, inputs, gains],
        scratch=[pltpu.VMEM((features, features), BF16)],
        flops=2 * count * features * features,
    )
    group_two = [normed_two] + plane_hops([normed_two] * 3, "two_bf")

    act, units_grad, back0, *backs, full_down = call(
        feed_kernel,
        "feed",
        [
            like(4 * count, padded),
            like(4 * count, wide),
            like(count, features, dtype=F32),
            *[like(count, features)] * 3,
            like(padded, features),
        ],
        [places, *group_two, *plane, units],
        scratch=[
            pltpu.VMEM((4 * count, features), BF16),
            pltpu.VMEM((4 * count, features), BF16),
            pltpu.VMEM((features, wide), BF16),
        ],
        flops=16 * count * features * padded * 3,
        limit=60 * 2**20,
    )
    backs = plane_hops(backs, "two_back_bf")
    units_own, units_send = call(
        feed_grads_kernel,
        "feed_grads",
        [like(na, 6 * held, wide)] * 2,
        [places, *group_two, *plane, act, units_grad],
        scratch=[
            pltpu.VMEM((4 * count, features), BF16),
            pltpu.VMEM((4 * count, features), BF16),
            pltpu.VMEM((2 * na, 6 * held, wide), BF16),
        ],
        flops=16 * count * features * padded * 2,
        limit=60 * 2**20,
    )

    ffn0, *ffn = call(
        feed_branch_kernel,
        "feed_branch",
        [like(count, features, dtype=F32)] + [like(count, features)] * 3,
        [act, full_down],
        flops=8 * count * features * padded,
        scalars=0,
        limit=60 * 2**20,
    )

    def add_c(own, send, tag, *earlier):
        send = after(hop(send, tag, c=1), *earlier)
        return (own.astype(F32) + send.astype(F32)).astype(BF16)

    units_part = add_c(units_own, units_send, "units_back_c")
    back0 = after(back0, units_part)
    units_part = lax.psum_scatter(units_part, "a", scatter_dimension=0, tiled=True)
    units_rs = units_part

    stream_grad, heads_grad, out_own, out_send = call(
        stream_back_kernel,
        "stream_back",
        [
            like(count, features, dtype=F32),
            like(4 * na, shard_len, width),
            *[like(na, 4 * held, features)] * 2,
        ],
        [places, back0, *backs, stream, gains, grads, parts, other_parts, attention],
        scratch=[
            pltpu.VMEM((2 * na, 4 * held, features), BF16),
            pltpu.VMEM((features, features), BF16),
        ],
        flops=4 * count * features * features,
        limit=60 * 2**20,
    )

    heads_grad = swap(heads_grad, "heads_back_abc", ("a", "b", "c"))
    ffn = plane_hops(ffn, "ffn_bf")

    cosine, sine = turn_tables(
        after(jnp.arange(length, dtype=jnp.int32) - row_starts, everything), width
    )
    kept, moved = call(
        attend_back_kernel,
        "attend_back",
        [like(2, na, shard_len, 3 * width)] * 2,
        [
            places,
            everything,
            row_starts[:, None],
            after(heads_grad.reshape(length, width), *ffn),
            cosine,
            sine,
        ],
        scratch=[
            pltpu.VMEM((length, width), F32),
            pltpu.VMEM((length, width), F32),
            pltpu.VMEM((length, 3 * width), BF16),
        ],
        flops=20 * length,
    )
    moved = hop(moved, "back_b", b=1)
    out_part = add_c(out_own, after(out_send, ffn[0]), "out_back_c")
    out_part = lax.psum_scatter(out_part, "a", scatter_dimension=0, tiled=True)
    out, total = call(
        finish_out_kernel,
        "finish_out",
        [like(count, features), like(16, width, dtype=F32)],
        [stream, after(ffn0, kept), *ffn, sums],
        scalars=0,
    )

    dn1 = call(
        unproject_other_kernel,
        "unproject_other",
        like(na, count, features),
        [kept, moved, qkv_weights],
        scratch=[pltpu.VMEM((na * count, 3 * width), BF16)],
        flops=2 * na * count * features * 3 * width,
        scalars=0,
    )
    dn1 = hop(dn1, "tokens_back_c", c=1)
    own, send = call(
        qkv_grads_kernel,
        "qkv_grads",
        [like(features * 3 // 4 + 16, width, dtype=F32), like(3, features * 3 // 4 + 16, width)],
        [places, kept, moved, normed[0], normed[1], total],
        scratch=[
            pltpu.VMEM((na * count, 3 * width), BF16),
            pltpu.VMEM((features, 3 * width), F32),
        ],
        flops=4 * na * count * features * 3 * width,
    )
    own_tokens, *send_tokens = call(
        unproject_own_kernel,
        "unproject_own",
        [like(count, features, dtype=F32)] + [like(count, features)] * 3,
        [kept, moved, qkv_weights, dn1],
        scratch=[pltpu.VMEM((na * count, 3 * width), BF16)],
        flops=2 * na * count * features * 3 * width,
        scalars=0,
    )
    token_grads = [hop(send_tokens[step - 1], "tokens_back_a", a=step) for step in a_steps]
    units_part = units_part[0]
    units_part = after(units_part, token_grads[0])
    rows = call(
        join_grads_kernel,
        "join_grads",
        like(4, held, wide + features),
        [units_part, out_part[0]],
        scalars=0,
    )
    rows = [rows[0]] + plane_hops([rows[k] for k in range(1, 4)], "units_back_bf")
    grad_gate_up, ffn_gain_grad, grad_down, grad_out_weights = call(
        gather_units_kernel,
        "gather_units",
        [
            like(*w_gate_up.shape, dtype=F32),
            like(held, 1, dtype=F32),
            like(hidden, features, dtype=F32),
            like(held, features, dtype=F32),
        ],
        [places, *rows, units_part[4 * held :], w_gate_up, gain_ffn.astype(F32)[:, None]],
        scratch=[pltpu.VMEM((4, held, wide), BF16)],
    )

    last = call(
        qkv_sum_kernel,
        "qkv_sum",
        like(2 * na, 3 * held + 16 + count, width),
        [places, after(own, own_tokens, units_rs), *plane_hops([send[k] for k in range(3)], "qkv_back_bf"), kept, moved],
    )
    last = swap(last, "qkv_back_ac", ("a", "c"))
    grad_qkv, attn_gain_grad, stats, grad_first = call(
        functools.partial(finish_kernel, float(count * features * nd)),
        "finish",
        [
            like(*w_qkv.shape, dtype=F32),
            like(held, 1, dtype=F32),
            like(8, width, dtype=F32),
            like(row_count, shard_len, features, dtype=F32),
        ],
        [places, last, w_qkv, gain_attn.astype(F32)[:, None]],
    )
    grad_tokens = call(
        tokens_back_kernel,
        "tokens_back",
        like(row_count, shard_len, features, dtype=F32),
        [
            places,
            after(own_tokens, grad_gate_up),
            *token_grads,
            mine,
            gains,
            stream_grad.reshape(row_count, shard_len, features),
        ],
    )

    return (
        out.reshape(tokens.shape),
        grad_tokens[None],
        grad_first[None],
        grad_qkv,
        grad_out_weights,
        grad_gate_up,
        grad_down,
        attn_gain_grad[:, 0],
        ffn_gain_grad[:, 0],
        stats[0, :3],
    )


def fits(mesh):
    return mesh.shape["seq"] == 4 * NA and mesh.shape["fsdp"] == 2


def solution(mesh):
    if fits(mesh):
        grid = Mesh(mesh.devices.reshape(mesh.shape["seq"] // 4, 2, 2, 2), GRID)
        seq, every = ("a", "b", "c"), GRID
        body = grid_body
        fsdp = "f"
    else:
        grid, body = mesh, ring_body
        seq, every, fsdp = "seq", ("seq", "fsdp"), "fsdp"
    return jax.shard_map(
        body,
        mesh=grid,
        in_specs=(
            P(fsdp, None, seq, None),
            P(fsdp, None, seq, None),
            P(fsdp, None, seq),
            P(fsdp, None, seq, None),
            P(every, None),
            P(every, None),
            P(every, None),
            P(every, None),
            P(every),
            P(every),
        ),
        out_specs=(
            P(fsdp, None, seq, None),
            P(fsdp, None, seq, None),
            P(fsdp, None, seq, None),
            P(every, None),
            P(every, None),
            P(every, None),
            P(every, None),
            P(every),
            P(every),
            P(),
        ),
        check_vma=False,
    )
```
